256 devices in a mesh: leaf: 32 (over z, y), samp: 8 (over x, core).
Axes of the slice: x: 4, y: 4, z: 8, core: 2. Of those that a mesh axis runs over, the one named last changes fastest.
Arguments:
- samples: bfloat16 [131072, 512], P('leaf', 'samp'), may hold values from -6 to 6
- omega: bfloat16 [131072, 512], P('leaf', 'samp'), may hold values from -6 to 6
- leaf_basis: bfloat16 [1024, 64, 128], P('leaf'), may hold values from -0.5 to 0.5
- near_blocks: bfloat16 [1024, 8, 128, 128], P('leaf'), may hold values from -0.1875 to 0.1875
- near_index: int32 [1024, 8], P('leaf'), may hold values from 0 to 1023, as said below
- near_count: int32 [1024], P('leaf'), may hold values from 2 to 8, as said below
- inner_transfer: bfloat16 [1984, 4096], P('leaf'), may hold values from -0.5 to 0.5
- upper_transfer: bfloat16 [62, 4096], replicated, may hold values from -0.5 to 0.5
Outputs:
- leaf_coeffs: float32 [1024, 64, 512], P('leaf', None, 'samp')
- leaf_gram: float32 [1024, 4096], P('leaf', 'samp')
- ancestor_coeffs: float32 [32, 5, 64, 512], P('leaf', None, None, 'samp')
The draws below stay inside these ranges and needn't reach their ends.
Inputs may be any that keep to these rules, and one draw needn't show every extreme that they name: `near_index`: slot 0 of leaf i names i itself, slot 1 names a leaf exactly 32 away from i, and every slot names a leaf at most 32 away from i. `near_count`: every group of 32 consecutive leaves has a leaf with all 8 slots live.
All inputs are finite; a program needn't handle non-finite values.
Results may differ from the reference program's by a relative error of at most 0.0029.
Values may be sent and summed in bfloat16 or wider, within the bound.
No kernel may reach another device: no remote copies, remote signals or barrier semaphores. Data moves between devices by JAX's collectives and lax.ppermute only.
A program may use at most 64 MiB of HBM per device.

```python
import jax
import jax.numpy as jnp
from jax import lax

LEAF = 128
R = 64
NB = 8
LEAF_DEV = 32
LEAVES = 1024
POINTS = 131072
SAMPLE_COLUMNS = 512
INNER_NODES = 1984
UPPER_TREE_NODES = 62
N_LEAF = 32


def draw_near_index(key, part):
    key_offset = jax.random.fold_in(key, 11)
    key_sign = jax.random.fold_in(key, 12)
    offsets = jax.random.randint(key_offset, (LEAVES, NB), -LEAF_DEV, LEAF_DEV + 1)
    sign_draw = 2 * jax.random.randint(key_sign, (LEAVES, 1), 0, 2) - 1
    column = jnp.arange(NB)[None, :]
    offsets = jnp.where(column == 0, 0, jnp.where(column == 1, sign_draw * LEAF_DEV, offsets))
    self_leaf_block = jnp.arange(LEAVES)[:, None]
    target = self_leaf_block + offsets
    inside = (target >= 0) & (target < LEAVES)
    return jnp.where(inside, target, self_leaf_block - offsets).astype(jnp.int32)


def draw_near_count(key, part):
    key_count = jax.random.fold_in(key, 21)
    key_place = jax.random.fold_in(key, 22)
    counts = jax.random.randint(key_count, (LEAVES,), 2, NB + 1)
    selected_entries = jax.random.randint(key_place, (), 0, LEAF_DEV)
    position = jnp.arange(LEAVES) % LEAF_DEV
    return jnp.where(position == selected_entries, NB, counts).astype(jnp.int32)


def level_of(key, dims, cuts, smallest, high):
    gain = 1.0
    for dim, parts in cuts:
        draws = jax.random.uniform(jax.random.fold_in(jax.random.fold_in(key, 6), dim), (parts,), jnp.float32, smallest / len(cuts), high / len(cuts))
        gain = gain * jnp.repeat(jnp.exp(draws), dims[dim] // parts).reshape((-1,) + (1,) * (len(dims) - 1 - dim))
    return gain


def gaussian(own_key, shape, width, reach, shards=(), kind=jnp.bfloat16):
    array = width * jax.random.normal(own_key, shape, jnp.float32)
    if shards:
        array = array * level_of(own_key, shape, shards, -0.22, 0.18)
    return jnp.clip(array, -reach, reach).astype(kind)


def setup_inputs(seed: int = 0) -> dict:
    key_list = jax.random.split(jax.random.key(seed), 9)
    samples = gaussian(key_list[0], (POINTS, SAMPLE_COLUMNS), 1.0, 6.0, ((0, 32), (1, 8)))
    omega = gaussian(key_list[1], (POINTS, SAMPLE_COLUMNS), 1.0, 6.0, ((0, 32), (1, 8)))
    leaf_basis = gaussian(key_list[2], (LEAVES, R, LEAF), LEAF ** -0.5, 0.5, ((0, 32),))
    near_blocks = gaussian(key_list[3], (LEAVES, NB, LEAF, LEAF), (LEAF * NB) ** -0.5, 0.1875, ((0, 32),))
    near_index = draw_near_index(jax.random.fold_in(key_list[8], 71), 0)
    near_count = draw_near_count(jax.random.fold_in(key_list[8], 71), 0)
    inner_transfer = gaussian(key_list[6], (INNER_NODES, R * R), (2 * R) ** -0.5, 0.5, ((0, 32),))
    upper_transfer = gaussian(key_list[7], (UPPER_TREE_NODES, R * R), (2 * R) ** -0.5, 0.5)
    return {"samples": samples, "omega": omega, "leaf_basis": leaf_basis, "near_blocks": near_blocks, "near_index": near_index, "near_count": near_count, "inner_transfer": inner_transfer, "upper_transfer": upper_transfer}


def merge_levels(current, transfer, node_count):
    offset = 0
    width_now = node_count
    while width_now > 1:
        mats = transfer[:, offset:offset + width_now]
        projected = jnp.einsum('gnab,gnas->gnbs', mats, current, precision=lax.Precision.HIGHEST)
        shape_now = projected.shape
        projected = projected.reshape(shape_now[0], width_now // 2, 2, shape_now[2], shape_now[3])
        current = projected[:, :, 0] + projected[:, :, 1]
        offset = offset + width_now
        width_now = width_now // 2
    return current[:, 0]


def upper_levels(current, transfer, node_count):
    offset = 0
    width_now = node_count
    levels = []
    while width_now > 1:
        mats = transfer[offset:offset + width_now]
        projected = jnp.einsum('nab,nas->nbs', mats, current, precision=lax.Precision.HIGHEST)
        projected = projected.reshape(width_now // 2, 2, projected.shape[1], projected.shape[2])
        current = projected[:, 0] + projected[:, 1]
        levels.append(jnp.repeat(current, node_count // (width_now // 2), axis=0))
        offset = offset + width_now
        width_now = width_now // 2
    return jnp.stack(levels, axis=1)


def reference(samples, omega, leaf_basis, near_blocks, near_index, near_count, inner_transfer, upper_transfer):
    omega_leaves = omega.reshape(LEAVES, LEAF, SAMPLE_COLUMNS)
    slot_identifiers = jnp.arange(NB)

    def leaf_group(inputs):
        blocks, index_rows, count_rows, sample_rows, basis = inputs
        fetched = omega_leaves[index_rows].astype(jnp.float32)
        live_mask = (slot_identifiers[None, :] < count_rows[:, None]).astype(jnp.float32)
        near_sum = jnp.einsum('gkab,gkbs,gk->gas', blocks.astype(jnp.float32), fetched, live_mask)
        far_part = (sample_rows.astype(jnp.float32) - near_sum).astype(jnp.bfloat16)
        return jnp.einsum('grb,gbs->grs', basis.astype(jnp.float32), far_part.astype(jnp.float32))

    cluster_coefficient_array = lax.map(leaf_group, (
        near_blocks.reshape(N_LEAF, LEAF_DEV, NB, LEAF, LEAF),
        near_index.reshape(N_LEAF, LEAF_DEV, NB),
        near_count.reshape(N_LEAF, LEAF_DEV),
        samples.reshape(N_LEAF, LEAF_DEV, LEAF, SAMPLE_COLUMNS),
        leaf_basis.reshape(N_LEAF, LEAF_DEV, R, LEAF)))
    leaf_coeffs = cluster_coefficient_array.reshape(LEAVES, R, SAMPLE_COLUMNS)
    gram = jnp.einsum('lrs,lts->lrt', leaf_coeffs, leaf_coeffs, precision=lax.Precision.HIGHEST) / SAMPLE_COLUMNS
    leaf_gram = gram.reshape(LEAVES, R * R)
    inner = inner_transfer.astype(jnp.float32).reshape(N_LEAF, 2 * LEAF_DEV - 2, R, R)
    group_coeffs = merge_levels(cluster_coefficient_array, inner, LEAF_DEV)
    upper = upper_transfer.astype(jnp.float32).reshape(UPPER_TREE_NODES, R, R)
    ancestor_coeffs = upper_levels(group_coeffs, upper, N_LEAF)
    return leaf_coeffs, leaf_gram, ancestor_coeffs
```

```python
import functools

import jax
import jax.numpy as jnp
from jax import lax
from jax.experimental import pallas as pl
from jax.experimental.pallas import tpu as pltpu
from jax.sharding import PartitionSpec as P

NT = (((1,), (1,)), ((), ()))
NN = (((1,), (0,)), ((), ()))


def dot(a, b, dims):
    return lax.dot_general(a, b, dims, preferred_element_type=jnp.float32)


def split(value):
    high = value.astype(jnp.bfloat16)
    return high, (value - high.astype(jnp.float32)).astype(jnp.bfloat16)


def leaf_kernel(
    scale,
    slot_ref,
    place_ref,
    left_ref,
    own_ref,
    right_ref,
    samples_ref,
    blocks_ref,
    basis_ref,
    path_high_ref,
    path_low_ref,
    coeff_ref,
    keep_ref,
    send_ref,
    part_ref,
    source,
    gram,
):
    step = pl.program_id(0)
    pairs = pl.num_programs(0)
    slots = blocks_ref.shape[2]
    size = blocks_ref.shape[3]
    columns = own_ref.shape[0]
    count = own_ref.shape[1] // size
    rank = basis_ref.shape[1]

    @pl.when(step == 0)
    def _():
        for place, ref in enumerate((left_ref, own_ref, right_ref)):
            for leaf in range(count):
                source[place * count + leaf] = ref[:, leaf * size : (leaf + 1) * size]
        source[3 * count] = jnp.zeros((columns, size), source.dtype)
        part_ref[...] = jnp.zeros_like(part_ref)

    both = []
    for half in range(2):
        leaf = step + half * pairs
        fetched = jnp.concatenate(
            [source[slot_ref[leaf * slots + k]] for k in range(slots)], axis=1
        )
        matrix = jnp.concatenate([blocks_ref[half, 0, k] for k in range(slots)], axis=1)
        near = dot(fetched, matrix, NT)
        start = pl.multiple_of(leaf * size, size)
        far = (samples_ref[:, pl.ds(start, size)].astype(jnp.float32) - near).astype(jnp.bfloat16)
        coeff = dot(basis_ref[leaf], far, NT)
        coeff_ref[leaf] = coeff
        both.append(coeff)
    stacked = jnp.concatenate(both, axis=0)
    high, low = split(stacked)
    product = dot(high, high, NT) + (dot(high, low, NT) + dot(low, high, NT))
    lane = lax.broadcasted_iota(jnp.int32, (rank, 2 * rank), 1)
    value = jnp.where(lane < rank, product[:rank], product[rank:]) * scale
    gram[pl.ds(step, rank, stride=pairs), :] = value
    path = path_high_ref[step]
    part_ref[...] += dot(path, high, NN) + (dot(path, low, NN) + dot(path_low_ref[step], high, NN))

    @pl.when(step == pairs - 1)
    def _():
        rows = rank // (2 * keep_ref.shape[0])
        for relative in range(2 * keep_ref.shape[0]):
            first = jnp.bitwise_xor(place_ref[0], relative) * rows
            for row in range(rows):
                at = pl.multiple_of((first + row) * pairs, pairs)
                tile = gram[pl.ds(at, pairs), :]
                if relative % 2:
                    send_ref[relative // 2, row] = tile.astype(send_ref.dtype)
                else:
                    keep_ref[relative // 2, row] = tile


def finish_kernel(total_ref, last_ref, out_ref):
    rows, pairs, width = total_ref.shape
    half = width // 2
    lane = lax.broadcasted_iota(jnp.int32, (pairs, width), 1)
    for row in range(0, rows, 2):
        even = total_ref[row] + last_ref[row].astype(jnp.float32)
        odd = total_ref[row + 1] + last_ref[row + 1].astype(jnp.float32)
        at = slice(row * half, (row + 2) * half)
        out_ref[:pairs, at] = jnp.where(lane < half, even, pltpu.roll(odd, half, 1))
        out_ref[pairs:, at] = jnp.where(lane < half, pltpu.roll(even, half, 1), odd)


def whole(shape):
    return pl.BlockSpec(shape, lambda step, *_: (0,) * len(shape))


def leaf_pass(slot, place, left, own, right, samples, blocks, basis, path_high, path_low, parts):
    count, slots, size, _ = blocks.shape
    rank = basis.shape[1]
    columns = own.shape[0]
    pairs = count // 2
    rows = rank // parts
    grid_spec = pltpu.PrefetchScalarGridSpec(
        num_scalar_prefetch=2,
        grid=(pairs,),
        in_specs=[
            whole(left.shape),
            whole(own.shape),
            whole(right.shape),
            whole(samples.shape),
            pl.BlockSpec((2, 1, slots, size, size), lambda step, *_: (0, step, 0, 0, 0)),
            whole(basis.shape),
            whole(path_high.shape),
            whole(path_low.shape),
        ],
        out_specs=[
            whole((count, rank, columns)),
            whole((parts // 2, rows, pairs, 2 * rank)),
            whole((parts // 2, rows, pairs, 2 * rank)),
            whole((rank, columns)),
        ],
        scratch_shapes=[
            pltpu.VMEM((3 * count + 1, columns, size), jnp.bfloat16),
            pltpu.VMEM((rank * pairs, 2 * rank), jnp.float32),
        ],
    )
    return pl.pallas_call(
        functools.partial(leaf_kernel, 1.0 / (columns * parts)),
        grid_spec=grid_spec,
        out_shape=(
            jax.ShapeDtypeStruct((count, rank, columns), jnp.float32),
            jax.ShapeDtypeStruct((parts // 2, rows, pairs, 2 * rank), jnp.float32),
            jax.ShapeDtypeStruct((parts // 2, rows, pairs, 2 * rank), jnp.bfloat16),
            jax.ShapeDtypeStruct((rank, columns), jnp.float32),
        ),
        name="leaf_pass",
    )(slot, place, left, own, right, samples, blocks.reshape(2, pairs, slots, size, size), basis, path_high, path_low)


def exchange(value, axis, flip):
    return lax.ppermute(value, axis, [(i, i ^ flip) for i in range(lax.axis_size(axis))])


def shards(
    samples, omega, leaf_basis, near_blocks, near_index, near_count, inner_transfer, upper_transfer
):
    count = near_count.shape[0]
    slots = near_index.shape[1]
    rank = leaf_basis.shape[1]
    groups = lax.axis_size("leaf")
    parts = lax.axis_size("samp")
    device = lax.axis_index("leaf")
    place = lax.axis_index("samp")

    own = omega.T
    left = lax.ppermute(own, "leaf", [(i, i + 1) for i in range(groups - 1)])
    right = lax.ppermute(own, "leaf", [(i + 1, i) for i in range(groups - 1)])

    live = jnp.arange(slots)[None, :] < near_count[:, None]
    slot = jnp.where(live, near_index - (device * count - count), 3 * count).reshape(-1)

    heights = groups.bit_length() - 1
    upper = []
    offset, width = 0, groups
    for height in range(heights):
        row = lax.dynamic_slice_in_dim(
            upper_transfer, offset + jnp.right_shift(device, height), 1, axis=0
        )
        upper.append(row.reshape(rank, rank).astype(jnp.float32))
        offset, width = offset + width, width // 2

    levels = []
    offset, width = 0, count
    while width > 1:
        levels.append(inner_transfer[offset : offset + width].reshape(width, rank, rank))
        offset, width = offset + width, width // 2
    path = upper[0][None]
    for mats in reversed(levels):
        path = jnp.einsum(
            "nmab,nbc->nmac",
            mats.astype(jnp.float32).reshape(-1, 2, rank, rank)
            if mats.shape[0] > 1
            else mats,
            path,
            precision=lax.Precision.HIGHEST,
        ).reshape(-1, rank, rank)
    path = path.reshape(2, count // 2, rank, rank).transpose(1, 3, 0, 2)
    path = path.reshape(count // 2, rank, 2 * rank)
    path_high, path_low = split(path)

    coeffs, keep, send, part = leaf_pass(
        slot.astype(jnp.int32),
        place.astype(jnp.int32).reshape(1),
        left,
        own,
        right,
        samples.T,
        near_blocks,
        leaf_basis,
        path_high,
        path_low,
        parts,
    )

    flips = (1, 3, 4, 8, 24)
    ancestors = []
    accum = part
    gram = None
    for height in range(heights):
        if height:
            accum = jnp.dot(upper[height].T, accum, precision=lax.Precision.HIGHEST)
        accum = accum + exchange(accum, "leaf", flips[height])
        ancestors.append(accum)
    gram = keep + exchange(send, "samp", 1).astype(jnp.float32)
    got = exchange(gram[1:3].astype(jnp.bfloat16), "samp", 2).astype(jnp.float32)
    near_total = gram[0] + got[0]
    far_total = gram[3] + got[1]
    last = exchange(far_total.astype(jnp.bfloat16), "samp", 6)
    leaf_gram = pl.pallas_call(
        finish_kernel,
        out_shape=jax.ShapeDtypeStruct((count, rank * rank // parts), jnp.float32),
        name="finish",
    )(near_total, last)
    return coeffs, leaf_gram, jnp.stack(ancestors, axis=0)[None]


def solution(mesh):
    return jax.shard_map(
        shards,
        mesh=mesh,
        in_specs=(
            P("leaf", "samp"),
            P("leaf", "samp"),
            P("leaf", None, None),
            P("leaf", None, None, None),
            P("leaf", None),
            P("leaf"),
            P("leaf", None),
            P(),
        ),
        out_specs=(P("leaf", None, "samp"), P("leaf", "samp"), P("leaf", None, None, "samp")),
        check_vma=False,
    )
```

```python
import functools

import jax
import jax.numpy as jnp
from jax import lax
from jax.experimental import pallas as pl
from jax.experimental.pallas import tpu as pltpu
from jax.sharding import PartitionSpec as P

NT = (((1,), (1,)), ((), ()))
NN = (((1,), (0,)), ((), ()))
PER_STEP = 8
TAIL = 2 * PER_STEP
VMEM = pl.BlockSpec(memory_space=pltpu.VMEM)
SMEM = pl.BlockSpec(memory_space=pltpu.SMEM)


def dot(a, b, dims):
    return lax.dot_general(a, b, dims, preferred_element_type=jnp.float32)


def split(value):
    high = value.astype(jnp.bfloat16)
    return high, (value - high.astype(jnp.float32)).astype(jnp.bfloat16)


def resident(value):
    return pltpu.with_memory_space_constraint(value, pltpu.VMEM)


def spread(source, first, ref, size):
    for leaf in range(ref.shape[1] // size):
        source[first + leaf] = ref[:, leaf * size : (leaf + 1) * size]


def subtract_near(total, steps, task_ref, source, blocks_ref, acc_ref, slots):
    shift = total.bit_length()
    low = (1 << shift) - 1

    def body(step, carry):
        done = []
        for task in range(PER_STEP):
            one = task_ref[(step * PER_STEP + task) * 2]
            two = task_ref[(step * PER_STEP + task) * 2 + 1]
            left, right = jnp.right_shift(one, shift), jnp.right_shift(two, shift)
            fetched = jnp.concatenate(
                [source[jnp.bitwise_and(one, low)], source[jnp.bitwise_and(two, low)]], axis=1
            )
            matrix = jnp.concatenate([blocks_ref[left], blocks_ref[right]], axis=1)
            done.append((lax.div(left, slots), dot(fetched, matrix, NT)))
        for leaf, near in done:
            acc_ref[leaf] = acc_ref[leaf] - near
        return carry

    lax.fori_loop(0, steps, body, 0)


def own_kernel(
    index_ref,
    number_ref,
    anchor_ref,
    own_ref,
    samples_ref,
    blocks_ref,
    acc_ref,
    far_task_ref,
    far_steps_ref,
    own_task,
    source,
):
    slots, count = index_ref.shape
    size = blocks_ref.shape[1]
    total = 2 * count
    shift = total.bit_length()
    for leaf in range(count):
        acc_ref[leaf] = samples_ref[:, leaf * size : (leaf + 1) * size].astype(jnp.float32)
    spread(source, 0, own_ref, size)
    source[count] = jnp.zeros_like(source[count])

    def sort_leaf(leaf, places):
        own_place, far_place = places
        live = number_ref[leaf]
        for slot in range(slots):
            block = jnp.left_shift(leaf * slots + slot, shift)
            at = index_ref[slot, leaf] - anchor_ref[0]
            inside = jnp.logical_and(at >= count, at < total)
            alive = slot < live
            own_task[own_place] = block + (at - count)
            far_task_ref[far_place] = block + jnp.where(at < count, at, at - count)
            own_place = own_place + jnp.where(jnp.logical_and(alive, inside), 1, 0)
            far_place = far_place + jnp.where(
                jnp.logical_and(alive, jnp.logical_not(inside)), 1, 0
            )
        block = jnp.left_shift(leaf * slots, shift)
        own_task[own_place] = block + count
        far_task_ref[far_place] = block + total
        return (
            own_place + jnp.bitwise_and(own_place, 1),
            far_place + jnp.bitwise_and(far_place, 1),
        )

    own_place, far_place = lax.fori_loop(0, count, sort_leaf, (0, 0))
    for place in range(TAIL):
        own_task[own_place + place] = count
        far_task_ref[far_place + place] = total
    far_steps_ref[0] = lax.div(far_place + TAIL - 1, TAIL)
    steps = lax.div(own_place + TAIL - 1, TAIL)
    subtract_near(total, steps, own_task, source, blocks_ref, acc_ref, slots)


def far_kernel(
    task_ref,
    steps_ref,
    left_ref,
    right_ref,
    near_ref,
    blocks_ref,
    basis_ref,
    path_high_ref,
    path_low_ref,
    coeff_ref,
    high_ref,
    part_ref,
    source,
    acc,
    low_ref,
):
    count, rank, size = basis_ref.shape
    slots = blocks_ref.shape[0] // count
    spread(source, 0, left_ref, size)
    spread(source, count, right_ref, size)
    source[2 * count] = jnp.zeros_like(source[2 * count])
    acc[...] = near_ref[...]
    subtract_near(2 * count, steps_ref[0], task_ref, source, blocks_ref, acc, slots)

    def leaf_step(step, carry):
        for inner in range(PER_STEP):
            leaf = step * PER_STEP + inner
            coeff = dot(basis_ref[leaf], acc[leaf].astype(jnp.bfloat16), NT)
            coeff_ref[leaf] = coeff
            high, low = split(coeff)
            rows = pl.ds(pl.multiple_of(leaf * rank, rank), rank)
            high_ref[rows, :] = high
            low_ref[rows, :] = low
        return carry

    lax.fori_loop(0, count // PER_STEP, leaf_step, 0)
    part = dot(path_high_ref[...], high_ref[...], NN)
    part += dot(path_low_ref[...], high_ref[...], NN)
    part += dot(path_high_ref[...], low_ref[...], NN)
    turned = part.T
    half = turned.shape[0] // 2
    part_ref[...] = jnp.concatenate([turned[:half], turned[half:]], axis=1)


def gram_kernel(scale, place_ref, high_ref, keep_ref, send_ref, gram):
    parts, rows, pairs, width = keep_ref.shape
    parts = 2 * parts
    rank = width // 2
    lane = lax.broadcasted_iota(jnp.int32, (rank, width), 1)

    def pair_step(step, carry):
        for inner in range(PER_STEP):
            pair = step * PER_STEP + inner
            one = high_ref[pl.ds(pl.multiple_of(pair * rank, rank), rank), :]
            two = high_ref[pl.ds(pl.multiple_of((pair + pairs) * rank, rank), rank), :]
            stacked = jnp.concatenate([one, two], axis=0)
            product = dot(stacked, stacked, NT)
            value = jnp.where(lane < rank, product[:rank], product[rank:]) * scale
            gram[pl.ds(pair, rank, stride=pairs), :] = value
        return carry

    lax.fori_loop(0, pairs // PER_STEP, pair_step, 0)
    for relative in range(parts):
        first = jnp.bitwise_xor(place_ref[0], relative) * rows
        target = send_ref if relative % 2 else keep_ref
        for row in range(rows):
            at = pl.multiple_of((first + row) * pairs, pairs)
            target[relative // 2, row] = gram[pl.ds(at, pairs), :]


def path_kernel(top_ref, mats_ref, high_ref, low_ref, work):
    rank = top_ref.shape[0]
    count = high_ref.shape[1] // rank
    top = top_ref[...].astype(jnp.float32).T
    nodes = [split(top)]
    width = 2
    offset = 2 * count - 2
    while width <= count:
        offset = offset - width
        later = []
        for parent, (high, low) in enumerate(nodes):
            first = (offset + 2 * parent) * rank
            pair = mats_ref[first : first + 2 * rank, :]
            product = dot(high, pair, NT) + dot(low, pair, NT)
            pair_high, pair_low = split(product)
            if width == count:
                high_ref[:, 2 * parent * rank : 2 * (parent + 1) * rank] = pair_high
                low_ref[:, 2 * parent * rank : 2 * (parent + 1) * rank] = pair_low
            else:
                later.append((pair_high[:, :rank], pair_low[:, :rank]))
                later.append((pair_high[:, rank:], pair_low[:, rank:]))
        nodes = later
        width = 2 * width


def finish_kernel(total_ref, last_ref, out_ref):
    rows, pairs, width = total_ref.shape
    half = width // 2
    lane = lax.broadcasted_iota(jnp.int32, (pairs, width), 1)
    for row in range(0, rows, 2):
        even = total_ref[row] + last_ref[row]
        odd = total_ref[row + 1] + last_ref[row + 1]
        at = slice(row * half, (row + 2) * half)
        out_ref[:pairs, at] = jnp.where(lane < half, even, pltpu.roll(odd, half, 1))
        out_ref[pairs:, at] = jnp.where(lane < half, pltpu.roll(even, half, 1), odd)


def params(mib):
    return pltpu.CompilerParams(vmem_limit_bytes=mib * 2**20)


def own_pass(index, number, anchor, own, samples, blocks):
    slots, count = index.shape
    size = blocks.shape[1]
    columns = own.shape[0]
    tasks = slots * count + TAIL
    return pl.pallas_call(
        own_kernel,
        in_specs=[SMEM, SMEM, SMEM, VMEM, VMEM, VMEM],
        out_specs=(VMEM, SMEM, SMEM),
        out_shape=(
            pltpu.VMEM((count, columns, size), jnp.float32),
            jax.ShapeDtypeStruct((tasks,), jnp.int32),
            jax.ShapeDtypeStruct((1,), jnp.int32),
        ),
        scratch_shapes=[
            pltpu.SMEM((tasks,), jnp.int32),
            pltpu.VMEM((count + 1, columns, size), jnp.bfloat16),
        ],
        compiler_params=params(8),
        name="own_pass",
    )(index, number, anchor, resident(own), resident(samples), resident(blocks))


def far_pass(tasks, steps, left, right, near, blocks, basis, path_high, path_low):
    count, rank, size = basis.shape
    columns = left.shape[0]
    return pl.pallas_call(
        far_kernel,
        in_specs=[SMEM, SMEM] + [VMEM] * 7,
        out_specs=(VMEM, VMEM, VMEM),
        out_shape=(
            pltpu.VMEM((count, rank, columns), jnp.float32),
            pltpu.VMEM((count * rank, columns), jnp.bfloat16),
            pltpu.VMEM((columns // 2, 2 * rank), jnp.float32),
        ),
        scratch_shapes=[
            pltpu.VMEM((2 * count + 1, columns, size), jnp.bfloat16),
            pltpu.VMEM((count, columns, size), jnp.float32),
            pltpu.VMEM((count * rank, columns), jnp.bfloat16),
        ],
        compiler_params=params(8),
        name="far_pass",
    )(
        tasks,
        steps,
        resident(left),
        resident(right),
        near,
        resident(blocks),
        resident(basis),
        path_high,
        path_low,
    )


def gram_pass(place, high, count, parts):
    columns = high.shape[1]
    rank = high.shape[0] // count
    pairs = count // 2
    shape = (parts // 2, rank // parts, pairs, 2 * rank)
    return pl.pallas_call(
        functools.partial(gram_kernel, 1.0 / (columns * parts)),
        in_specs=[SMEM, VMEM],
        out_specs=(VMEM, VMEM),
        out_shape=(pltpu.VMEM(shape, jnp.float32), pltpu.VMEM(shape, jnp.float32)),
        scratch_shapes=[pltpu.VMEM((rank * pairs, 2 * rank), jnp.float32)],
        compiler_params=params(8),
        name="gram_pass",
    )(place, high)


def path_pass(top, mats, count):
    rank = top.shape[0]
    shape = (rank, count * rank)
    return pl.pallas_call(
        path_kernel,
        in_specs=[VMEM, VMEM],
        out_specs=(VMEM, VMEM),
        out_shape=(pltpu.VMEM(shape, jnp.bfloat16), pltpu.VMEM(shape, jnp.bfloat16)),
        scratch_shapes=[pltpu.VMEM((8, 128), jnp.float32)],
        compiler_params=params(8),
        name="path_pass",
    )(resident(top), resident(mats))


def exchange(value, axis, flip):
    return lax.ppermute(value, axis, [(i, i ^ flip) for i in range(lax.axis_size(axis))])


def shards(
    samples, omega, leaf_basis, near_blocks, near_index, near_count, inner_transfer, upper_transfer
):
    count = near_count.shape[0]
    slots = near_index.shape[1]
    rank = leaf_basis.shape[1]
    size = leaf_basis.shape[2]
    groups = lax.axis_size("leaf")
    parts = lax.axis_size("samp")
    device = lax.axis_index("leaf")
    place = lax.axis_index("samp")

    own = omega.T
    left = lax.ppermute(own, "leaf", [(i, i + 1) for i in range(groups - 1)])
    right = lax.ppermute(own, "leaf", [(i + 1, i) for i in range(groups - 1)])

    blocks = near_blocks.reshape(count * slots, size, size)
    anchor = (device * count - count).astype(jnp.int32).reshape(1)
    near, tasks, steps = own_pass(near_index.T, near_count, anchor, own, samples.T, blocks)

    heights = groups.bit_length() - 1
    rows = []
    offset, width = 0, groups
    for height in range(heights):
        rows.append(
            lax.dynamic_slice_in_dim(
                upper_transfer, offset + jnp.right_shift(device, height), 1, axis=0
            )
        )
        offset, width = offset + width, width // 2
    upper = jnp.concatenate(rows, axis=0).reshape(heights, rank, rank)
    path_high, path_low = path_pass(upper[0], inner_transfer.reshape(-1, rank), count)
    both = jnp.zeros((heights, 2, rank, 2, rank), jnp.float32)
    both = both.at[:, 0, :, 0].set(upper.astype(jnp.float32))
    both = both.at[:, 1, :, 1].set(upper.astype(jnp.float32))
    both = both.reshape(heights, 2 * rank, 2 * rank)

    coeffs, high, part = far_pass(
        tasks, steps, left, right, near, blocks, leaf_basis, path_high, path_low
    )
    keep, send = gram_pass(place.astype(jnp.int32).reshape(1), high, count, parts)

    flips = (1, 3, 4, 8, 24)
    ancestors = []
    accum = part
    for height in range(heights):
        if height:
            accum = jnp.dot(accum, both[height], precision=lax.Precision.HIGHEST)
        accum = accum + exchange(accum, "leaf", flips[height])
        turned = accum.reshape(-1, 2, rank).transpose(2, 1, 0).reshape(rank, -1)
        ancestors.append(turned)
    gram = keep + exchange(send, "samp", 1)
    got = exchange(gram[1:3].astype(jnp.bfloat16), "samp", 2).astype(jnp.float32)
    near_total = gram[0] + got[0]
    far_total = gram[3] + got[1]
    last = exchange(far_total, "samp", 6)
    leaf_gram = pl.pallas_call(
        finish_kernel,
        in_specs=[VMEM, VMEM],
        out_specs=VMEM,
        out_shape=jax.ShapeDtypeStruct((count, rank * rank // parts), jnp.float32),
        compiler_params=params(8),
        name="finish",
    )(resident(near_total), resident(last))
    return coeffs, leaf_gram, jnp.stack(ancestors, axis=0)[None]


def solution(mesh):
    return jax.shard_map(
        shards,
        mesh=mesh,
        in_specs=(
            P("leaf", "samp"),
            P("leaf", "samp"),
            P("leaf", None, None),
            P("leaf", None, None, None),
            P("leaf", None),
            P("leaf"),
            P("leaf", None),
            P(),
        ),
        out_specs=(P("leaf", None, "samp"), P("leaf", "samp"), P("leaf", None, None, "samp")),
        check_vma=False,
    )
```

```python
import functools

import jax
import jax.numpy as jnp
from jax import lax
from jax.experimental import pallas as pl
from jax.experimental.pallas import tpu as pltpu
from jax.sharding import PartitionSpec as P

NT = (((1,), (1,)), ((), ()))
NN = (((1,), (0,)), ((), ()))
PER_STEP = 8
TAIL = 2 * PER_STEP
VMEM = pl.BlockSpec(memory_space=pltpu.VMEM)
SMEM = pl.BlockSpec(memory_space=pltpu.SMEM)
ANY = pl.BlockSpec(memory_space=pl.ANY)


def dot(a, b, dims):
    return lax.dot_general(a, b, dims, preferred_element_type=jnp.float32)


def split(value):
    high = value.astype(jnp.bfloat16)
    return high, (value - high.astype(jnp.float32)).astype(jnp.bfloat16)


def resident(value):
    return pltpu.with_memory_space_constraint(value, pltpu.VMEM)


def spread(source, first, ref, size):
    for leaf in range(ref.shape[1] // size):
        source[first + leaf] = ref[:, leaf * size : (leaf + 1) * size]


def subtract_near(total, steps, task_ref, source, blocks_ref, acc_ref, slots):
    shift = total.bit_length()
    low = (1 << shift) - 1

    def body(step, carry):
        done = []
        for task in range(PER_STEP):
            one = task_ref[(step * PER_STEP + task) * 2]
            two = task_ref[(step * PER_STEP + task) * 2 + 1]
            left, right = jnp.right_shift(one, shift), jnp.right_shift(two, shift)
            fetched = jnp.concatenate(
                [source[jnp.bitwise_and(one, low)], source[jnp.bitwise_and(two, low)]], axis=1
            )
            matrix = jnp.concatenate([blocks_ref[left], blocks_ref[right]], axis=1)
            done.append((lax.div(left, slots), dot(fetched, matrix, NT)))
        for leaf, near in done:
            acc_ref[leaf] = acc_ref[leaf] - near
        return carry

    lax.fori_loop(0, steps, body, 0)


def path_products(upper_ref, mats_ref, high_ref, low_ref):
    rank = upper_ref.shape[1]
    count = high_ref.shape[1] // rank
    top = upper_ref[0].astype(jnp.float32).T
    nodes = [split(top)]
    width = 2
    offset = 2 * count - 2
    while width <= count:
        offset = offset - width
        later = []
        for parent, (high, low) in enumerate(nodes):
            first = (offset + 2 * parent) * rank
            pair = mats_ref[first : first + 2 * rank, :]
            product = dot(high, pair, NT) + dot(low, pair, NT)
            pair_high, pair_low = split(product)
            if width == count:
                high_ref[:, 2 * parent * rank : 2 * (parent + 1) * rank] = pair_high
                low_ref[:, 2 * parent * rank : 2 * (parent + 1) * rank] = pair_low
            else:
                later.append((pair_high[:, :rank], pair_low[:, :rank]))
                later.append((pair_high[:, rank:], pair_low[:, rank:]))
        nodes = later
        width = 2 * width


def own_kernel(
    anchor_ref,
    index_any,
    number_any,
    upper_ref,
    mats_ref,
    own_any,
    samples_any,
    blocks_any,
    acc_ref,
    blocks_ref,
    path_high_ref,
    path_low_ref,
    twice_ref,
    far_task_ref,
    far_steps_ref,
    index_ref,
    number_ref,
    own_task,
    own_ref,
    samples_ref,
    source,
    sems,
):
    copies = [
        pltpu.make_async_copy(origin, target, sems.at[place])
        for place, (origin, target) in enumerate(
            (
                (index_any, index_ref),
                (number_any, number_ref),
                (own_any, own_ref),
                (samples_any, samples_ref),
                (blocks_any, blocks_ref),
            )
        )
    ]
    for copy in copies:
        copy.start()
    slots, count = index_ref.shape
    size = blocks_ref.shape[1]
    total = 2 * count
    shift = total.bit_length()
    path_products(upper_ref, mats_ref, path_high_ref, path_low_ref)
    for height in range(1, upper_ref.shape[0]):
        matrix = upper_ref[height].astype(jnp.float32)
        blank = jnp.zeros_like(matrix)
        rank = matrix.shape[0]
        twice_ref[height - 1, :rank] = jnp.concatenate([matrix, blank], axis=1)
        twice_ref[height - 1, rank:] = jnp.concatenate([blank, matrix], axis=1)
    copies[0].wait()
    copies[1].wait()

    def sort_leaf(leaf, places):
        own_place, far_place = places
        live = number_ref[leaf]
        for slot in range(slots):
            block = jnp.left_shift(leaf * slots + slot, shift)
            at = index_ref[slot, leaf] - anchor_ref[0]
            inside = jnp.logical_and(at >= count, at < total)
            alive = slot < live
            own_task[own_place] = block + (at - count)
            far_task_ref[far_place] = block + jnp.where(at < count, at, at - count)
            own_place = own_place + jnp.where(jnp.logical_and(alive, inside), 1, 0)
            far_place = far_place + jnp.where(
                jnp.logical_and(alive, jnp.logical_not(inside)), 1, 0
            )
        block = jnp.left_shift(leaf * slots, shift)
        own_task[own_place] = block + count
        far_task_ref[far_place] = block + total
        return (
            own_place + jnp.bitwise_and(own_place, 1),
            far_place + jnp.bitwise_and(far_place, 1),
        )

    own_place, far_place = lax.fori_loop(0, count, sort_leaf, (0, 0))
    for place in range(TAIL):
        own_task[own_place + place] = count
        far_task_ref[far_place + place] = total
    far_steps_ref[0] = lax.div(far_place + TAIL - 1, TAIL)
    steps = lax.div(own_place + TAIL - 1, TAIL)
    copies[2].wait()
    spread(source, 0, own_ref, size)
    source[count] = jnp.zeros_like(source[count])
    copies[3].wait()
    for leaf in range(count):
        acc_ref[leaf] = samples_ref[:, leaf * size : (leaf + 1) * size].astype(jnp.float32)
    copies[4].wait()
    subtract_near(total, steps, own_task, source, blocks_ref, acc_ref, slots)


def far_kernel(
    task_ref,
    steps_ref,
    left_ref,
    right_ref,
    near_ref,
    blocks_ref,
    basis_ref,
    path_high_ref,
    path_low_ref,
    coeff_ref,
    high_ref,
    part_ref,
    acc,
    source,
    low_ref,
):
    del near_ref
    count, rank, size = basis_ref.shape
    slots = blocks_ref.shape[0] // count
    spread(source, 0, left_ref, size)
    spread(source, count, right_ref, size)
    source[2 * count] = jnp.zeros_like(source[2 * count])
    subtract_near(2 * count, steps_ref[0], task_ref, source, blocks_ref, acc, slots)

    def leaf_step(step, carry):
        for inner in range(PER_STEP):
            leaf = step * PER_STEP + inner
            coeff = dot(basis_ref[leaf], acc[leaf].astype(jnp.bfloat16), NT)
            coeff_ref[leaf] = coeff
            high, low = split(coeff)
            rows = pl.ds(pl.multiple_of(leaf * rank, rank), rank)
            high_ref[rows, :] = high
            low_ref[rows, :] = low
        return carry

    lax.fori_loop(0, count // PER_STEP, leaf_step, 0)
    part = dot(path_high_ref[...], high_ref[...], NN)
    part += dot(path_low_ref[...], high_ref[...], NN)
    part += dot(path_high_ref[...], low_ref[...], NN)
    turned = part.T
    half = turned.shape[0] // 2
    part_ref[...] = jnp.concatenate([turned[:half], turned[half:]], axis=1)


def gram_kernel(scale, place_ref, high_ref, keep_ref, send_ref, gram):
    hops, cores, rows, pairs, width = keep_ref.shape
    rank = width // 2
    lane = lax.broadcasted_iota(jnp.int32, (rank, width), 1)

    def pair_step(step, carry):
        for inner in range(PER_STEP):
            pair = step * PER_STEP + inner
            one = high_ref[pl.ds(pl.multiple_of(pair * rank, rank), rank), :]
            two = high_ref[pl.ds(pl.multiple_of((pair + pairs) * rank, rank), rank), :]
            stacked = jnp.concatenate([one, two], axis=0)
            product = dot(stacked, stacked, NT)
            value = jnp.where(lane < rank, product[:rank], product[rank:]) * scale
            gram[pl.ds(pair, rank, stride=pairs), :] = value
        return carry

    lax.fori_loop(0, pairs // PER_STEP, pair_step, 0)
    for hop in range(hops):
        for core in range(cores):
            first = (jnp.bitwise_xor(place_ref[0], hop) * cores + core) * rows
            for row in range(rows):
                at = pl.multiple_of((first + row) * pairs, pairs)
                tile = gram[pl.ds(at, pairs), :]
                keep_ref[hop, core, row] = tile
                send_ref[hop, core, row] = tile.astype(send_ref.dtype)


def finish_kernel(core_ref, total_ref, other_ref, out_ref):
    rows, pairs, width = total_ref.shape
    half = width // 2
    lane = lax.broadcasted_iota(jnp.int32, (pairs, width), 1)
    first = jnp.broadcast_to(core_ref[0], (pairs, width)) == 0
    for row in range(0, rows, 2):
        even = jnp.where(first, total_ref[row], other_ref[row])
        odd = jnp.where(first, total_ref[row + 1], other_ref[row + 1])
        at = slice(row * half, (row + 2) * half)
        out_ref[:pairs, at] = jnp.where(lane < half, even, pltpu.roll(odd, half, 1))
        out_ref[pairs:, at] = jnp.where(lane < half, pltpu.roll(even, half, 1), odd)


def turn_kernel(core_ref, lower_ref, last_ref, *refs):
    levels, out_ref = refs[:-1], refs[-1]
    half, width = last_ref.shape
    first = jnp.broadcast_to(core_ref[0], (half, width)) == 0
    for height, held in enumerate(levels):
        at = slice(height * half, (height + 1) * half)
        sent = last_ref[...] if held is levels[-1] else lower_ref[at]
        turned = jnp.where(first, sent, held[:half]).T
        out_ref[height] = jnp.concatenate([turned[: width // 2], turned[width // 2 :]], axis=1)


def params(mib):
    return pltpu.CompilerParams(vmem_limit_bytes=mib * 2**20)


def own_pass(anchor, index, number, upper, mats, own, samples, blocks):
    slots, count = index.shape
    size = blocks.shape[1]
    columns = own.shape[0]
    heights, rank, _ = upper.shape
    tasks = slots * count + TAIL
    far = lambda value: pltpu.with_memory_space_constraint(value, pltpu.HBM)
    return pl.pallas_call(
        own_kernel,
        in_specs=[SMEM, ANY, ANY, VMEM, VMEM, ANY, ANY, ANY],
        out_specs=(VMEM, VMEM, VMEM, VMEM, VMEM, SMEM, SMEM),
        out_shape=(
            pltpu.VMEM((count, columns, size), jnp.float32),
            pltpu.VMEM(blocks.shape, blocks.dtype),
            pltpu.VMEM((rank, count * rank), jnp.bfloat16),
            pltpu.VMEM((rank, count * rank), jnp.bfloat16),
            pltpu.VMEM((heights - 1, 2 * rank, 2 * rank), jnp.float32),
            jax.ShapeDtypeStruct((tasks,), jnp.int32),
            jax.ShapeDtypeStruct((1,), jnp.int32),
        ),
        scratch_shapes=[
            pltpu.SMEM((slots, count), jnp.int32),
            pltpu.SMEM((count,), jnp.int32),
            pltpu.SMEM((tasks,), jnp.int32),
            pltpu.VMEM(own.shape, own.dtype),
            pltpu.VMEM(samples.shape, samples.dtype),
            pltpu.VMEM((count + 1, columns, size), jnp.bfloat16),
            pltpu.SemaphoreType.DMA((5,)),
        ],
        compiler_params=params(8),
        name="own_pass",
    )(
        anchor,
        far(index),
        far(number),
        resident(upper),
        resident(mats),
        far(own),
        far(samples),
        far(blocks),
    )


def far_pass(tasks, steps, left, right, near, blocks, basis, path_high, path_low):
    count, rank, size = basis.shape
    columns = left.shape[0]
    return pl.pallas_call(
        far_kernel,
        in_specs=[SMEM, SMEM] + [VMEM] * 7,
        out_specs=(VMEM, VMEM, VMEM, VMEM),
        out_shape=(
            pltpu.VMEM((count, rank, columns), jnp.float32),
            pltpu.VMEM((count * rank, columns), jnp.bfloat16),
            pltpu.VMEM((columns // 2, 2 * rank), jnp.float32),
            pltpu.VMEM((count, columns, size), jnp.float32),
        ),
        input_output_aliases={4: 3},
        scratch_shapes=[
            pltpu.VMEM((2 * count + 1, columns, size), jnp.bfloat16),
            pltpu.VMEM((count * rank, columns), jnp.bfloat16),
        ],
        compiler_params=params(8),
        name="far_pass",
    )(
        tasks,
        steps,
        resident(left),
        resident(right),
        near,
        blocks,
        resident(basis),
        path_high,
        path_low,
    )


def gram_pass(place, high, count, hops, cores):
    columns = high.shape[1]
    rank = high.shape[0] // count
    pairs = count // 2
    parts = hops * cores
    shape = (hops, cores, rank // parts, pairs, 2 * rank)
    return pl.pallas_call(
        functools.partial(gram_kernel, 1.0 / (columns * parts)),
        in_specs=[SMEM, VMEM],
        out_specs=(VMEM, VMEM),
        out_shape=(pltpu.VMEM(shape, jnp.float32), pltpu.VMEM(shape, jnp.bfloat16)),
        scratch_shapes=[pltpu.VMEM((rank * pairs, 2 * rank), jnp.float32)],
        compiler_params=params(8),
        name="gram_pass",
    )(place, high)


def exchange(value, core, leaf=0, samp=0):
    groups, parts = lax.axis_size("leaf"), lax.axis_size("samp")
    pairs = [
        (g * parts + s, (g ^ leaf) * parts + (s ^ samp))
        for g in range(groups)
        for s in range(core, parts, 2)
    ]
    return lax.ppermute(value, ("leaf", "samp"), pairs)


def hand_over(value, core):
    return lax.ppermute(
        value, "samp", [(s, s ^ 1) for s in range(core, lax.axis_size("samp"), 2)]
    )


def shards(
    samples, omega, leaf_basis, near_blocks, near_index, near_count, inner_transfer, upper_transfer
):
    count = near_count.shape[0]
    slots = near_index.shape[1]
    rank = leaf_basis.shape[1]
    size = leaf_basis.shape[2]
    groups = lax.axis_size("leaf")
    parts = lax.axis_size("samp")
    device = lax.axis_index("leaf")
    place = lax.axis_index("samp").astype(jnp.int32)
    hop, core = jnp.right_shift(place, 1).reshape(1), jnp.bitwise_and(place, 1).reshape(1)

    own = omega.T
    left = lax.ppermute(own, "leaf", [(i, i + 1) for i in range(groups - 1)])
    right = lax.ppermute(own, "leaf", [(i + 1, i) for i in range(groups - 1)])

    heights = groups.bit_length() - 1
    rows = []
    offset, width = 0, groups
    for height in range(heights):
        rows.append(
            lax.dynamic_slice_in_dim(
                upper_transfer, offset + jnp.right_shift(device, height), 1, axis=0
            )
        )
        offset, width = offset + width, width // 2
    upper = jnp.concatenate(rows, axis=0).reshape(heights, rank, rank)

    blocks = near_blocks.reshape(count * slots, size, size)
    anchor = (device * count - count).astype(jnp.int32).reshape(1)
    near, blocks, path_high, path_low, twice, tasks, steps = own_pass(
        anchor,
        near_index.T,
        near_count,
        upper,
        inner_transfer.reshape(-1, rank),
        own,
        samples.T,
        blocks,
    )
    coeffs, high, part, _ = far_pass(
        tasks, steps, left, right, near, blocks, leaf_basis, path_high, path_low
    )

    accum = jnp.concatenate([part, hand_over(part, 0)], axis=0)
    keep, send = gram_pass(hop, high, count, parts // 2, 2)
    flips = (1, 3, 4, 8, 24)
    held = []
    for height in range(heights):
        if height:
            accum = jnp.dot(accum, twice[height - 1], precision=lax.Precision.HIGHEST)
        accum = accum + exchange(accum, 1, leaf=flips[height])
        held.append(accum)
        if height == heights - 2:
            lower = hand_over(jnp.concatenate([a[part.shape[0] :] for a in held], axis=0), 1)
    last = hand_over(accum[part.shape[0] :], 1)
    ancestors = pl.pallas_call(
        turn_kernel,
        in_specs=[SMEM] + [VMEM] * (heights + 2),
        out_specs=VMEM,
        out_shape=jax.ShapeDtypeStruct((heights, rank, part.shape[0] * 2), jnp.float32),
        compiler_params=params(8),
        name="turn",
    )(core, resident(lower), resident(last), *map(resident, held))

    gram = keep + hand_over(send, 1).astype(jnp.float32)
    got = exchange(gram[1:3].astype(jnp.bfloat16), 0, samp=2).astype(jnp.float32)
    near_total = gram[0] + got[0]
    total = near_total + exchange(gram[3] + got[1], 0, samp=6)
    other = hand_over(total[1], 0)
    leaf_gram = pl.pallas_call(
        finish_kernel,
        in_specs=[SMEM, VMEM, VMEM],
        out_specs=VMEM,
        out_shape=jax.ShapeDtypeStruct((count, rank * rank // parts), jnp.float32),
        compiler_params=params(8),
        name="finish",
    )(core, resident(total[0]), resident(other))
    return coeffs, leaf_gram, ancestors[None]


def solution(mesh):
    return jax.shard_map(
        shards,
        mesh=mesh,
        in_specs=(
            P("leaf", "samp"),
            P("leaf", "samp"),
            P("leaf", None, None),
            P("leaf", None, None, None),
            P("leaf", None),
            P("leaf"),
            P("leaf", None),
            P(),
        ),
        out_specs=(P("leaf", None, "samp"), P("leaf", "samp"), P("leaf", None, None, "samp")),
        check_vma=False,
    )
```

```python
import functools

import jax
import jax.numpy as jnp
from jax import lax
from jax.experimental import pallas as pl
from jax.experimental.pallas import tpu as pltpu
from jax.sharding import PartitionSpec as P

NT = (((1,), (1,)), ((), ()))
NN = (((1,), (0,)), ((), ()))
PER_STEP = 8
TAIL = 2 * PER_STEP
VMEM = pl.BlockSpec(memory_space=pltpu.VMEM)
SMEM = pl.BlockSpec(memory_space=pltpu.SMEM)
ANY = pl.BlockSpec(memory_space=pl.ANY)


def dot(a, b, dims):
    return lax.dot_general(a, b, dims, preferred_element_type=jnp.float32)


def split(value):
    high = value.astype(jnp.bfloat16)
    return high, (value - high.astype(jnp.float32)).astype(jnp.bfloat16)


def resident(value):
    return pltpu.with_memory_space_constraint(value, pltpu.VMEM)


def spread(source, first, ref, size):
    for leaf in range(ref.shape[1] // size):
        source[first + leaf] = ref[:, leaf * size : (leaf + 1) * size]


def subtract_near(total, steps, task_ref, source, blocks_ref, acc_ref, slots):
    shift = total.bit_length()
    low = (1 << shift) - 1

    def body(step, carry):
        done = []
        for task in range(PER_STEP):
            one = task_ref[(step * PER_STEP + task) * 2]
            two = task_ref[(step * PER_STEP + task) * 2 + 1]
            left, right = jnp.right_shift(one, shift), jnp.right_shift(two, shift)
            fetched = jnp.concatenate(
                [source[jnp.bitwise_and(one, low)], source[jnp.bitwise_and(two, low)]], axis=1
            )
            matrix = jnp.concatenate([blocks_ref[left], blocks_ref[right]], axis=1)
            done.append((lax.div(left, slots), dot(fetched, matrix, NT)))
        for leaf, near in done:
            acc_ref[leaf] = acc_ref[leaf] - near
        return carry

    lax.fori_loop(0, steps, body, 0)


def path_products(upper_ref, mats_ref, high_ref, low_ref):
    rank = upper_ref.shape[1]
    count = high_ref.shape[1] // rank
    top = upper_ref[0].astype(jnp.float32).T
    nodes = [split(top)]
    width = 2
    offset = 2 * count - 2
    while width <= count:
        offset = offset - width
        later = []
        for parent, (high, low) in enumerate(nodes):
            first = (offset + 2 * parent) * rank
            pair = mats_ref[first : first + 2 * rank, :]
            product = dot(high, pair, NT) + dot(low, pair, NT)
            pair_high, pair_low = split(product)
            if width == count:
                high_ref[:, 2 * parent * rank : 2 * (parent + 1) * rank] = pair_high
                low_ref[:, 2 * parent * rank : 2 * (parent + 1) * rank] = pair_low
            else:
                later.append((pair_high[:, :rank], pair_low[:, :rank]))
                later.append((pair_high[:, rank:], pair_low[:, rank:]))
        nodes = later
        width = 2 * width


def own_kernel(
    anchor_ref,
    index_any,
    number_any,
    upper_ref,
    mats_ref,
    own_any,
    samples_any,
    blocks_any,
    acc_ref,
    blocks_ref,
    path_high_ref,
    path_low_ref,
    twice_ref,
    first_task_ref,
    first_steps_ref,
    second_task_ref,
    second_steps_ref,
    index_ref,
    number_ref,
    own_task,
    own_ref,
    samples_ref,
    source,
    sems,
):
    copies = [
        pltpu.make_async_copy(origin, target, sems.at[place])
        for place, (origin, target) in enumerate(
            (
                (index_any, index_ref),
                (number_any, number_ref),
                (own_any, own_ref),
                (samples_any, samples_ref),
                (blocks_any, blocks_ref),
            )
        )
    ]
    for copy in copies:
        copy.start()
    slots, count = index_ref.shape
    size = blocks_ref.shape[1]
    total = 2 * count
    shift = count.bit_length()
    path_products(upper_ref, mats_ref, path_high_ref, path_low_ref)
    for height in range(1, upper_ref.shape[0]):
        matrix = upper_ref[height].astype(jnp.float32)
        blank = jnp.zeros_like(matrix)
        rank = matrix.shape[0]
        twice_ref[height - 1, :rank] = jnp.concatenate([matrix, blank], axis=1)
        twice_ref[height - 1, rank:] = jnp.concatenate([blank, matrix], axis=1)
    copies[0].wait()
    copies[1].wait()

    lists = (own_task, first_task_ref, second_task_ref)
    odd = anchor_ref[1]

    def sort_leaf(leaf, places):
        places = list(places)
        live = number_ref[leaf]
        for slot in range(slots):
            block = jnp.left_shift(leaf * slots + slot, shift)
            at = index_ref[slot, leaf] - anchor_ref[0]
            before, after = at < count, at >= total
            alive = slot < live
            code = block + jnp.bitwise_and(at, count - 1)
            inside = jnp.logical_not(jnp.logical_or(before, after))
            chosen = (
                inside,
                jnp.where(odd == 1, after, before),
                jnp.where(odd == 1, before, after),
            )
            for which, (tasks, here) in enumerate(zip(lists, chosen)):
                tasks[places[which]] = code
                places[which] = places[which] + jnp.where(jnp.logical_and(alive, here), 1, 0)
        blank = jnp.left_shift(leaf * slots, shift) + count
        for which, tasks in enumerate(lists):
            tasks[places[which]] = blank
            places[which] = places[which] + jnp.bitwise_and(places[which], 1)
        return tuple(places)

    places = lax.fori_loop(0, count, sort_leaf, (0, 0, 0))
    for place in range(TAIL):
        for which, tasks in enumerate(lists):
            tasks[places[which] + place] = count
    steps = [lax.div(place + TAIL - 1, TAIL) for place in places]
    first_steps_ref[0] = steps[1]
    second_steps_ref[0] = steps[2]
    copies[2].wait()
    spread(source, 0, own_ref, size)
    source[count] = jnp.zeros_like(source[count])
    copies[3].wait()
    for leaf in range(count):
        acc_ref[leaf] = samples_ref[:, leaf * size : (leaf + 1) * size].astype(jnp.float32)
    copies[4].wait()
    subtract_near(count, steps[0], own_task, source, blocks_ref, acc_ref, slots)


def side_kernel(task_ref, steps_ref, side_ref, near_ref, blocks_ref, slots, acc, source):
    del near_ref
    count, _, size = acc.shape
    spread(source, 0, side_ref, size)
    source[count] = jnp.zeros_like(source[count])
    subtract_near(count, steps_ref[0], task_ref, source, blocks_ref, acc, slots)


def far_kernel(
    task_ref,
    steps_ref,
    side_ref,
    near_ref,
    blocks_ref,
    basis_ref,
    path_high_ref,
    path_low_ref,
    coeff_any,
    high_ref,
    part_ref,
    acc,
    source,
    low_ref,
    coeff_ref,
    sems,
):
    count, rank, size = basis_ref.shape
    slots = blocks_ref.shape[0] // count
    side_kernel(task_ref, steps_ref, side_ref, near_ref, blocks_ref, slots, acc, source)

    copies = []
    for step in range(count // PER_STEP):
        for leaf in range(step * PER_STEP, (step + 1) * PER_STEP):
            coeff = dot(basis_ref[leaf], acc[leaf].astype(jnp.bfloat16), NT)
            coeff_ref[leaf] = coeff
            high, low = split(coeff)
            rows = slice(leaf * rank, (leaf + 1) * rank)
            high_ref[rows, :] = high
            low_ref[rows, :] = low
        these = pl.ds(step * PER_STEP, PER_STEP)
        copies.append(
            pltpu.make_async_copy(coeff_ref.at[these], coeff_any.at[these], sems.at[step])
        )
        copies[-1].start()
    part = dot(path_high_ref[...], high_ref[...], NN)
    part += dot(path_low_ref[...], high_ref[...], NN)
    part += dot(path_high_ref[...], low_ref[...], NN)
    turned = part.T
    half = turned.shape[0] // 2
    part_ref[...] = jnp.concatenate([turned[:half], turned[half:]], axis=1)
    for copy in copies:
        copy.wait()


def gram_kernel(scale, place_ref, high_ref, keep_ref, send_ref, gram):
    parts, rows, pairs, width = keep_ref.shape
    parts = 2 * parts
    rank = width // 2
    lane = lax.broadcasted_iota(jnp.int32, (rank, width), 1)

    def pair_step(step, carry):
        for inner in range(PER_STEP):
            pair = step * PER_STEP + inner
            one = high_ref[pl.ds(pl.multiple_of(pair * rank, rank), rank), :]
            two = high_ref[pl.ds(pl.multiple_of((pair + pairs) * rank, rank), rank), :]
            stacked = jnp.concatenate([one, two], axis=0)
            product = dot(stacked, stacked, NT)
            value = jnp.where(lane < rank, product[:rank], product[rank:]) * scale
            gram[pl.ds(pair, rank, stride=pairs), :] = value
        return carry

    lax.fori_loop(0, pairs // PER_STEP, pair_step, 0)
    for relative in range(parts):
        first = jnp.bitwise_xor(place_ref[0], relative) * rows
        target = send_ref if relative % 2 else keep_ref
        for row in range(rows):
            at = pl.multiple_of((first + row) * pairs, pairs)
            target[relative // 2, row] = gram[pl.ds(at, pairs), :]


def finish_kernel(total_ref, last_ref, out_ref):
    rows, pairs, width = total_ref.shape
    half = width // 2
    lane = lax.broadcasted_iota(jnp.int32, (pairs, width), 1)
    for row in range(0, rows, 2):
        even = total_ref[row] + last_ref[row]
        odd = total_ref[row + 1] + last_ref[row + 1]
        at = slice(row * half, (row + 2) * half)
        out_ref[:pairs, at] = jnp.where(lane < half, even, pltpu.roll(odd, half, 1))
        out_ref[pairs:, at] = jnp.where(lane < half, pltpu.roll(even, half, 1), odd)


def turn_kernel(*refs):
    levels, out_ref = refs[:-1], refs[-1]
    for height, level in enumerate(levels):
        turned = level[...].T
        half = turned.shape[0] // 2
        out_ref[height] = jnp.concatenate([turned[:half], turned[half:]], axis=1)


def params(mib):
    return pltpu.CompilerParams(vmem_limit_bytes=mib * 2**20)


def own_pass(anchor, index, number, upper, mats, own, samples, blocks):
    slots, count = index.shape
    size = blocks.shape[1]
    columns = own.shape[0]
    heights, rank, _ = upper.shape
    tasks = slots * count + TAIL
    far = lambda value: pltpu.with_memory_space_constraint(value, pltpu.HBM)
    return pl.pallas_call(
        own_kernel,
        in_specs=[SMEM, ANY, ANY, VMEM, VMEM, ANY, ANY, ANY],
        out_specs=(VMEM, VMEM, VMEM, VMEM, VMEM, SMEM, SMEM, SMEM, SMEM),
        out_shape=(
            pltpu.VMEM((count, columns, size), jnp.float32),
            pltpu.VMEM(blocks.shape, blocks.dtype),
            pltpu.VMEM((rank, count * rank), jnp.bfloat16),
            pltpu.VMEM((rank, count * rank), jnp.bfloat16),
            pltpu.VMEM((heights - 1, 2 * rank, 2 * rank), jnp.float32),
            jax.ShapeDtypeStruct((tasks,), jnp.int32),
            jax.ShapeDtypeStruct((1,), jnp.int32),
            jax.ShapeDtypeStruct((tasks,), jnp.int32),
            jax.ShapeDtypeStruct((1,), jnp.int32),
        ),
        scratch_shapes=[
            pltpu.SMEM((slots, count), jnp.int32),
            pltpu.SMEM((count,), jnp.int32),
            pltpu.SMEM((tasks,), jnp.int32),
            pltpu.VMEM(own.shape, own.dtype),
            pltpu.VMEM(samples.shape, samples.dtype),
            pltpu.VMEM((count + 1, columns, size), jnp.bfloat16),
            pltpu.SemaphoreType.DMA((5,)),
        ],
        compiler_params=params(8),
        name="own_pass",
    )(
        anchor,
        far(index),
        far(number),
        resident(upper),
        resident(mats),
        far(own),
        far(samples),
        far(blocks),
    )


def side_pass(tasks, steps, side, near, blocks):
    count, columns, size = near.shape
    slots = blocks.shape[0] // count

    def kernel(task_ref, steps_ref, side_ref, near_ref, blocks_ref, acc, source):
        side_kernel(task_ref, steps_ref, side_ref, near_ref, blocks_ref, slots, acc, source)

    return pl.pallas_call(
        kernel,
        in_specs=[SMEM, SMEM] + [VMEM] * 3,
        out_specs=VMEM,
        out_shape=pltpu.VMEM((count, columns, size), jnp.float32),
        input_output_aliases={3: 0},
        scratch_shapes=[pltpu.VMEM((count + 1, columns, size), jnp.bfloat16)],
        compiler_params=params(8),
        name="side_pass",
    )(tasks, steps, resident(side), near, blocks)


def far_pass(tasks, steps, side, near, blocks, basis, path_high, path_low):
    count, rank, size = basis.shape
    columns = side.shape[0]
    return pl.pallas_call(
        far_kernel,
        in_specs=[SMEM, SMEM] + [VMEM] * 6,
        out_specs=(ANY, VMEM, VMEM, VMEM),
        out_shape=(
            pltpu.HBM((count, rank, columns), jnp.float32),
            pltpu.VMEM((count * rank, columns), jnp.bfloat16),
            pltpu.VMEM((columns // 2, 2 * rank), jnp.float32),
            pltpu.VMEM((count, columns, size), jnp.float32),
        ),
        input_output_aliases={3: 3},
        scratch_shapes=[
            pltpu.VMEM((count + 1, columns, size), jnp.bfloat16),
            pltpu.VMEM((count * rank, columns), jnp.bfloat16),
            pltpu.VMEM((count, rank, columns), jnp.float32),
            pltpu.SemaphoreType.DMA((count // PER_STEP,)),
        ],
        compiler_params=params(8),
        name="far_pass",
    )(tasks, steps, resident(side), near, blocks, resident(basis), path_high, path_low)


def gram_pass(place, high, count, parts):
    columns = high.shape[1]
    rank = high.shape[0] // count
    pairs = count // 2
    shape = (parts // 2, rank // parts, pairs, 2 * rank)
    return pl.pallas_call(
        functools.partial(gram_kernel, 1.0 / (columns * parts)),
        in_specs=[SMEM, VMEM],
        out_specs=(VMEM, VMEM),
        out_shape=(pltpu.VMEM(shape, jnp.float32), pltpu.VMEM(shape, jnp.float32)),
        scratch_shapes=[pltpu.VMEM((rank * pairs, 2 * rank), jnp.float32)],
        compiler_params=params(8),
        name="gram_pass",
    )(place, high)


def exchange(value, axis, flip):
    return lax.ppermute(value, axis, [(i, i ^ flip) for i in range(lax.axis_size(axis))])


def swap(value, axis, first):
    pairs = [(i, i + 1) for i in range(first, lax.axis_size(axis) - 1, 2)]
    return lax.ppermute(value, axis, pairs + [(j, i) for i, j in pairs])


def shards(
    samples, omega, leaf_basis, near_blocks, near_index, near_count, inner_transfer, upper_transfer
):
    count = near_count.shape[0]
    slots = near_index.shape[1]
    rank = leaf_basis.shape[1]
    size = leaf_basis.shape[2]
    groups = lax.axis_size("leaf")
    parts = lax.axis_size("samp")
    device = lax.axis_index("leaf")
    place = lax.axis_index("samp").astype(jnp.int32)

    own = omega.T
    first = swap(own, "leaf", 1)
    second = swap(own, "leaf", 0)

    heights = groups.bit_length() - 1
    rows = []
    offset, width = 0, groups
    for height in range(heights):
        rows.append(
            lax.dynamic_slice_in_dim(
                upper_transfer, offset + jnp.right_shift(device, height), 1, axis=0
            )
        )
        offset, width = offset + width, width // 2
    upper = jnp.concatenate(rows, axis=0).reshape(heights, rank, rank)

    blocks = near_blocks.reshape(count * slots, size, size)
    anchor = jnp.stack([device * count - count, jnp.bitwise_and(device, 1)]).astype(jnp.int32)
    near, blocks, path_high, path_low, twice, tasks, steps, later_tasks, later_steps = own_pass(
        anchor,
        near_index.T,
        near_count,
        upper,
        inner_transfer.reshape(-1, rank),
        own,
        samples.T,
        blocks,
    )
    near = side_pass(tasks, steps, first, near, blocks)
    coeffs, high, part, _ = far_pass(
        later_tasks, later_steps, second, near, blocks, leaf_basis, path_high, path_low
    )

    flips = (1, 3, 4, 8, 24)
    levels = []
    accum = part
    gram, middle = None, None
    for height in range(heights):
        if height:
            accum = jnp.dot(accum, twice[height - 1], precision=lax.Precision.HIGHEST)
        other = exchange(accum, "leaf", flips[height])
        if height == 0:
            keep, send = gram_pass(place.reshape(1), high, count, parts)
            got = exchange(send, "samp", 1)
        elif height == 1:
            gram = keep + got
            middle = gram[1:3].astype(jnp.bfloat16)
            other, _ = lax.optimization_barrier((other, middle))
            got = exchange(middle, "samp", 2).astype(jnp.float32)
        elif height == 2:
            near_total = gram[0] + got[0]
            far_total = gram[3] + got[1]
            other, _ = lax.optimization_barrier((other, far_total))
            got = exchange(far_total, "samp", 6)
        elif height == 3:
            leaf_gram = pl.pallas_call(
                finish_kernel,
                in_specs=[VMEM, VMEM],
                out_specs=VMEM,
                out_shape=jax.ShapeDtypeStruct((count, rank * rank // parts), jnp.float32),
                compiler_params=params(8),
                name="finish",
            )(resident(near_total), resident(got))
            other, _ = lax.optimization_barrier((other, leaf_gram))
        accum = accum + other
        levels.append(accum)
    ancestors = pl.pallas_call(
        turn_kernel,
        in_specs=[VMEM] * heights,
        out_specs=VMEM,
        out_shape=jax.ShapeDtypeStruct((heights, rank, 2 * part.shape[0]), jnp.float32),
        compiler_params=params(8),
        name="turn",
    )(*map(resident, levels))
    return coeffs, leaf_gram, ancestors[None]


def solution(mesh):
    return jax.shard_map(
        shards,
        mesh=mesh,
        in_specs=(
            P("leaf", "samp"),
            P("leaf", "samp"),
            P("leaf", None, None),
            P("leaf", None, None, None),
            P("leaf", None),
            P("leaf"),
            P("leaf", None),
            P(),
        ),
        out_specs=(P("leaf", None, "samp"), P("leaf", "samp"), P("leaf", None, None, "samp")),
        check_vma=False,
    )
```

```python
import functools

import jax
import jax.numpy as jnp
from jax import lax
from jax.experimental import pallas as pl
from jax.experimental.pallas import tpu as pltpu
from jax.sharding import PartitionSpec as P

NT = (((1,), (1,)), ((), ()))
NN = (((1,), (0,)), ((), ()))
PER_STEP = 8
PER_TASKS = 2 * PER_STEP
LANES = 128
TASK_ROWS = 8
LIST_ROWS = 3
VMEM = pl.BlockSpec(memory_space=pltpu.VMEM)
SMEM = pl.BlockSpec(memory_space=pltpu.SMEM)
ANY = pl.BlockSpec(memory_space=pl.ANY)


def dot(a, b, dims):
    return lax.dot_general(a, b, dims, preferred_element_type=jnp.float32)


def split(value):
    high = value.astype(jnp.bfloat16)
    return high, (value - high.astype(jnp.float32)).astype(jnp.bfloat16)


def resident(value):
    return pltpu.with_memory_space_constraint(value, pltpu.VMEM)


def spread(source, first, ref, size):
    for leaf in range(ref.shape[1] // size):
        source[first + leaf] = ref[:, leaf * size : (leaf + 1) * size]


def subtract_near(count, task_ref, source, blocks_ref, acc_ref, slots):
    shift = count.bit_length()
    low = (1 << shift) - 1
    per_row = LANES // PER_TASKS

    def body(step, carry):
        done = []
        row = lax.div(step, per_row)
        at = lax.rem(step, per_row) * PER_TASKS
        for task in range(PER_STEP):
            one = task_ref[row, at + 2 * task]
            two = task_ref[row, at + 2 * task + 1]
            left, right = jnp.right_shift(one, shift), jnp.right_shift(two, shift)
            fetched = jnp.concatenate(
                [source[jnp.bitwise_and(one, low)], source[jnp.bitwise_and(two, low)]], axis=1
            )
            matrix = jnp.concatenate([blocks_ref[left], blocks_ref[right]], axis=1)
            done.append((lax.div(left, slots), dot(fetched, matrix, NT)))
        for leaf, near in done:
            acc_ref[leaf] = acc_ref[leaf] - near
        return carry

    lax.fori_loop(0, task_ref[LIST_ROWS - 1, LANES - 1], body, 0)


def list_tasks(index, number, device, lists_ref):
    slots, count = index.shape
    shift = count.bit_length()
    slot = lax.broadcasted_iota(jnp.int32, (slots, count), 0)
    leaf = lax.broadcasted_iota(jnp.int32, (slots, count), 1)
    at = index - (device * count - count)
    alive = slot < number
    before, after = at < count, at >= 2 * count
    even = jnp.broadcast_to(jnp.bitwise_and(device, 1), at.shape) == 0
    side = jnp.where(before == even, 1, 2)
    kind = jnp.where(jnp.logical_or(before, after), side, 0)
    code = jnp.left_shift(leaf * slots + slot, shift) + jnp.bitwise_and(at, count - 1)
    blank = count
    earlier_slot = (
        lax.broadcasted_iota(jnp.int32, (slots, slots), 1)
        < lax.broadcasted_iota(jnp.int32, (slots, slots), 0)
    ).astype(jnp.bfloat16)
    earlier_leaf = (
        lax.broadcasted_iota(jnp.int32, (count, count), 0)
        < lax.broadcasted_iota(jnp.int32, (count, count), 1)
    ).astype(jnp.bfloat16)
    place = jnp.full((slots, count), -1, jnp.int32)
    steps = []
    for which in range(3):
        chosen = jnp.logical_and(alive, kind == which)
        mark = jnp.where(chosen, 1.0, 0.0)
        rank = dot(earlier_slot, mark.astype(jnp.bfloat16), NN)
        number_here = jnp.sum(mark, axis=0, keepdims=True).astype(jnp.int32)
        padded = (number_here + jnp.bitwise_and(number_here, 1)).astype(jnp.float32)
        base = dot(jnp.broadcast_to(padded, (slots, count)).astype(jnp.bfloat16), earlier_leaf, NN)
        here = (base + rank).astype(jnp.int32) + which * LIST_ROWS * LANES
        place = jnp.where(chosen, here, place)
        total = jnp.sum(padded, axis=1, keepdims=True).astype(jnp.int32)
        steps.append(jnp.right_shift(total + PER_TASKS - 1, PER_TASKS.bit_length() - 1))
    place, value = place.T, code.T - blank
    lane = lax.broadcasted_iota(jnp.int32, (count, LANES), 1)
    for which in range(3):
        for row in range(LIST_ROWS):
            target = lane + (which * LIST_ROWS + row) * LANES
            total = jnp.zeros((count, LANES), jnp.int32)
            for k in range(slots):
                total += jnp.where(place[:, k : k + 1] == target, value[:, k : k + 1], 0)
            line = jnp.sum(total, axis=0, keepdims=True) + blank
            if row == LIST_ROWS - 1:
                line = jnp.where(lane[:1] == LANES - 1, steps[which], line)
            lists_ref[which, row : row + 1] = line


def path_products(upper_ref, mats_ref, high_ref, low_ref):
    rank = upper_ref.shape[1]
    count = high_ref.shape[1] // rank
    top = upper_ref[0].astype(jnp.float32).T
    nodes = [split(top)]
    width = 2
    offset = 2 * count - 2
    while width <= count:
        offset = offset - width
        later = []
        for parent, (high, low) in enumerate(nodes):
            first = (offset + 2 * parent) * rank
            pair = mats_ref[first : first + 2 * rank, :]
            product = dot(high, pair, NT) + dot(low, pair, NT)
            pair_high, pair_low = split(product)
            if width == count:
                high_ref[:, 2 * parent * rank : 2 * (parent + 1) * rank] = pair_high
                low_ref[:, 2 * parent * rank : 2 * (parent + 1) * rank] = pair_low
            else:
                later.append((pair_high[:, :rank], pair_low[:, :rank]))
                later.append((pair_high[:, rank:], pair_low[:, rank:]))
        nodes = later
        width = 2 * width


def own_kernel(
    index_any,
    number_any,
    upper_ref,
    mats_ref,
    own_any,
    samples_any,
    blocks_any,
    acc_ref,
    blocks_ref,
    path_high_ref,
    path_low_ref,
    twice_ref,
    first_task_ref,
    second_task_ref,
    own_task,
    lists,
    index_ref,
    number_ref,
    own_ref,
    samples_ref,
    source,
    sems,
):
    pairs = (
        (index_any, index_ref),
        (number_any, number_ref),
        (own_any, own_ref),
        (samples_any, samples_ref),
        (blocks_any, blocks_ref),
        (lists.at[0], own_task),
        (lists.at[1], first_task_ref),
        (lists.at[2], second_task_ref),
    )
    copies = [
        pltpu.make_async_copy(origin, target, sems.at[place])
        for place, (origin, target) in enumerate(pairs)
    ]
    for copy in copies[:5]:
        copy.start()
    slots, count = index_ref.shape
    size = blocks_ref.shape[1]
    rank = upper_ref.shape[1]
    copies[0].wait()
    copies[1].wait()
    list_tasks(index_ref[...], number_ref[...], lax.axis_index("leaf"), lists)
    for copy in copies[5:]:
        copy.start()
    path_products(upper_ref, mats_ref, path_high_ref, path_low_ref)
    for height in range(1, upper_ref.shape[0]):
        matrix = upper_ref[height].astype(jnp.float32)
        blank = jnp.zeros_like(matrix)
        twice_ref[height - 1, :rank] = jnp.concatenate([matrix, blank], axis=1)
        twice_ref[height - 1, rank:] = jnp.concatenate([blank, matrix], axis=1)
    copies[2].wait()
    spread(source, 0, own_ref, size)
    source[count] = jnp.zeros_like(source[count])
    copies[3].wait()
    for leaf in range(count):
        acc_ref[leaf] = samples_ref[:, leaf * size : (leaf + 1) * size].astype(jnp.float32)
    for copy in copies[4:]:
        copy.wait()
    subtract_near(count, own_task, source, blocks_ref, acc_ref, slots)


def side_kernel(task_ref, side_ref, near_ref, blocks_ref, slots, acc, source):
    del near_ref
    count, _, size = acc.shape
    spread(source, 0, side_ref, size)
    source[count] = jnp.zeros_like(source[count])
    subtract_near(count, task_ref, source, blocks_ref, acc, slots)


def far_kernel(
    task_ref,
    side_ref,
    near_ref,
    blocks_ref,
    basis_ref,
    path_high_ref,
    path_low_ref,
    coeff_any,
    high_ref,
    part_ref,
    acc,
    source,
    low_ref,
    coeff_ref,
    sems,
):
    count, rank, size = basis_ref.shape
    slots = blocks_ref.shape[0] // count
    side_kernel(task_ref, side_ref, near_ref, blocks_ref, slots, acc, source)

    copies = []
    for step in range(count // PER_STEP):
        for leaf in range(step * PER_STEP, (step + 1) * PER_STEP):
            coeff = dot(basis_ref[leaf], acc[leaf].astype(jnp.bfloat16), NT)
            coeff_ref[leaf] = coeff
            high, low = split(coeff)
            rows = slice(leaf * rank, (leaf + 1) * rank)
            high_ref[rows, :] = high
            low_ref[rows, :] = low
        these = pl.ds(step * PER_STEP, PER_STEP)
        copies.append(
            pltpu.make_async_copy(coeff_ref.at[these], coeff_any.at[these], sems.at[step])
        )
        copies[-1].start()
    part = dot(path_high_ref[...], high_ref[...], NN)
    part += dot(path_low_ref[...], high_ref[...], NN)
    part += dot(path_high_ref[...], low_ref[...], NN)
    turned = part.T
    half = turned.shape[0] // 2
    part_ref[...] = jnp.concatenate([turned[:half], turned[half:]], axis=1)
    for copy in copies:
        copy.wait()


def gram_kernel(scale, place_ref, high_ref, keep_ref, send_ref, gram):
    parts, rows, pairs, width = keep_ref.shape
    parts = 2 * parts
    rank = width // 2
    lane = lax.broadcasted_iota(jnp.int32, (rank, width), 1)

    def pair_step(step, carry):
        for inner in range(PER_STEP):
            pair = step * PER_STEP + inner
            one = high_ref[pl.ds(pl.multiple_of(pair * rank, rank), rank), :]
            two = high_ref[pl.ds(pl.multiple_of((pair + pairs) * rank, rank), rank), :]
            stacked = jnp.concatenate([one, two], axis=0)
            product = dot(stacked, stacked, NT)
            value = jnp.where(lane < rank, product[:rank], product[rank:]) * scale
            gram[pl.ds(pair, rank, stride=pairs), :] = value
        return carry

    lax.fori_loop(0, pairs // PER_STEP, pair_step, 0)
    for relative in range(parts):
        first = jnp.bitwise_xor(place_ref[0], relative) * rows
        target = send_ref if relative % 2 else keep_ref
        for row in range(rows):
            at = pl.multiple_of((first + row) * pairs, pairs)
            target[relative // 2, row] = gram[pl.ds(at, pairs), :]


def finish_kernel(total_ref, last_ref, out_ref):
    rows, pairs, width = total_ref.shape
    half = width // 2
    lane = lax.broadcasted_iota(jnp.int32, (pairs, width), 1)
    for row in range(0, rows, 2):
        even = total_ref[row] + last_ref[row]
        odd = total_ref[row + 1] + last_ref[row + 1]
        at = slice(row * half, (row + 2) * half)
        out_ref[:pairs, at] = jnp.where(lane < half, even, pltpu.roll(odd, half, 1))
        out_ref[pairs:, at] = jnp.where(lane < half, pltpu.roll(even, half, 1), odd)


def turn_kernel(*refs):
    levels, out_ref = refs[:-1], refs[-1]
    for height, level in enumerate(levels):
        turned = level[...].T
        half = turned.shape[0] // 2
        out_ref[height] = jnp.concatenate([turned[:half], turned[half:]], axis=1)


def params(mib):
    return pltpu.CompilerParams(vmem_limit_bytes=mib * 2**20)


def own_pass(index, number, upper, mats, own, samples, blocks):
    slots, count = index.shape
    size = blocks.shape[1]
    columns = own.shape[0]
    heights, rank, _ = upper.shape
    tasks = pltpu.SMEM((TASK_ROWS, LANES), jnp.int32)
    far = lambda value: pltpu.with_memory_space_constraint(value, pltpu.HBM)
    return pl.pallas_call(
        own_kernel,
        in_specs=[ANY, ANY, VMEM, VMEM, ANY, ANY, ANY],
        out_specs=(VMEM, VMEM, VMEM, VMEM, VMEM, SMEM, SMEM),
        out_shape=(
            pltpu.VMEM((count, columns, size), jnp.float32),
            pltpu.VMEM(blocks.shape, blocks.dtype),
            pltpu.VMEM((rank, count * rank), jnp.bfloat16),
            pltpu.VMEM((rank, count * rank), jnp.bfloat16),
            pltpu.VMEM((heights - 1, 2 * rank, 2 * rank), jnp.float32),
            tasks,
            tasks,
        ),
        scratch_shapes=[
            tasks,
            pltpu.VMEM((3, TASK_ROWS, LANES), jnp.int32),
            pltpu.VMEM((slots, count), jnp.int32),
            pltpu.VMEM((1, count), jnp.int32),
            pltpu.VMEM(own.shape, own.dtype),
            pltpu.VMEM(samples.shape, samples.dtype),
            pltpu.VMEM((count + 1, columns, size), jnp.bfloat16),
            pltpu.SemaphoreType.DMA((8,)),
        ],
        compiler_params=params(8),
        name="own_pass",
    )(
        far(index),
        far(number),
        resident(upper),
        resident(mats),
        far(own),
        far(samples),
        far(blocks),
    )


def side_pass(tasks, side, near, blocks):
    count, columns, size = near.shape
    slots = blocks.shape[0] // count

    def kernel(task_ref, side_ref, near_ref, blocks_ref, acc, source):
        side_kernel(task_ref, side_ref, near_ref, blocks_ref, slots, acc, source)

    return pl.pallas_call(
        kernel,
        in_specs=[SMEM] + [VMEM] * 3,
        out_specs=VMEM,
        out_shape=pltpu.VMEM((count, columns, size), jnp.float32),
        input_output_aliases={2: 0},
        scratch_shapes=[pltpu.VMEM((count + 1, columns, size), jnp.bfloat16)],
        compiler_params=params(8),
        name="side_pass",
    )(tasks, resident(side), near, blocks)


def far_pass(tasks, side, near, blocks, basis, path_high, path_low):
    count, rank, size = basis.shape
    columns = side.shape[0]
    return pl.pallas_call(
        far_kernel,
        in_specs=[SMEM] + [VMEM] * 6,
        out_specs=(ANY, VMEM, VMEM, VMEM),
        out_shape=(
            pltpu.HBM((count, rank, columns), jnp.float32),
            pltpu.VMEM((count * rank, columns), jnp.bfloat16),
            pltpu.VMEM((columns // 2, 2 * rank), jnp.float32),
            pltpu.VMEM((count, columns, size), jnp.float32),
        ),
        input_output_aliases={2: 3},
        scratch_shapes=[
            pltpu.VMEM((count + 1, columns, size), jnp.bfloat16),
            pltpu.VMEM((count * rank, columns), jnp.bfloat16),
            pltpu.VMEM((count, rank, columns), jnp.float32),
            pltpu.SemaphoreType.DMA((count // PER_STEP,)),
        ],
        compiler_params=params(8),
        name="far_pass",
    )(tasks, resident(side), near, blocks, resident(basis), path_high, path_low)


def gram_pass(place, high, count, parts):
    columns = high.shape[1]
    rank = high.shape[0] // count
    pairs = count // 2
    shape = (parts // 2, rank // parts, pairs, 2 * rank)
    return pl.pallas_call(
        functools.partial(gram_kernel, 1.0 / (columns * parts)),
        in_specs=[SMEM, VMEM],
        out_specs=(VMEM, VMEM),
        out_shape=(pltpu.VMEM(shape, jnp.float32), pltpu.VMEM(shape, jnp.float32)),
        scratch_shapes=[pltpu.VMEM((rank * pairs, 2 * rank), jnp.float32)],
        compiler_params=params(8),
        name="gram_pass",
    )(place, high)


def exchange(value, axis, flip):
    return lax.ppermute(value, axis, [(i, i ^ flip) for i in range(lax.axis_size(axis))])


def swap(value, axis, first):
    pairs = [(i, i + 1) for i in range(first, lax.axis_size(axis) - 1, 2)]
    return lax.ppermute(value, axis, pairs + [(j, i) for i, j in pairs])


def shards(
    samples, omega, leaf_basis, near_blocks, near_index, near_count, inner_transfer, upper_transfer
):
    count = near_count.shape[0]
    slots = near_index.shape[1]
    rank = leaf_basis.shape[1]
    size = leaf_basis.shape[2]
    groups = lax.axis_size("leaf")
    parts = lax.axis_size("samp")
    device = lax.axis_index("leaf")
    place = lax.axis_index("samp").astype(jnp.int32)

    own = omega.T
    first = swap(own, "leaf", 1)
    second = swap(own, "leaf", 0)

    heights = groups.bit_length() - 1
    rows = []
    offset, width = 0, groups
    for height in range(heights):
        rows.append(
            lax.dynamic_slice_in_dim(
                upper_transfer, offset + jnp.right_shift(device, height), 1, axis=0
            )
        )
        offset, width = offset + width, width // 2
    upper = jnp.concatenate(rows, axis=0).reshape(heights, rank, rank)

    blocks = near_blocks.reshape(count * slots, size, size)
    near, blocks, path_high, path_low, twice, tasks, later_tasks = own_pass(
        near_index.T,
        near_count.reshape(1, count),
        upper,
        inner_transfer.reshape(-1, rank),
        own,
        samples.T,
        blocks,
    )
    near = side_pass(tasks, first, near, blocks)
    coeffs, high, part, _ = far_pass(
        later_tasks, second, near, blocks, leaf_basis, path_high, path_low
    )

    flips = (1, 3, 4, 8, 24)
    levels = []
    accum = part
    gram, middle = None, None
    for height in range(heights):
        if height:
            accum = jnp.dot(accum, twice[height - 1], precision=lax.Precision.HIGHEST)
        other = exchange(accum, "leaf", flips[height])
        if height == 0:
            keep, send = gram_pass(place.reshape(1), high, count, parts)
            got = exchange(send, "samp", 1)
        elif height == 2:
            gram = keep + got
            middle = gram[1:3].astype(jnp.bfloat16)
            other, _ = lax.optimization_barrier((other, middle))
            got = exchange(middle, "samp", 2).astype(jnp.float32)
        elif height == 3:
            near_total = gram[0] + got[0]
            far_total = gram[3] + got[1]
            other, _ = lax.optimization_barrier((other, far_total))
            got = exchange(far_total, "samp", 6)
        elif height == 4:
            leaf_gram = pl.pallas_call(
                finish_kernel,
                in_specs=[VMEM, VMEM],
                out_specs=VMEM,
                out_shape=jax.ShapeDtypeStruct((count, rank * rank // parts), jnp.float32),
                compiler_params=params(8),
                name="finish",
            )(resident(near_total), resident(got))
            other, _ = lax.optimization_barrier((other, leaf_gram))
        accum = accum + other
        levels.append(accum)
    ancestors = pl.pallas_call(
        turn_kernel,
        in_specs=[VMEM] * heights,
        out_specs=VMEM,
        out_shape=jax.ShapeDtypeStruct((heights, rank, 2 * part.shape[0]), jnp.float32),
        compiler_params=params(8),
        name="turn",
    )(*map(resident, levels))
    return coeffs, leaf_gram, ancestors[None]


def solution(mesh):
    return jax.shard_map(
        shards,
        mesh=mesh,
        in_specs=(
            P("leaf", "samp"),
            P("leaf", "samp"),
            P("leaf", None, None),
            P("leaf", None, None, None),
            P("leaf", None),
            P("leaf"),
            P("leaf", None),
            P(),
        ),
        out_specs=(P("leaf", None, "samp"), P("leaf", "samp"), P("leaf", None, None, "samp")),
        check_vma=False,
    )
```

```python
import functools

import jax
import jax.numpy as jnp
from jax import lax
from jax.experimental import pallas as pl
from jax.experimental.pallas import tpu as pltpu
from jax.sharding import PartitionSpec as P

NT = (((1,), (1,)), ((), ()))
NN = (((1,), (0,)), ((), ()))
PER_STEP = 8
PER_TASKS = 2 * PER_STEP
LANES = 128
TASK_ROWS = 8
LIST_ROWS = 3
VMEM = pl.BlockSpec(memory_space=pltpu.VMEM)
SMEM = pl.BlockSpec(memory_space=pltpu.SMEM)
ANY = pl.BlockSpec(memory_space=pl.ANY)


def dot(a, b, dims):
    return lax.dot_general(a, b, dims, preferred_element_type=jnp.float32)


def split(value):
    high = value.astype(jnp.bfloat16)
    return high, (value - high.astype(jnp.float32)).astype(jnp.bfloat16)


def resident(value):
    return pltpu.with_memory_space_constraint(value, pltpu.VMEM)


def spread(source, first, ref, size):
    for leaf in range(ref.shape[1] // size):
        source[first + leaf] = ref[:, leaf * size : (leaf + 1) * size]


def subtract_near(count, task_ref, source, blocks_ref, acc_ref, slots):
    shift = count.bit_length()
    low = (1 << shift) - 1
    per_row = LANES // PER_TASKS

    def body(step, carry):
        done = []
        row = lax.div(step, per_row)
        at = lax.rem(step, per_row) * PER_TASKS
        for task in range(PER_STEP):
            one = task_ref[row, at + 2 * task]
            two = task_ref[row, at + 2 * task + 1]
            left, right = jnp.right_shift(one, shift), jnp.right_shift(two, shift)
            fetched = jnp.concatenate(
                [source[jnp.bitwise_and(one, low)], source[jnp.bitwise_and(two, low)]], axis=1
            )
            matrix = jnp.concatenate([blocks_ref[left], blocks_ref[right]], axis=1)
            done.append((lax.div(left, slots), dot(fetched, matrix, NT)))
        for leaf, near in done:
            acc_ref[leaf] = acc_ref[leaf] - near
        return carry

    lax.fori_loop(0, task_ref[LIST_ROWS - 1, LANES - 1], body, 0)


def list_tasks(index, number, device, lists_ref):
    slots, count = index.shape
    shift = count.bit_length()
    slot = lax.broadcasted_iota(jnp.int32, (slots, count), 0)
    leaf = lax.broadcasted_iota(jnp.int32, (slots, count), 1)
    at = index - (device * count - count)
    alive = slot < number
    before, after = at < count, at >= 2 * count
    even = jnp.broadcast_to(jnp.bitwise_and(device, 1), at.shape) == 0
    side = jnp.where(before == even, 1, 2)
    kind = jnp.where(jnp.logical_or(before, after), side, 0)
    code = jnp.left_shift(leaf * slots + slot, shift) + jnp.bitwise_and(at, count - 1)
    blank = count
    earlier_slot = (
        lax.broadcasted_iota(jnp.int32, (slots, slots), 1)
        < lax.broadcasted_iota(jnp.int32, (slots, slots), 0)
    ).astype(jnp.bfloat16)
    earlier_leaf = (
        lax.broadcasted_iota(jnp.int32, (count, count), 0)
        < lax.broadcasted_iota(jnp.int32, (count, count), 1)
    ).astype(jnp.bfloat16)
    place = jnp.full((slots, count), -1, jnp.int32)
    steps = []
    for which in range(3):
        chosen = jnp.logical_and(alive, kind == which)
        mark = jnp.where(chosen, 1.0, 0.0)
        rank = dot(earlier_slot, mark.astype(jnp.bfloat16), NN)
        number_here = jnp.sum(mark, axis=0, keepdims=True).astype(jnp.int32)
        padded = (number_here + jnp.bitwise_and(number_here, 1)).astype(jnp.float32)
        base = dot(jnp.broadcast_to(padded, (slots, count)).astype(jnp.bfloat16), earlier_leaf, NN)
        here = (base + rank).astype(jnp.int32) + which * LIST_ROWS * LANES
        place = jnp.where(chosen, here, place)
        total = jnp.sum(padded, axis=1, keepdims=True).astype(jnp.int32)
        steps.append(jnp.right_shift(total + PER_TASKS - 1, PER_TASKS.bit_length() - 1))
    place, value = place.T, code.T - blank
    lane = lax.broadcasted_iota(jnp.int32, (count, LANES), 1)
    for which in range(3):
        for row in range(LIST_ROWS):
            target = lane + (which * LIST_ROWS + row) * LANES
            total = jnp.zeros((count, LANES), jnp.int32)
            for k in range(slots):
                total += jnp.where(place[:, k : k + 1] == target, value[:, k : k + 1], 0)
            line = jnp.sum(total, axis=0, keepdims=True) + blank
            if row == LIST_ROWS - 1:
                line = jnp.where(lane[:1] == LANES - 1, steps[which], line)
            lists_ref[which, row : row + 1] = line


def path_products(upper_ref, mats_ref, basis_ref, weight_ref):
    count, rank, size = basis_ref.shape
    nodes = [split(upper_ref[0].astype(jnp.float32).T)]
    blank = jnp.zeros((rank, size), basis_ref.dtype)
    width = 2
    offset = 2 * count - 2
    while width <= count:
        offset = offset - width
        later = []
        for parent, (high, low) in enumerate(nodes):
            first = (offset + 2 * parent) * rank
            pair = mats_ref[first : first + 2 * rank, :]
            product = dot(high, pair, NT) + dot(low, pair, NT)
            pair_high, pair_low = split(product)
            if width == count:
                bases = jnp.concatenate(
                    [
                        jnp.concatenate([basis_ref[2 * parent], blank], axis=1),
                        jnp.concatenate([blank, basis_ref[2 * parent + 1]], axis=1),
                    ],
                    axis=0,
                )
                weight = split(dot(pair_high, bases, NN) + dot(pair_low, bases, NN))
                at = slice(2 * parent * size, 2 * (parent + 1) * size)
                weight_ref[:rank, at], weight_ref[rank:, at] = weight
            else:
                later.append((pair_high[:, :rank], pair_low[:, :rank]))
                later.append((pair_high[:, rank:], pair_low[:, rank:]))
        nodes = later
        width = 2 * width


def own_kernel(
    index_any,
    number_any,
    upper_ref,
    mats_ref,
    own_any,
    samples_any,
    blocks_any,
    basis_any,
    acc_ref,
    blocks_ref,
    basis_ref,
    weight_ref,
    twice_ref,
    first_task_ref,
    second_task_ref,
    own_task,
    lists,
    index_ref,
    number_ref,
    own_ref,
    samples_ref,
    source,
    sems,
):
    pairs = (
        (index_any, index_ref),
        (number_any, number_ref),
        (own_any, own_ref),
        (samples_any, samples_ref),
        (blocks_any, blocks_ref),
        (basis_any, basis_ref),
        (lists.at[0], own_task),
        (lists.at[1], first_task_ref),
        (lists.at[2], second_task_ref),
    )
    copies = [
        pltpu.make_async_copy(origin, target, sems.at[place])
        for place, (origin, target) in enumerate(pairs)
    ]
    for copy in copies[:6]:
        copy.start()
    slots, count = index_ref.shape
    size = blocks_ref.shape[1]
    rank = upper_ref.shape[1]
    copies[0].wait()
    copies[1].wait()
    list_tasks(index_ref[...], number_ref[...], lax.axis_index("leaf"), lists)
    for copy in copies[6:]:
        copy.start()
    for height in range(1, upper_ref.shape[0]):
        matrix = upper_ref[height].astype(jnp.float32)
        blank = jnp.zeros_like(matrix)
        twice_ref[height - 1, :rank] = jnp.concatenate([matrix, blank], axis=1)
        twice_ref[height - 1, rank:] = jnp.concatenate([blank, matrix], axis=1)
    copies[2].wait()
    spread(source, 0, own_ref, size)
    source[count] = jnp.zeros_like(source[count])
    copies[3].wait()
    for leaf in range(count):
        acc_ref[leaf] = samples_ref[:, leaf * size : (leaf + 1) * size].astype(jnp.float32)
    for copy in copies[4:]:
        copy.wait()
    path_products(upper_ref, mats_ref, basis_ref, weight_ref)
    subtract_near(count, own_task, source, blocks_ref, acc_ref, slots)


def side_kernel(task_ref, side_ref, near_ref, blocks_ref, slots, acc, source):
    del near_ref
    count, _, size = acc.shape
    spread(source, 0, side_ref, size)
    source[count] = jnp.zeros_like(source[count])
    subtract_near(count, task_ref, source, blocks_ref, acc, slots)


def far_kernel(
    task_ref, side_ref, near_ref, blocks_ref, weight_ref, far_ref, part_ref, acc, source
):
    count, _, size = acc.shape
    slots = blocks_ref.shape[0] // count
    side_kernel(task_ref, side_ref, near_ref, blocks_ref, slots, acc, source)
    for leaf in range(count):
        far_ref[:, leaf * size : (leaf + 1) * size] = acc[leaf].astype(jnp.bfloat16)
    product = dot(weight_ref[...], far_ref[...], NT)
    rank = product.shape[0] // 2
    turned = (product[:rank] + product[rank:]).T
    half = turned.shape[0] // 2
    part_ref[...] = jnp.concatenate([turned[:half], turned[half:]], axis=1)


def gram_kernel(
    scale, place_ref, far_ref, basis_ref, coeff_any, keep_ref, send_ref, gram, coeff_ref, sems
):
    parts, rows, pairs, width = keep_ref.shape
    parts = 2 * parts
    rank = width // 2
    size = basis_ref.shape[2]
    lane = lax.broadcasted_iota(jnp.int32, (rank, width), 1)
    copies = []
    for first in range(0, pairs, PER_STEP):
        stacks = []
        for pair in range(first, first + PER_STEP):
            both = []
            for leaf in (pair, pair + pairs):
                far = far_ref[:, leaf * size : (leaf + 1) * size]
                coeff = dot(basis_ref[leaf], far, NT)
                coeff_ref[leaf] = coeff
                both.append(coeff.astype(jnp.bfloat16))
            stacks.append(jnp.concatenate(both, axis=0))
        for start in (first, first + pairs):
            these = pl.ds(start, PER_STEP)
            copies.append(
                pltpu.make_async_copy(
                    coeff_ref.at[these], coeff_any.at[these], sems.at[len(copies)]
                )
            )
            copies[-1].start()
        for pair, stacked in enumerate(stacks, first):
            product = dot(stacked, stacked, NT)
            value = jnp.where(lane < rank, product[:rank], product[rank:]) * scale
            gram[pl.ds(pair, rank, stride=pairs), :] = value
    for relative in range(parts):
        first = jnp.bitwise_xor(place_ref[0], relative) * rows
        target = send_ref if relative % 2 else keep_ref
        for row in range(rows):
            at = pl.multiple_of((first + row) * pairs, pairs)
            target[relative // 2, row] = gram[pl.ds(at, pairs), :]
    for copy in copies:
        copy.wait()


def finish_kernel(keep_ref, got_ref, *refs):
    others, out_ref = refs[:-1], refs[-1]
    _, rows, pairs, width = keep_ref.shape
    half = width // 2
    lane = lax.broadcasted_iota(jnp.int32, (pairs, width), 1)
    for row in range(0, rows, 2):
        even, odd = (keep_ref[0, at] + got_ref[0, at] for at in (row, row + 1))
        for other in others:
            even, odd = even + other[row], odd + other[row + 1]
        at = slice(row * half, (row + 2) * half)
        out_ref[:pairs, at] = jnp.where(lane < half, even, pltpu.roll(odd, half, 1))
        out_ref[pairs:, at] = jnp.where(lane < half, pltpu.roll(even, half, 1), odd)


def turn_kernel(*refs):
    levels, out_ref = refs[:-1], refs[-1]
    for height, level in enumerate(levels):
        turned = level[...].T
        half = turned.shape[0] // 2
        out_ref[height] = jnp.concatenate([turned[:half], turned[half:]], axis=1)


def params(mib):
    return pltpu.CompilerParams(vmem_limit_bytes=mib * 2**20)


def own_pass(index, number, upper, mats, own, samples, blocks, basis):
    slots, count = index.shape
    size = blocks.shape[1]
    columns = own.shape[0]
    heights, rank, _ = upper.shape
    tasks = pltpu.SMEM((TASK_ROWS, LANES), jnp.int32)
    far = lambda value: pltpu.with_memory_space_constraint(value, pltpu.HBM)
    return pl.pallas_call(
        own_kernel,
        in_specs=[ANY, ANY, VMEM, VMEM, ANY, ANY, ANY, ANY],
        out_specs=(VMEM, VMEM, VMEM, VMEM, VMEM, SMEM, SMEM),
        out_shape=(
            pltpu.VMEM((count, columns, size), jnp.float32),
            pltpu.VMEM(blocks.shape, blocks.dtype),
            pltpu.VMEM(basis.shape, basis.dtype),
            pltpu.VMEM((2 * rank, count * size), jnp.bfloat16),
            pltpu.VMEM((heights - 1, 2 * rank, 2 * rank), jnp.float32),
            tasks,
            tasks,
        ),
        scratch_shapes=[
            tasks,
            pltpu.VMEM((3, TASK_ROWS, LANES), jnp.int32),
            pltpu.VMEM((slots, count), jnp.int32),
            pltpu.VMEM((1, count), jnp.int32),
            pltpu.VMEM(own.shape, own.dtype),
            pltpu.VMEM(samples.shape, samples.dtype),
            pltpu.VMEM((count + 1, columns, size), jnp.bfloat16),
            pltpu.SemaphoreType.DMA((9,)),
        ],
        compiler_params=params(8),
        name="own_pass",
    )(
        far(index),
        far(number),
        resident(upper),
        resident(mats),
        far(own),
        far(samples),
        far(blocks),
        far(basis),
    )


def side_pass(tasks, side, near, blocks):
    count, columns, size = near.shape
    slots = blocks.shape[0] // count

    def kernel(task_ref, side_ref, near_ref, blocks_ref, acc, source):
        side_kernel(task_ref, side_ref, near_ref, blocks_ref, slots, acc, source)

    return pl.pallas_call(
        kernel,
        in_specs=[SMEM] + [VMEM] * 3,
        out_specs=VMEM,
        out_shape=pltpu.VMEM((count, columns, size), jnp.float32),
        input_output_aliases={2: 0},
        scratch_shapes=[pltpu.VMEM((count + 1, columns, size), jnp.bfloat16)],
        compiler_params=params(8),
        name="side_pass",
    )(tasks, resident(side), near, blocks)


def far_pass(tasks, side, near, blocks, weight):
    count, columns, size = near.shape
    rank = weight.shape[0] // 2
    return pl.pallas_call(
        far_kernel,
        in_specs=[SMEM] + [VMEM] * 4,
        out_specs=(VMEM, VMEM, VMEM),
        out_shape=(
            pltpu.VMEM((columns, count * size), jnp.bfloat16),
            pltpu.VMEM((columns // 2, 2 * rank), jnp.float32),
            pltpu.VMEM((count, columns, size), jnp.float32),
        ),
        input_output_aliases={2: 2},
        scratch_shapes=[pltpu.VMEM((count + 1, columns, size), jnp.bfloat16)],
        compiler_params=params(8),
        name="far_pass",
    )(tasks, resident(side), near, blocks, weight)


def gram_pass(place, far, basis, parts):
    count, rank, _ = basis.shape
    columns = far.shape[0]
    pairs = count // 2
    shape = (parts // 2, rank // parts, pairs, 2 * rank)
    return pl.pallas_call(
        functools.partial(gram_kernel, 1.0 / (columns * parts)),
        in_specs=[SMEM, VMEM, VMEM],
        out_specs=(ANY, VMEM, VMEM),
        out_shape=(
            pltpu.HBM((count, rank, columns), jnp.float32),
            pltpu.VMEM(shape, jnp.float32),
            pltpu.VMEM(shape, jnp.float32),
        ),
        scratch_shapes=[
            pltpu.VMEM((rank * pairs, 2 * rank), jnp.float32),
            pltpu.VMEM((count, rank, columns), jnp.float32),
            pltpu.SemaphoreType.DMA((count // PER_STEP,)),
        ],
        compiler_params=params(8),
        name="gram_pass",
    )(place, far, basis)


def exchange(value, axis, flip):
    return lax.ppermute(value, axis, [(i, i ^ flip) for i in range(lax.axis_size(axis))])


def swap(value, axis, first):
    pairs = [(i, i + 1) for i in range(first, lax.axis_size(axis) - 1, 2)]
    return lax.ppermute(value, axis, pairs + [(j, i) for i, j in pairs])


def shards(
    samples, omega, leaf_basis, near_blocks, near_index, near_count, inner_transfer, upper_transfer
):
    count = near_count.shape[0]
    slots = near_index.shape[1]
    rank = leaf_basis.shape[1]
    size = leaf_basis.shape[2]
    groups = lax.axis_size("leaf")
    parts = lax.axis_size("samp")
    device = lax.axis_index("leaf")
    place = lax.axis_index("samp").astype(jnp.int32)

    own = omega.T
    first = swap(own, "leaf", 1)
    second = swap(own, "leaf", 0)

    heights = groups.bit_length() - 1
    rows = []
    offset, width = 0, groups
    for height in range(heights):
        rows.append(
            lax.dynamic_slice_in_dim(
                upper_transfer, offset + jnp.right_shift(device, height), 1, axis=0
            )
        )
        offset, width = offset + width, width // 2
    upper = jnp.concatenate(rows, axis=0).reshape(heights, rank, rank)

    blocks = near_blocks.reshape(count * slots, size, size)
    near, blocks, basis, weight, twice, crossing_tasks, tasks = own_pass(
        near_index.T,
        near_count.reshape(1, count),
        upper,
        inner_transfer.reshape(-1, rank),
        own,
        samples.T,
        blocks,
        leaf_basis,
    )
    near = side_pass(tasks, second, near, blocks)
    far, part, _ = far_pass(crossing_tasks, first, near, blocks, weight)

    flips = (1, 3, 4, 8, 24)
    levels = []
    accum = part
    for height in range(heights):
        if height:
            accum = jnp.dot(accum, twice[height - 1], precision=lax.Precision.HIGHEST)
        other = exchange(accum, "leaf", flips[height])
        if height == 0:
            coeffs, keep, send = gram_pass(place.reshape(1), far, basis, parts)
            got = exchange(send, "samp", 1)
        elif height == 2:
            leaving = keep[1] + got[1]
            other, _ = lax.optimization_barrier((other, leaving))
            received = [exchange(leaving, "samp", 2)]
        elif height == 3:
            received += [exchange(keep[x] + got[x], "samp", 2 * x) for x in (2, 3)]
            other, _ = lax.optimization_barrier((other, received[0]))
        elif height == 4:
            leaf_gram = pl.pallas_call(
                finish_kernel,
                in_specs=[VMEM] * 5,
                out_specs=VMEM,
                out_shape=jax.ShapeDtypeStruct((count, rank * rank // parts), jnp.float32),
                compiler_params=params(8),
                name="finish",
            )(keep, *map(resident, [got] + received))
            other, _ = lax.optimization_barrier((other, leaf_gram))
        accum = accum + other
        levels.append(accum)
    ancestors = pl.pallas_call(
        turn_kernel,
        in_specs=[VMEM] * heights,
        out_specs=VMEM,
        out_shape=jax.ShapeDtypeStruct((heights, rank, 2 * part.shape[0]), jnp.float32),
        compiler_params=params(8),
        name="turn",
    )(*map(resident, levels))
    return coeffs, leaf_gram, ancestors[None]


def solution(mesh):
    return jax.shard_map(
        shards,
        mesh=mesh,
        in_specs=(
            P("leaf", "samp"),
            P("leaf", "samp"),
            P("leaf", None, None),
            P("leaf", None, None, None),
            P("leaf", None),
            P("leaf"),
            P("leaf", None),
            P(),
        ),
        out_specs=(P("leaf", None, "samp"), P("leaf", "samp"), P("leaf", None, None, "samp")),
        check_vma=False,
    )
```

```python
import functools

import jax
import jax.numpy as jnp
from jax import lax
from jax.experimental import pallas as pl
from jax.experimental.pallas import tpu as pltpu
from jax.sharding import PartitionSpec as P

NT = (((1,), (1,)), ((), ()))
NN = (((1,), (0,)), ((), ()))
PER_STEP = 8
PER_TASKS = 2 * PER_STEP
LANES = 128
TASK_ROWS = 8
LIST_ROWS = 3
VMEM = pl.BlockSpec(memory_space=pltpu.VMEM)
SMEM = pl.BlockSpec(memory_space=pltpu.SMEM)
ANY = pl.BlockSpec(memory_space=pl.ANY)


def dot(a, b, dims):
    return lax.dot_general(a, b, dims, preferred_element_type=jnp.float32)


def split(value):
    high = value.astype(jnp.bfloat16)
    return high, (value - high.astype(jnp.float32)).astype(jnp.bfloat16)


def resident(value):
    return pltpu.with_memory_space_constraint(value, pltpu.VMEM)


def spread(source, first, ref, size):
    for leaf in range(ref.shape[1] // size):
        source[first + leaf] = ref[:, leaf * size : (leaf + 1) * size]


def subtract_near(count, task_ref, source, blocks_ref, acc_ref, slots):
    shift = count.bit_length()
    low = (1 << shift) - 1
    per_row = LANES // PER_TASKS

    def body(step, carry):
        done = []
        row = lax.div(step, per_row)
        at = lax.rem(step, per_row) * PER_TASKS
        for task in range(PER_STEP):
            one = task_ref[row, at + 2 * task]
            two = task_ref[row, at + 2 * task + 1]
            left, right = jnp.right_shift(one, shift), jnp.right_shift(two, shift)
            fetched = jnp.concatenate(
                [source[jnp.bitwise_and(one, low)], source[jnp.bitwise_and(two, low)]], axis=1
            )
            matrix = jnp.concatenate([blocks_ref[left], blocks_ref[right]], axis=1)
            done.append((lax.div(left, slots), dot(fetched, matrix, NT)))
        for leaf, near in done:
            acc_ref[leaf] = acc_ref[leaf] - near
        return carry

    lax.fori_loop(0, task_ref[LIST_ROWS - 1, LANES - 1], body, 0)


def list_tasks(index, number, device, lists_ref):
    slots, count = index.shape
    shift = count.bit_length()
    slot = lax.broadcasted_iota(jnp.int32, (slots, count), 0)
    leaf = lax.broadcasted_iota(jnp.int32, (slots, count), 1)
    at = index - (device * count - count)
    alive = slot < number
    before, after = at < count, at >= 2 * count
    even = jnp.broadcast_to(jnp.bitwise_and(device, 1), at.shape) == 0
    side = jnp.where(before == even, 1, 2)
    kind = jnp.where(jnp.logical_or(before, after), side, 0)
    code = jnp.left_shift(leaf * slots + slot, shift) + jnp.bitwise_and(at, count - 1)
    blank = count
    earlier_slot = (
        lax.broadcasted_iota(jnp.int32, (slots, slots), 1)
        < lax.broadcasted_iota(jnp.int32, (slots, slots), 0)
    ).astype(jnp.bfloat16)
    earlier_leaf = (
        lax.broadcasted_iota(jnp.int32, (count, count), 0)
        < lax.broadcasted_iota(jnp.int32, (count, count), 1)
    ).astype(jnp.bfloat16)
    place = jnp.full((slots, count), -1, jnp.int32)
    steps = []
    for which in range(3):
        chosen = jnp.logical_and(alive, kind == which)
        mark = jnp.where(chosen, 1.0, 0.0)
        rank = dot(earlier_slot, mark.astype(jnp.bfloat16), NN)
        number_here = jnp.sum(mark, axis=0, keepdims=True).astype(jnp.int32)
        padded = (number_here + jnp.bitwise_and(number_here, 1)).astype(jnp.float32)
        base = dot(jnp.broadcast_to(padded, (slots, count)).astype(jnp.bfloat16), earlier_leaf, NN)
        here = (base + rank).astype(jnp.int32) + which * LIST_ROWS * LANES
        place = jnp.where(chosen, here, place)
        total = jnp.sum(padded, axis=1, keepdims=True).astype(jnp.int32)
        steps.append(jnp.right_shift(total + PER_TASKS - 1, PER_TASKS.bit_length() - 1))
    place, value = place.T, code.T - blank
    lane = lax.broadcasted_iota(jnp.int32, (count, LANES), 1)
    for which in range(3):
        for row in range(LIST_ROWS):
            target = lane + (which * LIST_ROWS + row) * LANES
            total = jnp.zeros((count, LANES), jnp.int32)
            for k in range(slots):
                total += jnp.where(place[:, k : k + 1] == target, value[:, k : k + 1], 0)
            line = jnp.sum(total, axis=0, keepdims=True) + blank
            if row == LIST_ROWS - 1:
                line = jnp.where(lane[:1] == LANES - 1, steps[which], line)
            lists_ref[which, row : row + 1] = line


def path_products(upper_ref, mats_ref, basis_ref, weight_ref):
    count, rank, size = basis_ref.shape
    nodes = [split(upper_ref[0].astype(jnp.float32).T)]
    blank = jnp.zeros((rank, size), basis_ref.dtype)
    width = 2
    offset = 2 * count - 2
    while width <= count:
        offset = offset - width
        later = []
        for parent, (high, low) in enumerate(nodes):
            first = (offset + 2 * parent) * rank
            pair = mats_ref[first : first + 2 * rank, :]
            product = dot(high, pair, NT) + dot(low, pair, NT)
            pair_high, pair_low = split(product)
            if width == count:
                bases = jnp.concatenate(
                    [
                        jnp.concatenate([basis_ref[2 * parent], blank], axis=1),
                        jnp.concatenate([blank, basis_ref[2 * parent + 1]], axis=1),
                    ],
                    axis=0,
                )
                weight = split(dot(pair_high, bases, NN) + dot(pair_low, bases, NN))
                at = slice(2 * parent * size, 2 * (parent + 1) * size)
                weight_ref[:rank, at], weight_ref[rank:, at] = weight
            else:
                later.append((pair_high[:, :rank], pair_low[:, :rank]))
                later.append((pair_high[:, rank:], pair_low[:, rank:]))
        nodes = later
        width = 2 * width


def own_kernel(
    index_any,
    number_any,
    upper_ref,
    mats_ref,
    own_any,
    samples_any,
    blocks_any,
    basis_any,
    acc_ref,
    blocks_ref,
    basis_ref,
    weight_ref,
    twice_ref,
    first_task_ref,
    second_task_ref,
    own_task,
    lists,
    index_ref,
    number_ref,
    own_ref,
    samples_ref,
    source,
    sems,
):
    pairs = (
        (index_any, index_ref),
        (number_any, number_ref),
        (basis_any, basis_ref),
        (own_any, own_ref),
        (samples_any, samples_ref),
        (blocks_any, blocks_ref),
        (lists.at[0], own_task),
        (lists.at[1], first_task_ref),
        (lists.at[2], second_task_ref),
    )
    copies = [
        pltpu.make_async_copy(origin, target, sems.at[place])
        for place, (origin, target) in enumerate(pairs)
    ]
    for copy in copies[:6]:
        copy.start()
    slots, count = index_ref.shape
    size = blocks_ref.shape[1]
    rank = upper_ref.shape[1]
    copies[0].wait()
    copies[1].wait()
    list_tasks(index_ref[...], number_ref[...], lax.axis_index("leaf"), lists)
    for copy in copies[6:]:
        copy.start()
    copies[2].wait()
    path_products(upper_ref, mats_ref, basis_ref, weight_ref)
    for height in range(1, upper_ref.shape[0]):
        matrix = upper_ref[height].astype(jnp.float32)
        blank = jnp.zeros_like(matrix)
        twice_ref[height - 1, :rank] = jnp.concatenate([matrix, blank], axis=1)
        twice_ref[height - 1, rank:] = jnp.concatenate([blank, matrix], axis=1)
    copies[3].wait()
    spread(source, 0, own_ref, size)
    source[count] = jnp.zeros_like(source[count])
    copies[4].wait()
    for leaf in range(count):
        acc_ref[leaf] = samples_ref[:, leaf * size : (leaf + 1) * size].astype(jnp.float32)
    for copy in copies[5:]:
        copy.wait()
    subtract_near(count, own_task, source, blocks_ref, acc_ref, slots)


def side_kernel(task_ref, side_ref, near_ref, blocks_ref, slots, acc, source):
    del near_ref
    count, _, size = acc.shape
    spread(source, 0, side_ref, size)
    source[count] = jnp.zeros_like(source[count])
    subtract_near(count, task_ref, source, blocks_ref, acc, slots)


def far_kernel(
    task_ref, side_ref, near_ref, blocks_ref, weight_ref, far_ref, part_ref, acc, source
):
    count, _, size = acc.shape
    slots = blocks_ref.shape[0] // count
    side_kernel(task_ref, side_ref, near_ref, blocks_ref, slots, acc, source)
    for leaf in range(count):
        far_ref[:, leaf * size : (leaf + 1) * size] = acc[leaf].astype(jnp.bfloat16)
    product = dot(weight_ref[...], far_ref[...], NT)
    rank = product.shape[0] // 2
    turned = (product[:rank] + product[rank:]).T
    half = turned.shape[0] // 2
    part_ref[...] = jnp.concatenate([turned[:half], turned[half:]], axis=1)


def gram_kernel(
    scale, place_ref, far_ref, basis_ref, coeff_any, keep_ref, send_ref, gram, coeff_ref, sems
):
    parts, rows, pairs, width = keep_ref.shape
    parts = 2 * parts
    rank = width // 2
    size = basis_ref.shape[2]
    lane = lax.broadcasted_iota(jnp.int32, (rank, width), 1)
    copies = []
    for first in range(0, pairs, PER_STEP):
        stacks = []
        for pair in range(first, first + PER_STEP):
            both = []
            for leaf in (pair, pair + pairs):
                far = far_ref[:, leaf * size : (leaf + 1) * size]
                coeff = dot(basis_ref[leaf], far, NT)
                coeff_ref[leaf] = coeff
                both.append(coeff.astype(jnp.bfloat16))
            stacks.append(jnp.concatenate(both, axis=0))
        for start in (first, first + pairs):
            these = pl.ds(start, PER_STEP)
            copies.append(
                pltpu.make_async_copy(
                    coeff_ref.at[these], coeff_any.at[these], sems.at[len(copies)]
                )
            )
            copies[-1].start()
        for pair, stacked in enumerate(stacks, first):
            product = dot(stacked, stacked, NT)
            value = jnp.where(lane < rank, product[:rank], product[rank:]) * scale
            gram[pl.ds(pair, rank, stride=pairs), :] = value
    for relative in range(parts):
        first = jnp.bitwise_xor(place_ref[0], relative) * rows
        target = send_ref if relative % 2 else keep_ref
        for row in range(rows):
            at = pl.multiple_of((first + row) * pairs, pairs)
            target[relative // 2, row] = gram[pl.ds(at, pairs), :]
    for copy in copies:
        copy.wait()


def finish_kernel(keep_ref, got_ref, *refs):
    others, out_ref = refs[:-1], refs[-1]
    _, rows, pairs, width = keep_ref.shape
    half = width // 2
    lane = lax.broadcasted_iota(jnp.int32, (pairs, width), 1)
    for row in range(0, rows, 2):
        even, odd = (keep_ref[0, at] + got_ref[0, at] for at in (row, row + 1))
        for other in others:
            even, odd = even + other[row], odd + other[row + 1]
        at = slice(row * half, (row + 2) * half)
        out_ref[:pairs, at] = jnp.where(lane < half, even, pltpu.roll(odd, half, 1))
        out_ref[pairs:, at] = jnp.where(lane < half, pltpu.roll(even, half, 1), odd)


def turn_kernel(*refs):
    levels, out_ref = refs[:-1], refs[-1]
    for height, level in enumerate(levels):
        turned = level[...].T
        half = turned.shape[0] // 2
        out_ref[height] = jnp.concatenate([turned[:half], turned[half:]], axis=1)


def params(mib):
    return pltpu.CompilerParams(vmem_limit_bytes=mib * 2**20)


def own_pass(index, number, upper, mats, own, samples, blocks, basis):
    slots, count = index.shape
    size = blocks.shape[1]
    columns = own.shape[0]
    heights, rank, _ = upper.shape
    tasks = pltpu.SMEM((TASK_ROWS, LANES), jnp.int32)
    far = lambda value: pltpu.with_memory_space_constraint(value, pltpu.HBM)
    return pl.pallas_call(
        own_kernel,
        in_specs=[ANY, ANY, VMEM, VMEM, ANY, ANY, ANY, ANY],
        out_specs=(VMEM, VMEM, VMEM, VMEM, VMEM, SMEM, SMEM),
        out_shape=(
            pltpu.VMEM((count, columns, size), jnp.float32),
            pltpu.VMEM(blocks.shape, blocks.dtype),
            pltpu.VMEM(basis.shape, basis.dtype),
            pltpu.VMEM((2 * rank, count * size), jnp.bfloat16),
            pltpu.VMEM((heights - 1, 2 * rank, 2 * rank), jnp.float32),
            tasks,
            tasks,
        ),
        scratch_shapes=[
            tasks,
            pltpu.VMEM((3, TASK_ROWS, LANES), jnp.int32),
            pltpu.VMEM((slots, count), jnp.int32),
            pltpu.VMEM((1, count), jnp.int32),
            pltpu.VMEM(own.shape, own.dtype),
            pltpu.VMEM(samples.shape, samples.dtype),
            pltpu.VMEM((count + 1, columns, size), jnp.bfloat16),
            pltpu.SemaphoreType.DMA((9,)),
        ],
        compiler_params=params(8),
        name="own_pass",
    )(
        far(index),
        far(number),
        resident(upper),
        resident(mats),
        far(own),
        far(samples),
        far(blocks),
        far(basis),
    )


def side_pass(tasks, side, near, blocks):
    count, columns, size = near.shape
    slots = blocks.shape[0] // count

    def kernel(task_ref, side_ref, near_ref, blocks_ref, acc, source):
        side_kernel(task_ref, side_ref, near_ref, blocks_ref, slots, acc, source)

    return pl.pallas_call(
        kernel,
        in_specs=[SMEM] + [VMEM] * 3,
        out_specs=VMEM,
        out_shape=pltpu.VMEM((count, columns, size), jnp.float32),
        input_output_aliases={2: 0},
        scratch_shapes=[pltpu.VMEM((count + 1, columns, size), jnp.bfloat16)],
        compiler_params=params(8),
        name="side_pass",
    )(tasks, resident(side), near, blocks)


def far_pass(tasks, side, near, blocks, weight):
    count, columns, size = near.shape
    rank = weight.shape[0] // 2
    return pl.pallas_call(
        far_kernel,
        in_specs=[SMEM] + [VMEM] * 4,
        out_specs=(VMEM, VMEM, VMEM),
        out_shape=(
            pltpu.VMEM((columns, count * size), jnp.bfloat16),
            pltpu.VMEM((columns // 2, 2 * rank), jnp.float32),
            pltpu.VMEM((count, columns, size), jnp.float32),
        ),
        input_output_aliases={2: 2},
        scratch_shapes=[pltpu.VMEM((count + 1, columns, size), jnp.bfloat16)],
        compiler_params=params(8),
        name="far_pass",
    )(tasks, resident(side), near, blocks, weight)


def gram_pass(place, far, basis, parts):
    count, rank, _ = basis.shape
    columns = far.shape[0]
    pairs = count // 2
    shape = (parts // 2, rank // parts, pairs, 2 * rank)
    return pl.pallas_call(
        functools.partial(gram_kernel, 1.0 / (columns * parts)),
        in_specs=[SMEM, VMEM, VMEM],
        out_specs=(ANY, VMEM, VMEM),
        out_shape=(
            pltpu.HBM((count, rank, columns), jnp.float32),
            pltpu.VMEM(shape, jnp.float32),
            pltpu.VMEM(shape, jnp.float32),
        ),
        scratch_shapes=[
            pltpu.VMEM((rank * pairs, 2 * rank), jnp.float32),
            pltpu.VMEM((count, rank, columns), jnp.float32),
            pltpu.SemaphoreType.DMA((count // PER_STEP,)),
        ],
        compiler_params=params(8),
        name="gram_pass",
    )(place, far, basis)


def exchange(value, axis, flip):
    return lax.ppermute(value, axis, [(i, i ^ flip) for i in range(lax.axis_size(axis))])


def swap(value, axis, first):
    pairs = [(i, i + 1) for i in range(first, lax.axis_size(axis) - 1, 2)]
    return lax.ppermute(value, axis, pairs + [(j, i) for i, j in pairs])


def shards(
    samples, omega, leaf_basis, near_blocks, near_index, near_count, inner_transfer, upper_transfer
):
    count = near_count.shape[0]
    slots = near_index.shape[1]
    rank = leaf_basis.shape[1]
    size = leaf_basis.shape[2]
    groups = lax.axis_size("leaf")
    parts = lax.axis_size("samp")
    device = lax.axis_index("leaf")
    place = lax.axis_index("samp").astype(jnp.int32)

    own = omega.T
    first = swap(own, "leaf", 1)
    second = swap(own, "leaf", 0)

    heights = groups.bit_length() - 1
    nodes = []
    offset, width = 0, groups
    for height in range(heights):
        node = jnp.right_shift(device, height)
        nodes.append(offset + node)
        if height == 1:
            sibling = offset + jnp.bitwise_xor(node, 1)
        offset, width = offset + width, width // 2
    rows = [lax.dynamic_slice_in_dim(upper_transfer, n, 1, axis=0) for n in nodes + [sibling]]
    upper = jnp.concatenate(rows, axis=0).reshape(heights + 1, rank, rank)

    blocks = near_blocks.reshape(count * slots, size, size)
    near, blocks, basis, weight, twice, crossing_tasks, tasks = own_pass(
        near_index.T,
        near_count.reshape(1, count),
        upper,
        inner_transfer.reshape(-1, rank),
        own,
        samples.T,
        blocks,
        leaf_basis,
    )
    near = side_pass(tasks, second, near, blocks)
    far, part, _ = far_pass(crossing_tasks, first, near, blocks, weight)

    def step(value, matrix):
        return jnp.dot(value, matrix, precision=lax.Precision.HIGHEST)

    third, other, fourth = (exchange(part, "leaf", flip) for flip in (2, 1, 3))
    coeffs, keep, send = gram_pass(place.reshape(1), far, basis, parts)
    got = exchange(send, "samp", 1)
    levels = [part + other]
    levels.append(step(levels[0], twice[0]) + step(third + fourth, twice[heights - 1]))
    flips = (4, 8, 24)
    for height, flip in enumerate(flips, 2):
        accum = step(levels[-1], twice[height - 1])
        other = exchange(accum, "leaf", flip)
        if height == 2:
            leaving = keep[1] + got[1]
            other, _ = lax.optimization_barrier((other, leaving))
            received = [exchange(leaving, "samp", 2)]
        elif height == 3:
            received += [exchange(keep[x] + got[x], "samp", 2 * x) for x in (2, 3)]
            other, _ = lax.optimization_barrier((other, received[0]))
        elif height == 4:
            leaf_gram = pl.pallas_call(
                finish_kernel,
                in_specs=[VMEM] * 5,
                out_specs=VMEM,
                out_shape=jax.ShapeDtypeStruct((count, rank * rank // parts), jnp.float32),
                compiler_params=params(8),
                name="finish",
            )(keep, *map(resident, [got] + received))
            other, _ = lax.optimization_barrier((other, leaf_gram))
        levels.append(accum + other)
    ancestors = pl.pallas_call(
        turn_kernel,
        in_specs=[VMEM] * heights,
        out_specs=VMEM,
        out_shape=jax.ShapeDtypeStruct((heights, rank, 2 * part.shape[0]), jnp.float32),
        compiler_params=params(8),
        name="turn",
    )(*map(resident, levels))
    return coeffs, leaf_gram, ancestors[None]


def solution(mesh):
    return jax.shard_map(
        shards,
        mesh=mesh,
        in_specs=(
            P("leaf", "samp"),
            P("leaf", "samp"),
            P("leaf", None, None),
            P("leaf", None, None, None),
            P("leaf", None),
            P("leaf"),
            P("leaf", None),
            P(),
        ),
        out_specs=(P("leaf", None, "samp"), P("leaf", "samp"), P("leaf", None, None, "samp")),
        check_vma=False,
    )
```

```python
import functools

import jax
import jax.numpy as jnp
from jax import lax
from jax.experimental import pallas as pl
from jax.experimental.pallas import tpu as pltpu
from jax.sharding import PartitionSpec as P

NT = (((1,), (1,)), ((), ()))
NN = (((1,), (0,)), ((), ()))
PER_STEP = 8
PER_TASKS = 2 * PER_STEP
LANES = 128
TASK_ROWS = 8
LIST_ROWS = 3
VMEM = pl.BlockSpec(memory_space=pltpu.VMEM)
SMEM = pl.BlockSpec(memory_space=pltpu.SMEM)
ANY = pl.BlockSpec(memory_space=pl.ANY)


def dot(a, b, dims):
    return lax.dot_general(a, b, dims, preferred_element_type=jnp.float32)


def split(value):
    high = value.astype(jnp.bfloat16)
    return high, (value - high.astype(jnp.float32)).astype(jnp.bfloat16)


def resident(value):
    return pltpu.with_memory_space_constraint(value, pltpu.VMEM)


def spread(source, first, ref, size):
    for leaf in range(ref.shape[1] // size):
        source[first + leaf] = ref[:, leaf * size : (leaf + 1) * size]


def subtract_near(count, task_ref, source, blocks_ref, acc_ref, slots):
    shift = count.bit_length()
    low = (1 << shift) - 1
    per_row = LANES // PER_TASKS

    def body(step, carry):
        done = []
        row = lax.div(step, per_row)
        at = lax.rem(step, per_row) * PER_TASKS
        for task in range(PER_STEP):
            one = task_ref[row, at + 2 * task]
            two = task_ref[row, at + 2 * task + 1]
            left, right = jnp.right_shift(one, shift), jnp.right_shift(two, shift)
            fetched = jnp.concatenate(
                [source[jnp.bitwise_and(one, low)], source[jnp.bitwise_and(two, low)]], axis=1
            )
            matrix = jnp.concatenate([blocks_ref[left], blocks_ref[right]], axis=1)
            done.append((lax.div(left, slots), dot(fetched, matrix, NT)))
        for leaf, near in done:
            acc_ref[leaf] = acc_ref[leaf] - near
        return carry

    lax.fori_loop(0, task_ref[LIST_ROWS - 1, LANES - 1], body, 0)


def list_tasks(index, number, device, lists_ref):
    slots, count = index.shape
    shift = count.bit_length()
    slot = lax.broadcasted_iota(jnp.int32, (slots, count), 0)
    leaf = lax.broadcasted_iota(jnp.int32, (slots, count), 1)
    at = index - (device * count - count)
    alive = slot < number
    before, after = at < count, at >= 2 * count
    even = jnp.broadcast_to(jnp.bitwise_and(device, 1), at.shape) == 0
    side = jnp.where(before == even, 1, 2)
    kind = jnp.where(jnp.logical_or(before, after), side, 0)
    code = jnp.left_shift(leaf * slots + slot, shift) + jnp.bitwise_and(at, count - 1)
    blank = count
    earlier_slot = (
        lax.broadcasted_iota(jnp.int32, (slots, slots), 1)
        < lax.broadcasted_iota(jnp.int32, (slots, slots), 0)
    ).astype(jnp.bfloat16)
    earlier_leaf = (
        lax.broadcasted_iota(jnp.int32, (count, count), 0)
        < lax.broadcasted_iota(jnp.int32, (count, count), 1)
    ).astype(jnp.bfloat16)
    place = jnp.full((slots, count), -1, jnp.int32)
    steps = []
    for which in range(3):
        chosen = jnp.logical_and(alive, kind == which)
        mark = jnp.where(chosen, 1.0, 0.0)
        rank = dot(earlier_slot, mark.astype(jnp.bfloat16), NN)
        number_here = jnp.sum(mark, axis=0, keepdims=True).astype(jnp.int32)
        padded = (number_here + jnp.bitwise_and(number_here, 1)).astype(jnp.float32)
        base = dot(jnp.broadcast_to(padded, (slots, count)).astype(jnp.bfloat16), earlier_leaf, NN)
        here = (base + rank).astype(jnp.int32) + which * LIST_ROWS * LANES
        place = jnp.where(chosen, here, place)
        total = jnp.sum(padded, axis=1, keepdims=True).astype(jnp.int32)
        steps.append(jnp.right_shift(total + PER_TASKS - 1, PER_TASKS.bit_length() - 1))
    place, value = place.T, code.T - blank
    lane = lax.broadcasted_iota(jnp.int32, (count, LANES), 1)
    for which in range(3):
        for row in range(LIST_ROWS):
            target = lane + (which * LIST_ROWS + row) * LANES
            total = jnp.zeros((count, LANES), jnp.int32)
            for k in range(slots):
                total += jnp.where(place[:, k : k + 1] == target, value[:, k : k + 1], 0)
            line = jnp.sum(total, axis=0, keepdims=True) + blank
            if row == LIST_ROWS - 1:
                line = jnp.where(lane[:1] == LANES - 1, steps[which], line)
            lists_ref[which, row : row + 1] = line


def path_products(upper_ref, mats_ref, basis_ref, weight_ref):
    count, rank, size = basis_ref.shape
    nodes = [split(upper_ref[0].astype(jnp.float32).T)]
    blank = jnp.zeros((rank, size), basis_ref.dtype)
    width = 2
    offset = 2 * count - 2
    while width <= count:
        offset = offset - width
        later = []
        for parent, (high, low) in enumerate(nodes):
            first = (offset + 2 * parent) * rank
            pair = mats_ref[first : first + 2 * rank, :]
            product = dot(high, pair, NT) + dot(low, pair, NT)
            pair_high, pair_low = split(product)
            if width == count:
                bases = jnp.concatenate(
                    [
                        jnp.concatenate([basis_ref[2 * parent], blank], axis=1),
                        jnp.concatenate([blank, basis_ref[2 * parent + 1]], axis=1),
                    ],
                    axis=0,
                )
                weight = split(dot(pair_high, bases, NN) + dot(pair_low, bases, NN))
                at = slice(2 * parent * size, 2 * (parent + 1) * size)
                weight_ref[:rank, at], weight_ref[rank:, at] = weight
            else:
                later.append((pair_high[:, :rank], pair_low[:, :rank]))
                later.append((pair_high[:, rank:], pair_low[:, rank:]))
        nodes = later
        width = 2 * width


def own_kernel(
    index_any,
    number_any,
    upper_ref,
    mats_ref,
    own_any,
    samples_any,
    blocks_any,
    basis_any,
    acc_ref,
    blocks_ref,
    basis_ref,
    weight_ref,
    twice_ref,
    first_task_ref,
    second_task_ref,
    own_task,
    lists,
    index_ref,
    number_ref,
    own_ref,
    samples_ref,
    source,
    sems,
):
    pairs = (
        (index_any, index_ref),
        (number_any, number_ref),
        (basis_any, basis_ref),
        (own_any, own_ref),
        (samples_any, samples_ref),
        (blocks_any, blocks_ref),
        (lists.at[0], own_task),
        (lists.at[1], first_task_ref),
        (lists.at[2], second_task_ref),
    )
    copies = [
        pltpu.make_async_copy(origin, target, sems.at[place])
        for place, (origin, target) in enumerate(pairs)
    ]
    for copy in copies[:6]:
        copy.start()
    slots, count = index_ref.shape
    size = blocks_ref.shape[1]
    rank = upper_ref.shape[1]
    copies[0].wait()
    copies[1].wait()
    list_tasks(index_ref[...], number_ref[...], lax.axis_index("leaf"), lists)
    for copy in copies[6:]:
        copy.start()
    copies[2].wait()
    path_products(upper_ref, mats_ref, basis_ref, weight_ref)
    for height in range(1, upper_ref.shape[0]):
        matrix = upper_ref[height].astype(jnp.float32)
        blank = jnp.zeros_like(matrix)
        twice_ref[height - 1, :rank] = jnp.concatenate([matrix, blank], axis=1)
        twice_ref[height - 1, rank:] = jnp.concatenate([blank, matrix], axis=1)
    copies[3].wait()
    spread(source, 0, own_ref, size)
    source[count] = jnp.zeros_like(source[count])
    copies[4].wait()
    for leaf in range(count):
        acc_ref[leaf] = samples_ref[:, leaf * size : (leaf + 1) * size].astype(jnp.float32)
    for copy in copies[5:]:
        copy.wait()
    subtract_near(count, own_task, source, blocks_ref, acc_ref, slots)


def side_kernel(task_ref, side_ref, near_ref, blocks_ref, slots, acc, source):
    del near_ref
    count, _, size = acc.shape
    spread(source, 0, side_ref, size)
    source[count] = jnp.zeros_like(source[count])
    subtract_near(count, task_ref, source, blocks_ref, acc, slots)


def far_kernel(
    task_ref, side_ref, near_ref, blocks_ref, weight_ref, far_ref, part_ref, acc, source
):
    count, _, size = acc.shape
    slots = blocks_ref.shape[0] // count
    side_kernel(task_ref, side_ref, near_ref, blocks_ref, slots, acc, source)
    for leaf in range(count):
        far_ref[:, leaf * size : (leaf + 1) * size] = acc[leaf].astype(jnp.bfloat16)
    product = dot(weight_ref[...], far_ref[...], NT)
    rank = product.shape[0] // 2
    turned = (product[:rank] + product[rank:]).T
    half = turned.shape[0] // 2
    part_ref[...] = jnp.concatenate([turned[:half], turned[half:]], axis=1)


def gram_kernel(
    scale, place_ref, far_ref, basis_ref, coeff_any, keep_ref, send_ref, gram, coeff_ref, sems
):
    parts, rows, pairs, width = keep_ref.shape
    parts = 2 * parts
    rank = width // 2
    size = basis_ref.shape[2]
    lane = lax.broadcasted_iota(jnp.int32, (rank, width), 1)
    copies = []
    for first in range(0, pairs, PER_STEP):
        stacks = []
        for pair in range(first, first + PER_STEP):
            both = []
            for leaf in (pair, pair + pairs):
                far = far_ref[:, leaf * size : (leaf + 1) * size]
                coeff = dot(basis_ref[leaf], far, NT)
                coeff_ref[leaf] = coeff
                both.append(coeff.astype(jnp.bfloat16))
            stacks.append(jnp.concatenate(both, axis=0))
        for start in (first, first + pairs):
            these = pl.ds(start, PER_STEP)
            copies.append(
                pltpu.make_async_copy(
                    coeff_ref.at[these], coeff_any.at[these], sems.at[len(copies)]
                )
            )
            copies[-1].start()
        for pair, stacked in enumerate(stacks, first):
            product = dot(stacked, stacked, NT)
            value = jnp.where(lane < rank, product[:rank], product[rank:]) * scale
            gram[pl.ds(pair, rank, stride=pairs), :] = value
    for relative in range(parts):
        first = jnp.bitwise_xor(place_ref[0], relative) * rows
        target = send_ref if relative % 2 else keep_ref
        for row in range(rows):
            at = pl.multiple_of((first + row) * pairs, pairs)
            target[relative // 2, row] = gram[pl.ds(at, pairs), :]
    for copy in copies:
        copy.wait()


def finish_kernel(keep_ref, got_ref, received_ref, last_ref, out_ref):
    _, rows, pairs, width = keep_ref.shape
    half = width // 2
    lane = lax.broadcasted_iota(jnp.int32, (pairs, width), 1)
    for row in range(0, rows, 2):
        even, odd = (
            keep_ref[0, at]
            + got_ref[0, at]
            + received_ref[0, at].astype(jnp.float32)
            + last_ref[at]
            for at in (row, row + 1)
        )
        at = slice(row * half, (row + 2) * half)
        out_ref[:pairs, at] = jnp.where(lane < half, even, pltpu.roll(odd, half, 1))
        out_ref[pairs:, at] = jnp.where(lane < half, pltpu.roll(even, half, 1), odd)


def turn_kernel(*refs):
    levels, out_ref = refs[:-1], refs[-1]
    for height, level in enumerate(levels):
        turned = level[...].T
        half = turned.shape[0] // 2
        out_ref[height] = jnp.concatenate([turned[:half], turned[half:]], axis=1)


def params(mib):
    return pltpu.CompilerParams(vmem_limit_bytes=mib * 2**20)


def own_pass(index, number, upper, mats, own, samples, blocks, basis):
    slots, count = index.shape
    size = blocks.shape[1]
    columns = own.shape[0]
    heights, rank, _ = upper.shape
    tasks = pltpu.SMEM((TASK_ROWS, LANES), jnp.int32)
    far = lambda value: pltpu.with_memory_space_constraint(value, pltpu.HBM)
    return pl.pallas_call(
        own_kernel,
        in_specs=[ANY, ANY, VMEM, VMEM, ANY, ANY, ANY, ANY],
        out_specs=(VMEM, VMEM, VMEM, VMEM, VMEM, SMEM, SMEM),
        out_shape=(
            pltpu.VMEM((count, columns, size), jnp.float32),
            pltpu.VMEM(blocks.shape, blocks.dtype),
            pltpu.VMEM(basis.shape, basis.dtype),
            pltpu.VMEM((2 * rank, count * size), jnp.bfloat16),
            pltpu.VMEM((heights - 1, 2 * rank, 2 * rank), jnp.float32),
            tasks,
            tasks,
        ),
        scratch_shapes=[
            tasks,
            pltpu.VMEM((3, TASK_ROWS, LANES), jnp.int32),
            pltpu.VMEM((slots, count), jnp.int32),
            pltpu.VMEM((1, count), jnp.int32),
            pltpu.VMEM(own.shape, own.dtype),
            pltpu.VMEM(samples.shape, samples.dtype),
            pltpu.VMEM((count + 1, columns, size), jnp.bfloat16),
            pltpu.SemaphoreType.DMA((9,)),
        ],
        compiler_params=params(8),
        name="own_pass",
    )(
        far(index),
        far(number),
        resident(upper),
        resident(mats),
        far(own),
        far(samples),
        far(blocks),
        far(basis),
    )


def side_pass(tasks, side, near, blocks):
    count, columns, size = near.shape
    slots = blocks.shape[0] // count

    def kernel(task_ref, side_ref, near_ref, blocks_ref, acc, source):
        side_kernel(task_ref, side_ref, near_ref, blocks_ref, slots, acc, source)

    return pl.pallas_call(
        kernel,
        in_specs=[SMEM] + [VMEM] * 3,
        out_specs=VMEM,
        out_shape=pltpu.VMEM((count, columns, size), jnp.float32),
        input_output_aliases={2: 0},
        scratch_shapes=[pltpu.VMEM((count + 1, columns, size), jnp.bfloat16)],
        compiler_params=params(8),
        name="side_pass",
    )(tasks, resident(side), near, blocks)


def far_pass(tasks, side, near, blocks, weight):
    count, columns, size = near.shape
    rank = weight.shape[0] // 2
    return pl.pallas_call(
        far_kernel,
        in_specs=[SMEM] + [VMEM] * 4,
        out_specs=(VMEM, VMEM, VMEM),
        out_shape=(
            pltpu.VMEM((columns, count * size), jnp.bfloat16),
            pltpu.VMEM((columns // 2, 2 * rank), jnp.float32),
            pltpu.VMEM((count, columns, size), jnp.float32),
        ),
        input_output_aliases={2: 2},
        scratch_shapes=[pltpu.VMEM((count + 1, columns, size), jnp.bfloat16)],
        compiler_params=params(8),
        name="far_pass",
    )(tasks, resident(side), near, blocks, weight)


def gram_pass(place, far, basis, parts):
    count, rank, _ = basis.shape
    columns = far.shape[0]
    pairs = count // 2
    shape = (parts // 2, rank // parts, pairs, 2 * rank)
    return pl.pallas_call(
        functools.partial(gram_kernel, 1.0 / (columns * parts)),
        in_specs=[SMEM, VMEM, VMEM],
        out_specs=(ANY, VMEM, VMEM),
        out_shape=(
            pltpu.HBM((count, rank, columns), jnp.float32),
            pltpu.VMEM(shape, jnp.float32),
            pltpu.VMEM(shape, jnp.float32),
        ),
        scratch_shapes=[
            pltpu.VMEM((rank * pairs, 2 * rank), jnp.float32),
            pltpu.VMEM((count, rank, columns), jnp.float32),
            pltpu.SemaphoreType.DMA((count // PER_STEP,)),
        ],
        compiler_params=params(8),
        name="gram_pass",
    )(place, far, basis)


def exchange(value, axis, flip):
    return lax.ppermute(value, axis, [(i, i ^ flip) for i in range(lax.axis_size(axis))])


def swap(value, axis, first):
    pairs = [(i, i + 1) for i in range(first, lax.axis_size(axis) - 1, 2)]
    return lax.ppermute(value, axis, pairs + [(j, i) for i, j in pairs])


def shards(
    samples, omega, leaf_basis, near_blocks, near_index, near_count, inner_transfer, upper_transfer
):
    count = near_count.shape[0]
    slots = near_index.shape[1]
    rank = leaf_basis.shape[1]
    size = leaf_basis.shape[2]
    groups = lax.axis_size("leaf")
    parts = lax.axis_size("samp")
    device = lax.axis_index("leaf")
    place = lax.axis_index("samp").astype(jnp.int32)

    own = omega.T
    first = swap(own, "leaf", 1)
    second = swap(own, "leaf", 0)

    heights = groups.bit_length() - 1
    rows = []
    offset, width = 0, groups
    for height in range(heights):
        rows.append(
            lax.dynamic_slice_in_dim(
                upper_transfer, offset + jnp.right_shift(device, height), 1, axis=0
            )
        )
        offset, width = offset + width, width // 2
    upper = jnp.concatenate(rows, axis=0).reshape(heights, rank, rank)

    blocks = near_blocks.reshape(count * slots, size, size)
    near, blocks, basis, weight, twice, crossing_tasks, tasks = own_pass(
        near_index.T,
        near_count.reshape(1, count),
        upper,
        inner_transfer.reshape(-1, rank),
        own,
        samples.T,
        blocks,
        leaf_basis,
    )
    near = side_pass(tasks, second, near, blocks)
    far, part, _ = far_pass(crossing_tasks, first, near, blocks, weight)

    flips = (1, 3, 4, 8, 24)
    levels = []
    accum = part
    for height in range(heights):
        if height:
            accum = jnp.dot(accum, twice[height - 1], precision=lax.Precision.HIGHEST)
        other = exchange(accum, "leaf", flips[height])
        if height == 0:
            coeffs, keep, send = gram_pass(place.reshape(1), far, basis, parts)
            got = exchange(send, "samp", 1)
        elif height == 2:
            leaving = (keep[1:3] + got[1:3]).astype(jnp.bfloat16)
            other, _ = lax.optimization_barrier((other, leaving))
            received = exchange(leaving, "samp", 2)
        elif height == 3:
            leaving = keep[3] + got[3] + received[1].astype(jnp.float32)
            other, _ = lax.optimization_barrier((other, leaving))
            last = exchange(leaving, "samp", 6)
        elif height == 4:
            leaf_gram = pl.pallas_call(
                finish_kernel,
                in_specs=[VMEM] * 4,
                out_specs=VMEM,
                out_shape=jax.ShapeDtypeStruct((count, rank * rank // parts), jnp.float32),
                compiler_params=params(8),
                name="finish",
            )(keep, *map(resident, [got, received, last]))
            other, _ = lax.optimization_barrier((other, leaf_gram))
        accum = accum + other
        levels.append(accum)
    ancestors = pl.pallas_call(
        turn_kernel,
        in_specs=[VMEM] * heights,
        out_specs=VMEM,
        out_shape=jax.ShapeDtypeStruct((heights, rank, 2 * part.shape[0]), jnp.float32),
        compiler_params=params(8),
        name="turn",
    )(*map(resident, levels))
    return coeffs, leaf_gram, ancestors[None]


def solution(mesh):
    return jax.shard_map(
        shards,
        mesh=mesh,
        in_specs=(
            P("leaf", "samp"),
            P("leaf", "samp"),
            P("leaf", None, None),
            P("leaf", None, None, None),
            P("leaf", None),
            P("leaf"),
            P("leaf", None),
            P(),
        ),
        out_specs=(P("leaf", None, "samp"), P("leaf", "samp"), P("leaf", None, None, "samp")),
        check_vma=False,
    )
```

```python
import functools

import jax
import jax.numpy as jnp
from jax import lax
from jax.experimental import pallas as pl
from jax.experimental.pallas import tpu as pltpu
from jax.sharding import PartitionSpec as P

NT = (((1,), (1,)), ((), ()))
NN = (((1,), (0,)), ((), ()))
PER_STEP = 8
PER_TASKS = 2 * PER_STEP
LANES = 128
TASK_ROWS = 8
LIST_ROWS = 3
VMEM = pl.BlockSpec(memory_space=pltpu.VMEM)
SMEM = pl.BlockSpec(memory_space=pltpu.SMEM)
ANY = pl.BlockSpec(memory_space=pl.ANY)


def dot(a, b, dims):
    return lax.dot_general(a, b, dims, preferred_element_type=jnp.float32)


def split(value):
    high = value.astype(jnp.bfloat16)
    return high, (value - high.astype(jnp.float32)).astype(jnp.bfloat16)


def resident(value):
    return pltpu.with_memory_space_constraint(value, pltpu.VMEM)


def spread(source, first, ref, size):
    for leaf in range(ref.shape[1] // size):
        source[first + leaf] = ref[:, leaf * size : (leaf + 1) * size]


def subtract_near(count, task_ref, source, blocks_ref, acc_ref, slots):
    shift = count.bit_length()
    low = (1 << shift) - 1
    per_row = LANES // PER_TASKS

    def body(step, carry):
        done = []
        row = lax.div(step, per_row)
        at = lax.rem(step, per_row) * PER_TASKS
        for task in range(PER_STEP):
            one = task_ref[row, at + 2 * task]
            two = task_ref[row, at + 2 * task + 1]
            left, right = jnp.right_shift(one, shift), jnp.right_shift(two, shift)
            fetched = jnp.concatenate(
                [source[jnp.bitwise_and(one, low)], source[jnp.bitwise_and(two, low)]], axis=1
            )
            matrix = jnp.concatenate([blocks_ref[left], blocks_ref[right]], axis=1)
            done.append((lax.div(left, slots), dot(fetched, matrix, NT)))
        for leaf, near in done:
            acc_ref[leaf] = acc_ref[leaf] - near
        return carry

    lax.fori_loop(0, task_ref[LIST_ROWS - 1, LANES - 1], body, 0)


def list_tasks(index, number, device, lists_ref):
    slots, count = index.shape
    shift = count.bit_length()
    slot = lax.broadcasted_iota(jnp.int32, (slots, count), 0)
    leaf = lax.broadcasted_iota(jnp.int32, (slots, count), 1)
    at = index - (device * count - count)
    alive = slot < number
    before, after = at < count, at >= 2 * count
    even = jnp.broadcast_to(jnp.bitwise_and(device, 1), at.shape) == 0
    side = jnp.where(before == even, 1, 2)
    kind = jnp.where(jnp.logical_or(before, after), side, 0)
    code = jnp.left_shift(leaf * slots + slot, shift) + jnp.bitwise_and(at, count - 1)
    blank = count
    earlier_slot = (
        lax.broadcasted_iota(jnp.int32, (slots, slots), 1)
        < lax.broadcasted_iota(jnp.int32, (slots, slots), 0)
    ).astype(jnp.bfloat16)
    earlier_leaf = (
        lax.broadcasted_iota(jnp.int32, (count, count), 0)
        < lax.broadcasted_iota(jnp.int32, (count, count), 1)
    ).astype(jnp.bfloat16)
    place = jnp.full((slots, count), -1, jnp.int32)
    steps = []
    for which in range(3):
        chosen = jnp.logical_and(alive, kind == which)
        mark = jnp.where(chosen, 1.0, 0.0)
        rank = dot(earlier_slot, mark.astype(jnp.bfloat16), NN)
        number_here = jnp.sum(mark, axis=0, keepdims=True).astype(jnp.int32)
        padded = (number_here + jnp.bitwise_and(number_here, 1)).astype(jnp.float32)
        base = dot(jnp.broadcast_to(padded, (slots, count)).astype(jnp.bfloat16), earlier_leaf, NN)
        here = (base + rank).astype(jnp.int32) + which * LIST_ROWS * LANES
        place = jnp.where(chosen, here, place)
        total = jnp.sum(padded, axis=1, keepdims=True).astype(jnp.int32)
        steps.append(jnp.right_shift(total + PER_TASKS - 1, PER_TASKS.bit_length() - 1))
    place, value = place.T, code.T - blank
    lane = lax.broadcasted_iota(jnp.int32, (count, LANES), 1)
    for which in range(3):
        for row in range(LIST_ROWS):
            target = lane + (which * LIST_ROWS + row) * LANES
            total = jnp.zeros((count, LANES), jnp.int32)
            for k in range(slots):
                total += jnp.where(place[:, k : k + 1] == target, value[:, k : k + 1], 0)
            line = jnp.sum(total, axis=0, keepdims=True) + blank
            if row == LIST_ROWS - 1:
                line = jnp.where(lane[:1] == LANES - 1, steps[which], line)
            lists_ref[which, row : row + 1] = line


def path_products(upper_ref, mats_ref, basis_ref, weight_ref):
    count, rank, size = basis_ref.shape
    nodes = [split(upper_ref[0].astype(jnp.float32).T)]
    blank = jnp.zeros((rank, size), basis_ref.dtype)
    width = 2
    offset = 2 * count - 2
    while width <= count:
        offset = offset - width
        later = []
        for parent, (high, low) in enumerate(nodes):
            first = (offset + 2 * parent) * rank
            pair = mats_ref[first : first + 2 * rank, :]
            product = dot(high, pair, NT) + dot(low, pair, NT)
            pair_high, pair_low = split(product)
            if width == count:
                bases = jnp.concatenate(
                    [
                        jnp.concatenate([basis_ref[2 * parent], blank], axis=1),
                        jnp.concatenate([blank, basis_ref[2 * parent + 1]], axis=1),
                    ],
                    axis=0,
                )
                weight = split(dot(pair_high, bases, NN) + dot(pair_low, bases, NN))
                at = slice(2 * parent * size, 2 * (parent + 1) * size)
                weight_ref[:rank, at], weight_ref[rank:, at] = weight
            else:
                later.append((pair_high[:, :rank], pair_low[:, :rank]))
                later.append((pair_high[:, rank:], pair_low[:, rank:]))
        nodes = later
        width = 2 * width


def own_kernel(
    index_any,
    number_any,
    upper_ref,
    mats_ref,
    own_any,
    samples_any,
    blocks_any,
    basis_any,
    acc_ref,
    blocks_ref,
    basis_ref,
    weight_ref,
    twice_ref,
    first_task_ref,
    second_task_ref,
    own_task,
    lists,
    index_ref,
    number_ref,
    own_ref,
    samples_ref,
    source,
    sems,
):
    pairs = (
        (index_any, index_ref),
        (number_any, number_ref),
        (basis_any, basis_ref),
        (own_any, own_ref),
        (samples_any, samples_ref),
        (blocks_any, blocks_ref),
        (lists.at[0], own_task),
        (lists.at[1], first_task_ref),
        (lists.at[2], second_task_ref),
    )
    copies = [
        pltpu.make_async_copy(origin, target, sems.at[place])
        for place, (origin, target) in enumerate(pairs)
    ]
    for copy in copies[:6]:
        copy.start()
    slots, count = index_ref.shape
    size = blocks_ref.shape[1]
    rank = upper_ref.shape[1]
    copies[0].wait()
    copies[1].wait()
    list_tasks(index_ref[...], number_ref[...], lax.axis_index("leaf"), lists)
    for copy in copies[6:]:
        copy.start()
    copies[2].wait()
    path_products(upper_ref, mats_ref, basis_ref, weight_ref)
    for height in range(1, upper_ref.shape[0]):
        matrix = upper_ref[height].astype(jnp.float32)
        blank = jnp.zeros_like(matrix)
        twice_ref[height - 1, :rank] = jnp.concatenate([matrix, blank], axis=1)
        twice_ref[height - 1, rank:] = jnp.concatenate([blank, matrix], axis=1)
    copies[3].wait()
    spread(source, 0, own_ref, size)
    source[count] = jnp.zeros_like(source[count])
    copies[4].wait()
    for leaf in range(count):
        acc_ref[leaf] = samples_ref[:, leaf * size : (leaf + 1) * size].astype(jnp.float32)
    for copy in copies[5:]:
        copy.wait()
    subtract_near(count, own_task, source, blocks_ref, acc_ref, slots)


def side_kernel(task_ref, side_ref, near_ref, blocks_ref, slots, acc, source):
    del near_ref
    count, _, size = acc.shape
    spread(source, 0, side_ref, size)
    source[count] = jnp.zeros_like(source[count])
    subtract_near(count, task_ref, source, blocks_ref, acc, slots)


def far_kernel(
    task_ref, side_ref, near_ref, blocks_ref, weight_ref, far_ref, part_ref, acc, source
):
    count, _, size = acc.shape
    slots = blocks_ref.shape[0] // count
    side_kernel(task_ref, side_ref, near_ref, blocks_ref, slots, acc, source)
    for leaf in range(count):
        far_ref[:, leaf * size : (leaf + 1) * size] = acc[leaf].astype(jnp.bfloat16)
    product = dot(weight_ref[...], far_ref[...], NT)
    rank = product.shape[0] // 2
    turned = (product[:rank] + product[rank:]).T
    half = turned.shape[0] // 2
    part_ref[...] = jnp.concatenate([turned[:half], turned[half:]], axis=1)


def gram_kernel(
    scale, place_ref, far_ref, basis_ref, coeff_any, keep_ref, send_ref, gram, coeff_ref, sems
):
    parts, rows, pairs, width = keep_ref.shape
    parts = 2 * parts
    rank = width // 2
    size = basis_ref.shape[2]
    lane = lax.broadcasted_iota(jnp.int32, (rank, width), 1)
    copies = []
    for first in range(0, pairs, PER_STEP):
        stacks = []
        for pair in range(first, first + PER_STEP):
            both = []
            for leaf in (pair, pair + pairs):
                far = far_ref[:, leaf * size : (leaf + 1) * size]
                coeff = dot(basis_ref[leaf], far, NT)
                coeff_ref[leaf] = coeff
                both.append(coeff.astype(jnp.bfloat16))
            stacks.append(jnp.concatenate(both, axis=0))
        for start in (first, first + pairs):
            these = pl.ds(start, PER_STEP)
            copies.append(
                pltpu.make_async_copy(
                    coeff_ref.at[these], coeff_any.at[these], sems.at[len(copies)]
                )
            )
            copies[-1].start()
        for pair, stacked in enumerate(stacks, first):
            product = dot(stacked, stacked, NT)
            value = jnp.where(lane < rank, product[:rank], product[rank:]) * scale
            gram[pl.ds(pair, rank, stride=pairs), :] = value
    for relative in range(parts):
        first = jnp.bitwise_xor(place_ref[0], relative) * rows
        target = send_ref if relative % 2 else keep_ref
        for row in range(rows):
            at = pl.multiple_of((first + row) * pairs, pairs)
            target[relative // 2, row] = gram[pl.ds(at, pairs), :].astype(target.dtype)
    for copy in copies:
        copy.wait()


def finish_kernel(keep_ref, got_ref, received_ref, last_ref, out_ref):
    _, rows, pairs, width = keep_ref.shape
    half = width // 2
    lane = lax.broadcasted_iota(jnp.int32, (pairs, width), 1)
    for row in range(0, rows, 2):
        even, odd = (
            keep_ref[0, at]
            + got_ref[0, at].astype(jnp.float32)
            + received_ref[0, at].astype(jnp.float32)
            + last_ref[at]
            for at in (row, row + 1)
        )
        at = slice(row * half, (row + 2) * half)
        out_ref[:pairs, at] = jnp.where(lane < half, even, pltpu.roll(odd, half, 1))
        out_ref[pairs:, at] = jnp.where(lane < half, pltpu.roll(even, half, 1), odd)


def turn_kernel(*refs):
    levels, out_ref = refs[:-1], refs[-1]
    for height, level in enumerate(levels):
        turned = level[...].T
        half = turned.shape[0] // 2
        out_ref[height] = jnp.concatenate([turned[:half], turned[half:]], axis=1)


def params(mib):
    return pltpu.CompilerParams(vmem_limit_bytes=mib * 2**20)


def own_pass(index, number, upper, mats, own, samples, blocks, basis):
    slots, count = index.shape
    size = blocks.shape[1]
    columns = own.shape[0]
    heights, rank, _ = upper.shape
    tasks = pltpu.SMEM((TASK_ROWS, LANES), jnp.int32)
    far = lambda value: pltpu.with_memory_space_constraint(value, pltpu.HBM)
    return pl.pallas_call(
        own_kernel,
        in_specs=[ANY, ANY, VMEM, VMEM, ANY, ANY, ANY, ANY],
        out_specs=(VMEM, VMEM, VMEM, VMEM, VMEM, SMEM, SMEM),
        out_shape=(
            pltpu.VMEM((count, columns, size), jnp.float32),
            pltpu.VMEM(blocks.shape, blocks.dtype),
            pltpu.VMEM(basis.shape, basis.dtype),
            pltpu.VMEM((2 * rank, count * size), jnp.bfloat16),
            pltpu.VMEM((heights - 1, 2 * rank, 2 * rank), jnp.float32),
            tasks,
            tasks,
        ),
        scratch_shapes=[
            tasks,
            pltpu.VMEM((3, TASK_ROWS, LANES), jnp.int32),
            pltpu.VMEM((slots, count), jnp.int32),
            pltpu.VMEM((1, count), jnp.int32),
            pltpu.VMEM(own.shape, own.dtype),
            pltpu.VMEM(samples.shape, samples.dtype),
            pltpu.VMEM((count + 1, columns, size), jnp.bfloat16),
            pltpu.SemaphoreType.DMA((9,)),
        ],
        compiler_params=params(8),
        name="own_pass",
    )(
        far(index),
        far(number),
        resident(upper),
        resident(mats),
        far(own),
        far(samples),
        far(blocks),
        far(basis),
    )


def side_pass(tasks, side, near, blocks):
    count, columns, size = near.shape
    slots = blocks.shape[0] // count

    def kernel(task_ref, side_ref, near_ref, blocks_ref, acc, source):
        side_kernel(task_ref, side_ref, near_ref, blocks_ref, slots, acc, source)

    return pl.pallas_call(
        kernel,
        in_specs=[SMEM] + [VMEM] * 3,
        out_specs=VMEM,
        out_shape=pltpu.VMEM((count, columns, size), jnp.float32),
        input_output_aliases={2: 0},
        scratch_shapes=[pltpu.VMEM((count + 1, columns, size), jnp.bfloat16)],
        compiler_params=params(8),
        name="side_pass",
    )(tasks, resident(side), near, blocks)


def far_pass(tasks, side, near, blocks, weight):
    count, columns, size = near.shape
    rank = weight.shape[0] // 2
    return pl.pallas_call(
        far_kernel,
        in_specs=[SMEM] + [VMEM] * 4,
        out_specs=(VMEM, VMEM, VMEM),
        out_shape=(
            pltpu.VMEM((columns, count * size), jnp.bfloat16),
            pltpu.VMEM((columns // 2, 2 * rank), jnp.float32),
            pltpu.VMEM((count, columns, size), jnp.float32),
        ),
        input_output_aliases={2: 2},
        scratch_shapes=[pltpu.VMEM((count + 1, columns, size), jnp.bfloat16)],
        compiler_params=params(8),
        name="far_pass",
    )(tasks, resident(side), near, blocks, weight)


def gram_pass(place, far, basis, parts):
    count, rank, _ = basis.shape
    columns = far.shape[0]
    pairs = count // 2
    shape = (parts // 2, rank // parts, pairs, 2 * rank)
    return pl.pallas_call(
        functools.partial(gram_kernel, 1.0 / (columns * parts)),
        in_specs=[SMEM, VMEM, VMEM],
        out_specs=(ANY, VMEM, VMEM),
        out_shape=(
            pltpu.HBM((count, rank, columns), jnp.float32),
            pltpu.VMEM(shape, jnp.float32),
            pltpu.VMEM(shape, jnp.bfloat16),
        ),
        scratch_shapes=[
            pltpu.VMEM((rank * pairs, 2 * rank), jnp.float32),
            pltpu.VMEM((count, rank, columns), jnp.float32),
            pltpu.SemaphoreType.DMA((count // PER_STEP,)),
        ],
        compiler_params=params(8),
        name="gram_pass",
    )(place, far, basis)


def exchange(value, axis, flip):
    return lax.ppermute(value, axis, [(i, i ^ flip) for i in range(lax.axis_size(axis))])


def swap(value, axis, first):
    pairs = [(i, i + 1) for i in range(first, lax.axis_size(axis) - 1, 2)]
    return lax.ppermute(value, axis, pairs + [(j, i) for i, j in pairs])


def shards(
    samples, omega, leaf_basis, near_blocks, near_index, near_count, inner_transfer, upper_transfer
):
    count = near_count.shape[0]
    slots = near_index.shape[1]
    rank = leaf_basis.shape[1]
    size = leaf_basis.shape[2]
    groups = lax.axis_size("leaf")
    parts = lax.axis_size("samp")
    device = lax.axis_index("leaf")
    place = lax.axis_index("samp").astype(jnp.int32)

    own = omega.T
    first = swap(own, "leaf", 1)
    second = swap(own, "leaf", 0)

    heights = groups.bit_length() - 1
    rows = []
    offset, width = 0, groups
    for height in range(heights):
        rows.append(
            lax.dynamic_slice_in_dim(
                upper_transfer, offset + jnp.right_shift(device, height), 1, axis=0
            )
        )
        offset, width = offset + width, width // 2
    upper = jnp.concatenate(rows, axis=0).reshape(heights, rank, rank)

    blocks = near_blocks.reshape(count * slots, size, size)
    near, blocks, basis, weight, twice, crossing_tasks, tasks = own_pass(
        near_index.T,
        near_count.reshape(1, count),
        upper,
        inner_transfer.reshape(-1, rank),
        own,
        samples.T,
        blocks,
        leaf_basis,
    )
    near = side_pass(tasks, second, near, blocks)
    far, part, _ = far_pass(crossing_tasks, first, near, blocks, weight)

    flips = (1, 3, 4, 8, 24)
    levels = []
    accum = part
    for height in range(heights):
        if height:
            accum = jnp.dot(accum, twice[height - 1], precision=lax.Precision.HIGHEST)
        other = exchange(accum, "leaf", flips[height])
        if height == 0:
            coeffs, keep, send = gram_pass(place.reshape(1), far, basis, parts)
            got = exchange(send, "samp", 1)
        elif height == 2:
            leaving = (keep[1:3] + got[1:3].astype(jnp.float32)).astype(jnp.bfloat16)
            other, _ = lax.optimization_barrier((other, leaving))
            received = exchange(leaving, "samp", 2)
        elif height == 3:
            leaving = keep[3] + got[3].astype(jnp.float32) + received[1].astype(jnp.float32)
            other, _ = lax.optimization_barrier((other, leaving))
            last = exchange(leaving, "samp", 6)
        elif height == 4:
            leaf_gram = pl.pallas_call(
                finish_kernel,
                in_specs=[VMEM] * 4,
                out_specs=VMEM,
                out_shape=jax.ShapeDtypeStruct((count, rank * rank // parts), jnp.float32),
                compiler_params=params(8),
                name="finish",
            )(keep, *map(resident, [got, received, last]))
            other, _ = lax.optimization_barrier((other, leaf_gram))
        accum = accum + other
        levels.append(accum)
    ancestors = pl.pallas_call(
        turn_kernel,
        in_specs=[VMEM] * heights,
        out_specs=VMEM,
        out_shape=jax.ShapeDtypeStruct((heights, rank, 2 * part.shape[0]), jnp.float32),
        compiler_params=params(8),
        name="turn",
    )(*map(resident, levels))
    return coeffs, leaf_gram, ancestors[None]


def solution(mesh):
    return jax.shard_map(
        shards,
        mesh=mesh,
        in_specs=(
            P("leaf", "samp"),
            P("leaf", "samp"),
            P("leaf", None, None),
            P("leaf", None, None, None),
            P("leaf", None),
            P("leaf"),
            P("leaf", None),
            P(),
        ),
        out_specs=(P("leaf", None, "samp"), P("leaf", "samp"), P("leaf", None, None, "samp")),
        check_vma=False,
    )
```

```python
import functools

import jax
import jax.numpy as jnp
from jax import lax
from jax.experimental import pallas as pl
from jax.experimental.pallas import tpu as pltpu
from jax.sharding import PartitionSpec as P

NT = (((1,), (1,)), ((), ()))
NN = (((1,), (0,)), ((), ()))
PER_STEP = 8
PER_TASKS = 2 * PER_STEP
LANES = 128
TASK_ROWS = 8
LIST_ROWS = 3
VMEM = pl.BlockSpec(memory_space=pltpu.VMEM)
SMEM = pl.BlockSpec(memory_space=pltpu.SMEM)
ANY = pl.BlockSpec(memory_space=pl.ANY)


def dot(a, b, dims):
    return lax.dot_general(a, b, dims, preferred_element_type=jnp.float32)


def split(value):
    high = value.astype(jnp.bfloat16)
    return high, (value - high.astype(jnp.float32)).astype(jnp.bfloat16)


def resident(value):
    return pltpu.with_memory_space_constraint(value, pltpu.VMEM)


def spread(source, first, ref, size):
    for leaf in range(ref.shape[1] // size):
        source[first + leaf] = ref[:, leaf * size : (leaf + 1) * size]


def subtract_near(count, task_ref, source, blocks_ref, acc_ref, slots):
    shift = count.bit_length()
    low = (1 << shift) - 1
    per_row = LANES // PER_TASKS

    def body(step, carry):
        done = []
        row = lax.div(step, per_row)
        at = lax.rem(step, per_row) * PER_TASKS
        for task in range(PER_STEP):
            one = task_ref[row, at + 2 * task]
            two = task_ref[row, at + 2 * task + 1]
            left, right = jnp.right_shift(one, shift), jnp.right_shift(two, shift)
            fetched = jnp.concatenate(
                [source[jnp.bitwise_and(one, low)], source[jnp.bitwise_and(two, low)]], axis=1
            )
            matrix = jnp.concatenate([blocks_ref[left], blocks_ref[right]], axis=1)
            done.append((lax.div(left, slots), dot(fetched, matrix, NT)))
        for leaf, near in done:
            acc_ref[leaf] = acc_ref[leaf] - near
        return carry

    lax.fori_loop(0, task_ref[LIST_ROWS - 1, LANES - 1], body, 0)


def list_tasks(index, number, device, lists_ref):
    slots, count = index.shape
    shift = count.bit_length()
    slot = lax.broadcasted_iota(jnp.int32, (slots, count), 0)
    leaf = lax.broadcasted_iota(jnp.int32, (slots, count), 1)
    at = index - (device * count - count)
    alive = slot < number
    before, after = at < count, at >= 2 * count
    even = jnp.broadcast_to(jnp.bitwise_and(device, 1), at.shape) == 0
    side = jnp.where(before == even, 1, 2)
    kind = jnp.where(jnp.logical_or(before, after), side, 0)
    code = jnp.left_shift(leaf * slots + slot, shift) + jnp.bitwise_and(at, count - 1)
    blank = count
    earlier_slot = (
        lax.broadcasted_iota(jnp.int32, (slots, slots), 1)
        < lax.broadcasted_iota(jnp.int32, (slots, slots), 0)
    ).astype(jnp.bfloat16)
    earlier_leaf = (
        lax.broadcasted_iota(jnp.int32, (count, count), 0)
        < lax.broadcasted_iota(jnp.int32, (count, count), 1)
    ).astype(jnp.bfloat16)
    place = jnp.full((slots, count), -1, jnp.int32)
    steps = []
    for which in range(3):
        chosen = jnp.logical_and(alive, kind == which)
        mark = jnp.where(chosen, 1.0, 0.0)
        rank = dot(earlier_slot, mark.astype(jnp.bfloat16), NN)
        number_here = jnp.sum(mark, axis=0, keepdims=True).astype(jnp.int32)
        padded = (number_here + jnp.bitwise_and(number_here, 1)).astype(jnp.float32)
        base = dot(jnp.broadcast_to(padded, (slots, count)).astype(jnp.bfloat16), earlier_leaf, NN)
        here = (base + rank).astype(jnp.int32) + which * LIST_ROWS * LANES
        place = jnp.where(chosen, here, place)
        total = jnp.sum(padded, axis=1, keepdims=True).astype(jnp.int32)
        steps.append(jnp.right_shift(total + PER_TASKS - 1, PER_TASKS.bit_length() - 1))
    place, value = place.T, code.T - blank
    lane = lax.broadcasted_iota(jnp.int32, (count, LANES), 1)
    for which in range(3):
        for row in range(LIST_ROWS):
            target = lane + (which * LIST_ROWS + row) * LANES
            total = jnp.zeros((count, LANES), jnp.int32)
            for k in range(slots):
                total += jnp.where(place[:, k : k + 1] == target, value[:, k : k + 1], 0)
            line = jnp.sum(total, axis=0, keepdims=True) + blank
            if row == LIST_ROWS - 1:
                line = jnp.where(lane[:1] == LANES - 1, steps[which], line)
            lists_ref[which, row : row + 1] = line


def path_products(upper_ref, mats_ref, basis_ref, weight_ref):
    count, rank, size = basis_ref.shape
    nodes = [split(upper_ref[0].astype(jnp.float32).T)]
    blank = jnp.zeros((rank, size), basis_ref.dtype)
    width = 2
    offset = 2 * count - 2
    while width <= count:
        offset = offset - width
        later = []
        for parent, (high, low) in enumerate(nodes):
            first = (offset + 2 * parent) * rank
            pair = mats_ref[first : first + 2 * rank, :]
            product = dot(high, pair, NT) + dot(low, pair, NT)
            pair_high, pair_low = split(product)
            if width == count:
                bases = jnp.concatenate(
                    [
                        jnp.concatenate([basis_ref[2 * parent], blank], axis=1),
                        jnp.concatenate([blank, basis_ref[2 * parent + 1]], axis=1),
                    ],
                    axis=0,
                )
                weight = split(dot(pair_high, bases, NN) + dot(pair_low, bases, NN))
                at = slice(2 * parent * size, 2 * (parent + 1) * size)
                weight_ref[:rank, at], weight_ref[rank:, at] = weight
            else:
                later.append((pair_high[:, :rank], pair_low[:, :rank]))
                later.append((pair_high[:, rank:], pair_low[:, rank:]))
        nodes = later
        width = 2 * width


def own_kernel(
    index_any,
    number_any,
    upper_ref,
    mats_ref,
    own_any,
    samples_any,
    blocks_any,
    basis_any,
    acc_ref,
    blocks_ref,
    basis_ref,
    weight_ref,
    twice_ref,
    first_task_ref,
    second_task_ref,
    own_task,
    lists,
    index_ref,
    number_ref,
    own_ref,
    samples_ref,
    source,
    sems,
):
    pairs = (
        (index_any, index_ref),
        (number_any, number_ref),
        (basis_any, basis_ref),
        (own_any, own_ref),
        (samples_any, samples_ref),
        (blocks_any, blocks_ref),
        (lists.at[0], own_task),
        (lists.at[1], first_task_ref),
        (lists.at[2], second_task_ref),
    )
    copies = [
        pltpu.make_async_copy(origin, target, sems.at[place])
        for place, (origin, target) in enumerate(pairs)
    ]
    for copy in copies[:6]:
        copy.start()
    slots, count = index_ref.shape
    size = blocks_ref.shape[1]
    rank = upper_ref.shape[1]
    copies[0].wait()
    copies[1].wait()
    list_tasks(index_ref[...], number_ref[...], lax.axis_index("leaf"), lists)
    for copy in copies[6:]:
        copy.start()
    copies[2].wait()
    path_products(upper_ref, mats_ref, basis_ref, weight_ref)
    for height in range(1, upper_ref.shape[0]):
        matrix = upper_ref[height].astype(jnp.float32)
        blank = jnp.zeros_like(matrix)
        twice_ref[height - 1, :rank] = jnp.concatenate([matrix, blank], axis=1)
        twice_ref[height - 1, rank:] = jnp.concatenate([blank, matrix], axis=1)
    copies[3].wait()
    spread(source, 0, own_ref, size)
    source[count] = jnp.zeros_like(source[count])
    copies[4].wait()
    for leaf in range(count):
        acc_ref[leaf] = samples_ref[:, leaf * size : (leaf + 1) * size].astype(jnp.float32)
    for copy in copies[5:]:
        copy.wait()
    subtract_near(count, own_task, source, blocks_ref, acc_ref, slots)


def side_kernel(task_ref, side_ref, near_ref, blocks_ref, slots, acc, source):
    del near_ref
    count, _, size = acc.shape
    spread(source, 0, side_ref, size)
    source[count] = jnp.zeros_like(source[count])
    subtract_near(count, task_ref, source, blocks_ref, acc, slots)


def far_kernel(
    task_ref, side_ref, near_ref, blocks_ref, weight_ref, far_ref, part_ref, acc, source
):
    count, _, size = acc.shape
    slots = blocks_ref.shape[0] // count
    side_kernel(task_ref, side_ref, near_ref, blocks_ref, slots, acc, source)
    for leaf in range(count):
        far_ref[:, leaf * size : (leaf + 1) * size] = acc[leaf].astype(jnp.bfloat16)
    product = dot(weight_ref[...], far_ref[...], NT)
    rank = product.shape[0] // 2
    turned = (product[:rank] + product[rank:]).T
    half = turned.shape[0] // 2
    part_ref[...] = jnp.concatenate([turned[:half], turned[half:]], axis=1)


def gram_kernel(
    scale, place_ref, far_ref, basis_ref, coeff_any, keep_ref, send_ref, gram, coeff_ref, sems
):
    parts, rows, pairs, width = keep_ref.shape
    parts = 2 * parts
    rank = width // 2
    size = basis_ref.shape[2]
    lane = lax.broadcasted_iota(jnp.int32, (rank, width), 1)
    copies = []
    for first in range(0, pairs, PER_STEP):
        stacks = []
        for pair in range(first, first + PER_STEP):
            both = []
            for leaf in (pair, pair + pairs):
                far = far_ref[:, leaf * size : (leaf + 1) * size]
                coeff = dot(basis_ref[leaf], far, NT)
                coeff_ref[leaf] = coeff
                both.append(coeff.astype(jnp.bfloat16))
            stacks.append(jnp.concatenate(both, axis=0))
        for start in (first, first + pairs):
            these = pl.ds(start, PER_STEP)
            copies.append(
                pltpu.make_async_copy(
                    coeff_ref.at[these], coeff_any.at[these], sems.at[len(copies)]
                )
            )
            copies[-1].start()
        for pair, stacked in enumerate(stacks, first):
            product = dot(stacked, stacked, NT)
            value = jnp.where(lane < rank, product[:rank], product[rank:]) * scale
            gram[pl.ds(pair, rank, stride=pairs), :] = value
    for relative in range(parts):
        first = jnp.bitwise_xor(place_ref[0], relative) * rows
        target = send_ref if relative % 2 else keep_ref
        for row in range(rows):
            at = pl.multiple_of((first + row) * pairs, pairs)
            target[relative // 2, row] = gram[pl.ds(at, pairs), :].astype(target.dtype)
    for copy in copies:
        copy.wait()


def finish_kernel(keep_ref, got_ref, received_ref, last_ref, out_ref):
    _, rows, pairs, width = keep_ref.shape
    half = width // 2
    lane = lax.broadcasted_iota(jnp.int32, (pairs, width), 1)
    for row in range(0, rows, 2):
        even, odd = (
            keep_ref[0, at]
            + got_ref[0, at].astype(jnp.float32)
            + received_ref[0, at].astype(jnp.float32)
            + last_ref[at]
            for at in (row, row + 1)
        )
        at = slice(row * half, (row + 2) * half)
        out_ref[:pairs, at] = jnp.where(lane < half, even, pltpu.roll(odd, half, 1))
        out_ref[pairs:, at] = jnp.where(lane < half, pltpu.roll(even, half, 1), odd)


def turn_kernel(*refs):
    levels, out_ref = refs[:-1], refs[-1]
    for height, level in enumerate(levels):
        turned = level[...].T
        half = turned.shape[0] // 2
        out_ref[height] = jnp.concatenate([turned[:half], turned[half:]], axis=1)


def params(mib):
    return pltpu.CompilerParams(vmem_limit_bytes=mib * 2**20)


def own_pass(index, number, upper, mats, own, samples, blocks, basis):
    slots, count = index.shape
    size = blocks.shape[1]
    columns = own.shape[0]
    heights, rank, _ = upper.shape
    tasks = pltpu.SMEM((TASK_ROWS, LANES), jnp.int32)
    far = lambda value: pltpu.with_memory_space_constraint(value, pltpu.HBM)
    return pl.pallas_call(
        own_kernel,
        in_specs=[ANY, ANY, VMEM, VMEM, ANY, ANY, ANY, ANY],
        out_specs=(VMEM, VMEM, VMEM, VMEM, VMEM, SMEM, SMEM),
        out_shape=(
            pltpu.VMEM((count, columns, size), jnp.float32),
            pltpu.VMEM(blocks.shape, blocks.dtype),
            pltpu.VMEM(basis.shape, basis.dtype),
            pltpu.VMEM((2 * rank, count * size), jnp.bfloat16),
            pltpu.VMEM((heights - 1, 2 * rank, 2 * rank), jnp.float32),
            tasks,
            tasks,
        ),
        scratch_shapes=[
            tasks,
            pltpu.VMEM((3, TASK_ROWS, LANES), jnp.int32),
            pltpu.VMEM((slots, count), jnp.int32),
            pltpu.VMEM((1, count), jnp.int32),
            pltpu.VMEM(own.shape, own.dtype),
            pltpu.VMEM(samples.shape, samples.dtype),
            pltpu.VMEM((count + 1, columns, size), jnp.bfloat16),
            pltpu.SemaphoreType.DMA((9,)),
        ],
        compiler_params=params(8),
        name="own_pass",
    )(
        far(index),
        far(number),
        resident(upper),
        resident(mats),
        far(own),
        far(samples),
        far(blocks),
        far(basis),
    )


def side_pass(tasks, side, near, blocks):
    count, columns, size = near.shape
    slots = blocks.shape[0] // count

    def kernel(task_ref, side_ref, near_ref, blocks_ref, acc, source):
        side_kernel(task_ref, side_ref, near_ref, blocks_ref, slots, acc, source)

    return pl.pallas_call(
        kernel,
        in_specs=[SMEM] + [VMEM] * 3,
        out_specs=VMEM,
        out_shape=pltpu.VMEM((count, columns, size), jnp.float32),
        input_output_aliases={2: 0},
        scratch_shapes=[pltpu.VMEM((count + 1, columns, size), jnp.bfloat16)],
        compiler_params=params(8),
        name="side_pass",
    )(tasks, resident(side), near, blocks)


def far_pass(tasks, side, near, blocks, weight):
    count, columns, size = near.shape
    rank = weight.shape[0] // 2
    return pl.pallas_call(
        far_kernel,
        in_specs=[SMEM] + [VMEM] * 4,
        out_specs=(VMEM, VMEM, VMEM),
        out_shape=(
            pltpu.VMEM((columns, count * size), jnp.bfloat16),
            pltpu.VMEM((columns // 2, 2 * rank), jnp.float32),
            pltpu.VMEM((count, columns, size), jnp.float32),
        ),
        input_output_aliases={2: 2},
        scratch_shapes=[pltpu.VMEM((count + 1, columns, size), jnp.bfloat16)],
        compiler_params=params(8),
        name="far_pass",
    )(tasks, resident(side), near, blocks, weight)


def gram_pass(place, far, basis, parts):
    count, rank, _ = basis.shape
    columns = far.shape[0]
    pairs = count // 2
    shape = (parts // 2, rank // parts, pairs, 2 * rank)
    return pl.pallas_call(
        functools.partial(gram_kernel, 1.0 / (columns * parts)),
        in_specs=[SMEM, VMEM, VMEM],
        out_specs=(ANY, VMEM, VMEM),
        out_shape=(
            pltpu.HBM((count, rank, columns), jnp.float32),
            pltpu.VMEM(shape, jnp.float32),
            pltpu.VMEM(shape, jnp.bfloat16),
        ),
        scratch_shapes=[
            pltpu.VMEM((rank * pairs, 2 * rank), jnp.float32),
            pltpu.VMEM((count, rank, columns), jnp.float32),
            pltpu.SemaphoreType.DMA((count // PER_STEP,)),
        ],
        compiler_params=params(8),
        name="gram_pass",
    )(place, far, basis)


def exchange(value, axis, flip):
    return lax.ppermute(value, axis, [(i, i ^ flip) for i in range(lax.axis_size(axis))])


def swap(value, axis, first):
    pairs = [(i, i + 1) for i in range(first, lax.axis_size(axis) - 1, 2)]
    return lax.ppermute(value, axis, pairs + [(j, i) for i, j in pairs])


def shards(
    samples, omega, leaf_basis, near_blocks, near_index, near_count, inner_transfer, upper_transfer
):
    count = near_count.shape[0]
    slots = near_index.shape[1]
    rank = leaf_basis.shape[1]
    size = leaf_basis.shape[2]
    groups = lax.axis_size("leaf")
    parts = lax.axis_size("samp")
    device = lax.axis_index("leaf")
    place = lax.axis_index("samp").astype(jnp.int32)

    own = omega.T
    first = swap(own, "leaf", 1)
    second = swap(own, "leaf", 0)

    heights = groups.bit_length() - 1
    rows = []
    offset, width = 0, groups
    for height in range(heights):
        rows.append(
            lax.dynamic_slice_in_dim(
                upper_transfer, offset + jnp.right_shift(device, height), 1, axis=0
            )
        )
        offset, width = offset + width, width // 2
    upper = jnp.concatenate(rows, axis=0).reshape(heights, rank, rank)

    blocks = near_blocks.reshape(count * slots, size, size)
    near, blocks, basis, weight, twice, crossing_tasks, tasks = own_pass(
        near_index.T,
        near_count.reshape(1, count),
        upper,
        inner_transfer.reshape(-1, rank),
        own,
        samples.T,
        blocks,
        leaf_basis,
    )
    near = side_pass(tasks, second, near, blocks)
    far, part, _ = far_pass(crossing_tasks, first, near, blocks, weight)

    flips = (1, 3, 4, 8, 24)
    levels = []
    accum = part
    for height in range(heights):
        if height:
            accum = jnp.dot(accum, twice[height - 1], precision=lax.Precision.HIGHEST)
        other = exchange(accum, "leaf", flips[height])
        if height == 0:
            coeffs, keep, send = gram_pass(place.reshape(1), far, basis, parts)
            got = exchange(send, "samp", 1)
        elif height == 1:
            leaving = (keep[1:3] + got[1:3].astype(jnp.float32)).astype(jnp.bfloat16)
            other, _ = lax.optimization_barrier((other, leaving))
            received = exchange(leaving, "samp", 2)
        elif height == 2:
            leaving = keep[3] + got[3].astype(jnp.float32) + received[1].astype(jnp.float32)
            other, _ = lax.optimization_barrier((other, leaving))
            last = exchange(leaving, "samp", 6)
        elif height == 4:
            leaf_gram = pl.pallas_call(
                finish_kernel,
                in_specs=[VMEM] * 4,
                out_specs=VMEM,
                out_shape=jax.ShapeDtypeStruct((count, rank * rank // parts), jnp.float32),
                compiler_params=params(8),
                name="finish",
            )(keep, *map(resident, [got, received, last]))
            other, _ = lax.optimization_barrier((other, leaf_gram))
        accum = accum + other
        levels.append(accum)
    ancestors = pl.pallas_call(
        turn_kernel,
        in_specs=[VMEM] * heights,
        out_specs=VMEM,
        out_shape=jax.ShapeDtypeStruct((heights, rank, 2 * part.shape[0]), jnp.float32),
        compiler_params=params(8),
        name="turn",
    )(*map(resident, levels))
    return coeffs, leaf_gram, ancestors[None]


def solution(mesh):
    return jax.shard_map(
        shards,
        mesh=mesh,
        in_specs=(
            P("leaf", "samp"),
            P("leaf", "samp"),
            P("leaf", None, None),
            P("leaf", None, None, None),
            P("leaf", None),
            P("leaf"),
            P("leaf", None),
            P(),
        ),
        out_specs=(P("leaf", None, "samp"), P("leaf", "samp"), P("leaf", None, None, "samp")),
        check_vma=False,
    )
```

```python
import functools

import jax
import jax.numpy as jnp
from jax import lax
from jax.experimental import pallas as pl
from jax.experimental.pallas import tpu as pltpu
from jax.sharding import PartitionSpec as P

NT = (((1,), (1,)), ((), ()))
NN = (((1,), (0,)), ((), ()))
PER_STEP = 8
PER_TASKS = 2 * PER_STEP
LANES = 128
TASK_ROWS = 8
LIST_ROWS = 3
VMEM = pl.BlockSpec(memory_space=pltpu.VMEM)
SMEM = pl.BlockSpec(memory_space=pltpu.SMEM)
ANY = pl.BlockSpec(memory_space=pl.ANY)


def dot(a, b, dims):
    return lax.dot_general(a, b, dims, preferred_element_type=jnp.float32)


def split(value):
    high = value.astype(jnp.bfloat16)
    return high, (value - high.astype(jnp.float32)).astype(jnp.bfloat16)


def resident(value):
    return pltpu.with_memory_space_constraint(value, pltpu.VMEM)


def spread(source, first, ref, size):
    for leaf in range(ref.shape[1] // size):
        source[first + leaf] = ref[:, leaf * size : (leaf + 1) * size]


def subtract_near(count, task_ref, source, blocks_ref, acc_ref, slots):
    shift = count.bit_length()
    low = (1 << shift) - 1
    per_row = LANES // PER_TASKS

    def body(step, carry):
        done = []
        row = lax.div(step, per_row)
        at = lax.rem(step, per_row) * PER_TASKS
        for task in range(PER_STEP):
            one = task_ref[row, at + 2 * task]
            two = task_ref[row, at + 2 * task + 1]
            left, right = jnp.right_shift(one, shift), jnp.right_shift(two, shift)
            fetched = jnp.concatenate(
                [source[jnp.bitwise_and(one, low)], source[jnp.bitwise_and(two, low)]], axis=1
            )
            matrix = jnp.concatenate([blocks_ref[left], blocks_ref[right]], axis=1)
            done.append((lax.div(left, slots), dot(fetched, matrix, NT)))
        for leaf, near in done:
            acc_ref[leaf] = acc_ref[leaf] - near
        return carry

    lax.fori_loop(0, task_ref[LIST_ROWS - 1, LANES - 1], body, 0)


def list_tasks(index, number, device, lists_ref):
    slots, count = index.shape
    shift = count.bit_length()
    slot = lax.broadcasted_iota(jnp.int32, (slots, count), 0)
    leaf = lax.broadcasted_iota(jnp.int32, (slots, count), 1)
    at = index - (device * count - count)
    alive = slot < number
    before, after = at < count, at >= 2 * count
    even = jnp.broadcast_to(jnp.bitwise_and(device, 1), at.shape) == 0
    side = jnp.where(before == even, 1, 2)
    kind = jnp.where(jnp.logical_or(before, after), side, 0)
    code = jnp.left_shift(leaf * slots + slot, shift) + jnp.bitwise_and(at, count - 1)
    blank = count
    earlier_slot = (
        lax.broadcasted_iota(jnp.int32, (slots, slots), 1)
        < lax.broadcasted_iota(jnp.int32, (slots, slots), 0)
    ).astype(jnp.bfloat16)
    earlier_leaf = (
        lax.broadcasted_iota(jnp.int32, (count, count), 0)
        < lax.broadcasted_iota(jnp.int32, (count, count), 1)
    ).astype(jnp.bfloat16)
    place = jnp.full((slots, count), -1, jnp.int32)
    steps = []
    for which in range(3):
        chosen = jnp.logical_and(alive, kind == which)
        mark = jnp.where(chosen, 1.0, 0.0)
        rank = dot(earlier_slot, mark.astype(jnp.bfloat16), NN)
        number_here = jnp.sum(mark, axis=0, keepdims=True).astype(jnp.int32)
        padded = (number_here + jnp.bitwise_and(number_here, 1)).astype(jnp.float32)
        base = dot(jnp.broadcast_to(padded, (slots, count)).astype(jnp.bfloat16), earlier_leaf, NN)
        here = (base + rank).astype(jnp.int32) + which * LIST_ROWS * LANES
        place = jnp.where(chosen, here, place)
        total = jnp.sum(padded, axis=1, keepdims=True).astype(jnp.int32)
        steps.append(jnp.right_shift(total + PER_TASKS - 1, PER_TASKS.bit_length() - 1))
    place, value = place.T, code.T - blank
    lane = lax.broadcasted_iota(jnp.int32, (count, LANES), 1)
    for which in range(3):
        for row in range(LIST_ROWS):
            target = lane + (which * LIST_ROWS + row) * LANES
            total = jnp.zeros((count, LANES), jnp.int32)
            for k in range(slots):
                total += jnp.where(place[:, k : k + 1] == target, value[:, k : k + 1], 0)
            line = jnp.sum(total, axis=0, keepdims=True) + blank
            if row == LIST_ROWS - 1:
                line = jnp.where(lane[:1] == LANES - 1, steps[which], line)
            lists_ref[which, row : row + 1] = line


def path_products(upper_ref, mats_ref, basis_ref, weight_ref):
    count, rank, size = basis_ref.shape
    nodes = [split(upper_ref[0].astype(jnp.float32).T)]
    blank = jnp.zeros((rank, size), basis_ref.dtype)
    width = 2
    offset = 2 * count - 2
    while width <= count:
        offset = offset - width
        later = []
        for parent, (high, low) in enumerate(nodes):
            first = (offset + 2 * parent) * rank
            pair = mats_ref[first : first + 2 * rank, :]
            product = dot(high, pair, NT) + dot(low, pair, NT)
            pair_high, pair_low = split(product)
            if width == count:
                bases = jnp.concatenate(
                    [
                        jnp.concatenate([basis_ref[2 * parent], blank], axis=1),
                        jnp.concatenate([blank, basis_ref[2 * parent + 1]], axis=1),
                    ],
                    axis=0,
                )
                weight = split(dot(pair_high, bases, NN) + dot(pair_low, bases, NN))
                at = slice(2 * parent * size, 2 * (parent + 1) * size)
                weight_ref[:rank, at], weight_ref[rank:, at] = weight
            else:
                later.append((pair_high[:, :rank], pair_low[:, :rank]))
                later.append((pair_high[:, rank:], pair_low[:, rank:]))
        nodes = later
        width = 2 * width


def own_kernel(
    index_any,
    number_any,
    upper_ref,
    mats_ref,
    own_any,
    samples_any,
    blocks_any,
    basis_any,
    acc_ref,
    blocks_ref,
    basis_ref,
    weight_ref,
    twice_ref,
    first_task_ref,
    second_task_ref,
    own_task,
    lists,
    index_ref,
    number_ref,
    own_ref,
    samples_ref,
    source,
    sems,
):
    pairs = (
        (index_any, index_ref),
        (number_any, number_ref),
        (basis_any, basis_ref),
        (own_any, own_ref),
        (samples_any, samples_ref),
        (blocks_any, blocks_ref),
        (lists.at[0], own_task),
        (lists.at[1], first_task_ref),
        (lists.at[2], second_task_ref),
    )
    copies = [
        pltpu.make_async_copy(origin, target, sems.at[place])
        for place, (origin, target) in enumerate(pairs)
    ]
    for copy in copies[:6]:
        copy.start()
    slots, count = index_ref.shape
    size = blocks_ref.shape[1]
    rank = upper_ref.shape[1]
    copies[0].wait()
    copies[1].wait()
    list_tasks(index_ref[...], number_ref[...], lax.axis_index("leaf"), lists)
    for copy in copies[6:]:
        copy.start()
    copies[2].wait()
    path_products(upper_ref, mats_ref, basis_ref, weight_ref)
    for height in range(1, upper_ref.shape[0]):
        matrix = upper_ref[height].astype(jnp.float32)
        blank = jnp.zeros_like(matrix)
        twice_ref[height - 1, :rank] = jnp.concatenate([matrix, blank], axis=1)
        twice_ref[height - 1, rank:] = jnp.concatenate([blank, matrix], axis=1)
    copies[3].wait()
    spread(source, 0, own_ref, size)
    source[count] = jnp.zeros_like(source[count])
    copies[4].wait()
    for leaf in range(count):
        acc_ref[leaf] = samples_ref[:, leaf * size : (leaf + 1) * size].astype(jnp.float32)
    for copy in copies[5:]:
        copy.wait()
    subtract_near(count, own_task, source, blocks_ref, acc_ref, slots)


def side_kernel(task_ref, side_ref, near_ref, blocks_ref, slots, acc, source):
    del near_ref
    count, _, size = acc.shape
    spread(source, 0, side_ref, size)
    source[count] = jnp.zeros_like(source[count])
    subtract_near(count, task_ref, source, blocks_ref, acc, slots)


def far_kernel(
    task_ref, side_ref, near_ref, blocks_ref, weight_ref, far_ref, part_ref, acc, source
):
    count, _, size = acc.shape
    slots = blocks_ref.shape[0] // count
    side_kernel(task_ref, side_ref, near_ref, blocks_ref, slots, acc, source)
    for leaf in range(count):
        far_ref[:, leaf * size : (leaf + 1) * size] = acc[leaf].astype(jnp.bfloat16)
    product = dot(weight_ref[...], far_ref[...], NT)
    rank = product.shape[0] // 2
    turned = (product[:rank] + product[rank:]).T
    half = turned.shape[0] // 2
    part_ref[...] = jnp.concatenate([turned[:half], turned[half:]], axis=1)


def gram_kernel(
    scale, place_ref, far_ref, basis_ref, coeff_any, keep_ref, send_ref, gram, coeff_ref, sems
):
    parts, rows, pairs, width = keep_ref.shape
    parts = 2 * parts
    rank = width // 2
    size = basis_ref.shape[2]
    lane = lax.broadcasted_iota(jnp.int32, (rank, width), 1)
    copies = []
    for first in range(0, pairs, PER_STEP):
        stacks = []
        for pair in range(first, first + PER_STEP):
            both = []
            for leaf in (pair, pair + pairs):
                far = far_ref[:, leaf * size : (leaf + 1) * size]
                coeff = dot(basis_ref[leaf], far, NT)
                coeff_ref[leaf] = coeff
                both.append(coeff.astype(jnp.bfloat16))
            stacks.append(jnp.concatenate(both, axis=0))
        for start in (first, first + pairs):
            these = pl.ds(start, PER_STEP)
            copies.append(
                pltpu.make_async_copy(
                    coeff_ref.at[these], coeff_any.at[these], sems.at[len(copies)]
                )
            )
            copies[-1].start()
        for pair, stacked in enumerate(stacks, first):
            product = dot(stacked, stacked, NT)
            value = jnp.where(lane < rank, product[:rank], product[rank:]) * scale
            gram[pl.ds(pair, rank, stride=pairs), :] = value
    for relative in range(parts):
        first = jnp.bitwise_xor(place_ref[0], relative) * rows
        target = send_ref if relative % 2 else keep_ref
        for row in range(rows):
            at = pl.multiple_of((first + row) * pairs, pairs)
            target[relative // 2, row] = gram[pl.ds(at, pairs), :].astype(target.dtype)
    for copy in copies:
        copy.wait()


def finish_kernel(keep_ref, got_ref, received_ref, last_ref, out_ref):
    _, rows, pairs, width = keep_ref.shape
    half = width // 2
    lane = lax.broadcasted_iota(jnp.int32, (pairs, width), 1)
    for row in range(0, rows, 2):
        even, odd = (
            keep_ref[0, at]
            + got_ref[0, at].astype(jnp.float32)
            + received_ref[0, at].astype(jnp.float32)
            + last_ref[at]
            for at in (row, row + 1)
        )
        at = slice(row * half, (row + 2) * half)
        out_ref[:pairs, at] = jnp.where(lane < half, even, pltpu.roll(odd, half, 1))
        out_ref[pairs:, at] = jnp.where(lane < half, pltpu.roll(even, half, 1), odd)


def turn_kernel(*refs):
    levels, out_ref = refs[:-1], refs[-1]
    for height, level in enumerate(levels):
        turned = level[...].T
        half = turned.shape[0] // 2
        out_ref[height] = jnp.concatenate([turned[:half], turned[half:]], axis=1)


def params(mib):
    return pltpu.CompilerParams(vmem_limit_bytes=mib * 2**20)


def own_pass(index, number, upper, mats, own, samples, blocks, basis):
    slots, count = index.shape
    size = blocks.shape[1]
    columns = own.shape[0]
    heights, rank, _ = upper.shape
    tasks = pltpu.SMEM((TASK_ROWS, LANES), jnp.int32)
    far = lambda value: pltpu.with_memory_space_constraint(value, pltpu.HBM)
    return pl.pallas_call(
        own_kernel,
        in_specs=[ANY, ANY, VMEM, VMEM, ANY, ANY, ANY, ANY],
        out_specs=(VMEM, VMEM, VMEM, VMEM, VMEM, SMEM, SMEM),
        out_shape=(
            pltpu.VMEM((count, columns, size), jnp.float32),
            pltpu.VMEM(blocks.shape, blocks.dtype),
            pltpu.VMEM(basis.shape, basis.dtype),
            pltpu.VMEM((2 * rank, count * size), jnp.bfloat16),
            pltpu.VMEM((heights - 1, 2 * rank, 2 * rank), jnp.float32),
            tasks,
            tasks,
        ),
        scratch_shapes=[
            tasks,
            pltpu.VMEM((3, TASK_ROWS, LANES), jnp.int32),
            pltpu.VMEM((slots, count), jnp.int32),
            pltpu.VMEM((1, count), jnp.int32),
            pltpu.VMEM(own.shape, own.dtype),
            pltpu.VMEM(samples.shape, samples.dtype),
            pltpu.VMEM((count + 1, columns, size), jnp.bfloat16),
            pltpu.SemaphoreType.DMA((9,)),
        ],
        compiler_params=params(8),
        name="own_pass",
    )(
        far(index),
        far(number),
        resident(upper),
        resident(mats),
        far(own),
        far(samples),
        far(blocks),
        far(basis),
    )


def side_pass(tasks, side, near, blocks):
    count, columns, size = near.shape
    slots = blocks.shape[0] // count

    def kernel(task_ref, side_ref, near_ref, blocks_ref, acc, source):
        side_kernel(task_ref, side_ref, near_ref, blocks_ref, slots, acc, source)

    return pl.pallas_call(
        kernel,
        in_specs=[SMEM] + [VMEM] * 3,
        out_specs=VMEM,
        out_shape=pltpu.VMEM((count, columns, size), jnp.float32),
        input_output_aliases={2: 0},
        scratch_shapes=[pltpu.VMEM((count + 1, columns, size), jnp.bfloat16)],
        compiler_params=params(8),
        name="side_pass",
    )(tasks, resident(side), near, blocks)


def far_pass(tasks, side, near, blocks, weight):
    count, columns, size = near.shape
    rank = weight.shape[0] // 2
    return pl.pallas_call(
        far_kernel,
        in_specs=[SMEM] + [VMEM] * 4,
        out_specs=(VMEM, VMEM, VMEM),
        out_shape=(
            pltpu.VMEM((columns, count * size), jnp.bfloat16),
            pltpu.VMEM((columns // 2, 2 * rank), jnp.float32),
            pltpu.VMEM((count, columns, size), jnp.float32),
        ),
        input_output_aliases={2: 2},
        scratch_shapes=[pltpu.VMEM((count + 1, columns, size), jnp.bfloat16)],
        compiler_params=params(8),
        name="far_pass",
    )(tasks, resident(side), near, blocks, weight)


def gram_pass(place, far, basis, parts):
    count, rank, _ = basis.shape
    columns = far.shape[0]
    pairs = count // 2
    shape = (parts // 2, rank // parts, pairs, 2 * rank)
    return pl.pallas_call(
        functools.partial(gram_kernel, 1.0 / (columns * parts)),
        in_specs=[SMEM, VMEM, VMEM],
        out_specs=(ANY, VMEM, VMEM),
        out_shape=(
            pltpu.HBM((count, rank, columns), jnp.float32),
            pltpu.VMEM(shape, jnp.float32),
            pltpu.VMEM(shape, jnp.bfloat16),
        ),
        scratch_shapes=[
            pltpu.VMEM((rank * pairs, 2 * rank), jnp.float32),
            pltpu.VMEM((count, rank, columns), jnp.float32),
            pltpu.SemaphoreType.DMA((count // PER_STEP,)),
        ],
        compiler_params=params(8),
        name="gram_pass",
    )(place, far, basis)


def exchange(value, axis, flip):
    return lax.ppermute(value, axis, [(i, i ^ flip) for i in range(lax.axis_size(axis))])


def swap(value, axis, first):
    pairs = [(i, i + 1) for i in range(first, lax.axis_size(axis) - 1, 2)]
    return lax.ppermute(value, axis, pairs + [(j, i) for i, j in pairs])


def shards(
    samples, omega, leaf_basis, near_blocks, near_index, near_count, inner_transfer, upper_transfer
):
    count = near_count.shape[0]
    slots = near_index.shape[1]
    rank = leaf_basis.shape[1]
    size = leaf_basis.shape[2]
    groups = lax.axis_size("leaf")
    parts = lax.axis_size("samp")
    device = lax.axis_index("leaf")
    place = lax.axis_index("samp").astype(jnp.int32)

    own = omega.T
    first = swap(own, "leaf", 1)
    second = swap(own, "leaf", 0)

    heights = groups.bit_length() - 1
    nodes = []
    offset, width = 0, groups
    for height in range(heights):
        node = jnp.right_shift(device, height)
        nodes.append(offset + node)
        sibling = offset + jnp.bitwise_xor(node, 1)
        offset, width = offset + width, width // 2
    rows = [lax.dynamic_slice_in_dim(upper_transfer, n, 1, axis=0) for n in nodes + [sibling]]
    upper = jnp.concatenate(rows, axis=0).reshape(heights + 1, rank, rank)

    blocks = near_blocks.reshape(count * slots, size, size)
    near, blocks, basis, weight, twice, crossing_tasks, tasks = own_pass(
        near_index.T,
        near_count.reshape(1, count),
        upper,
        inner_transfer.reshape(-1, rank),
        own,
        samples.T,
        blocks,
        leaf_basis,
    )
    near = side_pass(tasks, second, near, blocks)
    far, part, _ = far_pass(crossing_tasks, first, near, blocks, weight)

    def step(value, matrix):
        return jnp.dot(value, matrix, precision=lax.Precision.HIGHEST)

    levels = []
    accum = part
    for height, flip in enumerate((1, 3, 4)):
        if height:
            accum = step(accum, twice[height - 1])
        other = exchange(accum, "leaf", flip)
        if height == 0:
            coeffs, keep, send = gram_pass(place.reshape(1), far, basis, parts)
            got = exchange(send, "samp", 1)
        elif height == 1:
            leaving = keep[1:3] + got[1:3].astype(jnp.float32)
            leaving = leaving.astype(jnp.bfloat16)
            other, _ = lax.optimization_barrier((other, leaving))
            received = exchange(leaving, "samp", 2)
        elif height == 2:
            leaving = keep[3] + got[3].astype(jnp.float32) + received[1].astype(jnp.float32)
            other, _ = lax.optimization_barrier((other, leaving))
            last = exchange(leaving, "samp", 6)
        accum = accum + other
        levels.append(accum)
    accum = step(accum, twice[2])
    others = [exchange(accum, "leaf", flip) for flip in (24, 8, 20)]
    leaf_gram = pl.pallas_call(
        finish_kernel,
        in_specs=[VMEM] * 4,
        out_specs=VMEM,
        out_shape=jax.ShapeDtypeStruct((count, rank * rank // parts), jnp.float32),
        compiler_params=params(8),
        name="finish",
    )(keep, *map(resident, [got, received, last]))
    *others, _ = lax.optimization_barrier((*others, leaf_gram))
    third, sibling, fourth = others
    levels.append(accum + sibling)
    levels.append(step(levels[-1], twice[3]) + step(third + fourth, twice[4]))
    ancestors = pl.pallas_call(
        turn_kernel,
        in_specs=[VMEM] * heights,
        out_specs=VMEM,
        out_shape=jax.ShapeDtypeStruct((heights, rank, 2 * part.shape[0]), jnp.float32),
        compiler_params=params(8),
        name="turn",
    )(*map(resident, levels))
    return coeffs, leaf_gram, ancestors[None]


def solution(mesh):
    return jax.shard_map(
        shards,
        mesh=mesh,
        in_specs=(
            P("leaf", "samp"),
            P("leaf", "samp"),
            P("leaf", None, None),
            P("leaf", None, None, None),
            P("leaf", None),
            P("leaf"),
            P("leaf", None),
            P(),
        ),
        out_specs=(P("leaf", None, "samp"), P("leaf", "samp"), P("leaf", None, None, "samp")),
        check_vma=False,
    )
```

```python
import functools

import jax
import jax.numpy as jnp
from jax import lax
from jax.experimental import pallas as pl
from jax.experimental.pallas import tpu as pltpu
from jax.sharding import PartitionSpec as P

NT = (((1,), (1,)), ((), ()))
NN = (((1,), (0,)), ((), ()))
PER_STEP = 8
PER_TASKS = 2 * PER_STEP
LANES = 128
TASK_ROWS = 8
LIST_ROWS = 3
VMEM = pl.BlockSpec(memory_space=pltpu.VMEM)
SMEM = pl.BlockSpec(memory_space=pltpu.SMEM)
ANY = pl.BlockSpec(memory_space=pl.ANY)


def dot(a, b, dims):
    return lax.dot_general(a, b, dims, preferred_element_type=jnp.float32)


def split(value):
    high = value.astype(jnp.bfloat16)
    return high, (value - high.astype(jnp.float32)).astype(jnp.bfloat16)


def resident(value):
    return pltpu.with_memory_space_constraint(value, pltpu.VMEM)


def spread(source, first, ref, size):
    for leaf in range(ref.shape[1] // size):
        source[first + leaf] = ref[:, leaf * size : (leaf + 1) * size]


def subtract_near(count, task_ref, source, blocks_ref, acc_ref, slots):
    shift = count.bit_length()
    low = (1 << shift) - 1
    per_row = LANES // PER_TASKS

    def body(step, carry):
        done = []
        row = lax.div(step, per_row)
        at = lax.rem(step, per_row) * PER_TASKS
        for task in range(PER_STEP):
            one = task_ref[row, at + 2 * task]
            two = task_ref[row, at + 2 * task + 1]
            left, right = jnp.right_shift(one, shift), jnp.right_shift(two, shift)
            fetched = jnp.concatenate(
                [source[jnp.bitwise_and(one, low)], source[jnp.bitwise_and(two, low)]], axis=1
            )
            matrix = jnp.concatenate([blocks_ref[left], blocks_ref[right]], axis=1)
            done.append((lax.div(left, slots), dot(fetched, matrix, NT)))
        for leaf, near in done:
            acc_ref[leaf] = acc_ref[leaf] - near
        return carry

    lax.fori_loop(0, task_ref[LIST_ROWS - 1, LANES - 1], body, 0)


def list_tasks(index, number, device, lists_ref):
    slots, count = index.shape
    shift = count.bit_length()
    slot = lax.broadcasted_iota(jnp.int32, (slots, count), 0)
    leaf = lax.broadcasted_iota(jnp.int32, (slots, count), 1)
    at = index - (device * count - count)
    alive = slot < number
    before, after = at < count, at >= 2 * count
    even = jnp.broadcast_to(jnp.bitwise_and(device, 1), at.shape) == 0
    side = jnp.where(before == even, 1, 2)
    kind = jnp.where(jnp.logical_or(before, after), side, 0)
    code = jnp.left_shift(leaf * slots + slot, shift) + jnp.bitwise_and(at, count - 1)
    blank = count
    earlier_slot = (
        lax.broadcasted_iota(jnp.int32, (slots, slots), 1)
        < lax.broadcasted_iota(jnp.int32, (slots, slots), 0)
    ).astype(jnp.bfloat16)
    earlier_leaf = (
        lax.broadcasted_iota(jnp.int32, (count, count), 0)
        < lax.broadcasted_iota(jnp.int32, (count, count), 1)
    ).astype(jnp.bfloat16)
    place = jnp.full((slots, count), -1, jnp.int32)
    steps = []
    for which in range(3):
        chosen = jnp.logical_and(alive, kind == which)
        mark = jnp.where(chosen, 1.0, 0.0)
        rank = dot(earlier_slot, mark.astype(jnp.bfloat16), NN)
        number_here = jnp.sum(mark, axis=0, keepdims=True).astype(jnp.int32)
        padded = (number_here + jnp.bitwise_and(number_here, 1)).astype(jnp.float32)
        base = dot(jnp.broadcast_to(padded, (slots, count)).astype(jnp.bfloat16), earlier_leaf, NN)
        here = (base + rank).astype(jnp.int32) + which * LIST_ROWS * LANES
        place = jnp.where(chosen, here, place)
        total = jnp.sum(padded, axis=1, keepdims=True).astype(jnp.int32)
        steps.append(jnp.right_shift(total + PER_TASKS - 1, PER_TASKS.bit_length() - 1))
    place, value = place.T, code.T - blank
    lane = lax.broadcasted_iota(jnp.int32, (count, LANES), 1)
    for which in range(3):
        for row in range(LIST_ROWS):
            target = lane + (which * LIST_ROWS + row) * LANES
            total = jnp.zeros((count, LANES), jnp.int32)
            for k in range(slots):
                total += jnp.where(place[:, k : k + 1] == target, value[:, k : k + 1], 0)
            line = jnp.sum(total, axis=0, keepdims=True) + blank
            if row == LIST_ROWS - 1:
                line = jnp.where(lane[:1] == LANES - 1, steps[which], line)
            lists_ref[which, row : row + 1] = line


def path_products(upper_ref, mats_ref, basis_ref, weight_ref):
    count, rank, size = basis_ref.shape
    nodes = [split(upper_ref[0].astype(jnp.float32).T)]
    blank = jnp.zeros((rank, size), basis_ref.dtype)
    width = 2
    offset = 2 * count - 2
    while width <= count:
        offset = offset - width
        later = []
        for parent, (high, low) in enumerate(nodes):
            first = (offset + 2 * parent) * rank
            pair = mats_ref[first : first + 2 * rank, :]
            product = dot(high, pair, NT) + dot(low, pair, NT)
            pair_high, pair_low = split(product)
            if width == count:
                bases = jnp.concatenate(
                    [
                        jnp.concatenate([basis_ref[2 * parent], blank], axis=1),
                        jnp.concatenate([blank, basis_ref[2 * parent + 1]], axis=1),
                    ],
                    axis=0,
                )
                weight = split(dot(pair_high, bases, NN) + dot(pair_low, bases, NN))
                at = slice(2 * parent * size, 2 * (parent + 1) * size)
                weight_ref[:rank, at], weight_ref[rank:, at] = weight
            else:
                later.append((pair_high[:, :rank], pair_low[:, :rank]))
                later.append((pair_high[:, rank:], pair_low[:, rank:]))
        nodes = later
        width = 2 * width


def own_kernel(
    index_any,
    number_any,
    upper_ref,
    mats_ref,
    own_any,
    samples_any,
    blocks_any,
    basis_any,
    acc_ref,
    blocks_ref,
    basis_ref,
    weight_ref,
    twice_ref,
    first_task_ref,
    second_task_ref,
    own_task,
    lists,
    index_ref,
    number_ref,
    own_ref,
    samples_ref,
    source,
    sems,
):
    pairs = (
        (index_any, index_ref),
        (number_any, number_ref),
        (basis_any, basis_ref),
        (own_any, own_ref),
        (samples_any, samples_ref),
        (blocks_any, blocks_ref),
        (lists.at[0], own_task),
        (lists.at[1], first_task_ref),
        (lists.at[2], second_task_ref),
    )
    copies = [
        pltpu.make_async_copy(origin, target, sems.at[place])
        for place, (origin, target) in enumerate(pairs)
    ]
    for copy in copies[:6]:
        copy.start()
    slots, count = index_ref.shape
    size = blocks_ref.shape[1]
    rank = upper_ref.shape[1]
    copies[0].wait()
    copies[1].wait()
    list_tasks(index_ref[...], number_ref[...], lax.axis_index("leaf"), lists)
    for copy in copies[6:]:
        copy.start()
    copies[2].wait()
    path_products(upper_ref, mats_ref, basis_ref, weight_ref)
    for height in range(1, upper_ref.shape[0]):
        matrix = upper_ref[height].astype(jnp.float32)
        blank = jnp.zeros_like(matrix)
        twice_ref[height - 1, :rank] = jnp.concatenate([matrix, blank], axis=1)
        twice_ref[height - 1, rank:] = jnp.concatenate([blank, matrix], axis=1)
    copies[3].wait()
    spread(source, 0, own_ref, size)
    source[count] = jnp.zeros_like(source[count])
    copies[4].wait()
    for leaf in range(count):
        acc_ref[leaf] = samples_ref[:, leaf * size : (leaf + 1) * size].astype(jnp.float32)
    for copy in copies[5:]:
        copy.wait()
    subtract_near(count, own_task, source, blocks_ref, acc_ref, slots)


def side_kernel(task_ref, side_ref, near_ref, blocks_ref, slots, acc, source):
    del near_ref
    count, _, size = acc.shape
    spread(source, 0, side_ref, size)
    source[count] = jnp.zeros_like(source[count])
    subtract_near(count, task_ref, source, blocks_ref, acc, slots)


def far_kernel(
    task_ref, side_ref, near_ref, blocks_ref, weight_ref, far_ref, part_ref, acc, source
):
    count, _, size = acc.shape
    slots = blocks_ref.shape[0] // count
    side_kernel(task_ref, side_ref, near_ref, blocks_ref, slots, acc, source)
    for leaf in range(count):
        far_ref[:, leaf * size : (leaf + 1) * size] = acc[leaf].astype(jnp.bfloat16)
    product = dot(weight_ref[...], far_ref[...], NT)
    rank = product.shape[0] // 2
    turned = (product[:rank] + product[rank:]).T
    half = turned.shape[0] // 2
    part_ref[...] = jnp.concatenate([turned[:half], turned[half:]], axis=1)


def coeff_kernel(far_ref, basis_ref, coeff_any, coeff_ref, sems):
    count, _, size = basis_ref.shape
    copies = []
    for first in range(0, count, PER_STEP):
        for leaf in range(first, first + PER_STEP):
            far = far_ref[:, leaf * size : (leaf + 1) * size]
            coeff_ref[leaf] = dot(basis_ref[leaf], far, NT)
        these = pl.ds(first, PER_STEP)
        copies.append(
            pltpu.make_async_copy(coeff_ref.at[these], coeff_any.at[these], sems.at[len(copies)])
        )
        copies[-1].start()
    for copy in copies:
        copy.wait()


def gram_kernel(scale, place_ref, far_ref, basis_ref, keep_ref, send_ref, gram):
    parts, rows, pairs, width = keep_ref.shape
    parts = 2 * parts
    rank = width // 2
    size = basis_ref.shape[2]
    lane = lax.broadcasted_iota(jnp.int32, (rank, width), 1)
    for first in range(0, pairs, PER_STEP):
        stacks = []
        for pair in range(first, first + PER_STEP):
            both = [
                dot(basis_ref[leaf], far_ref[:, leaf * size : (leaf + 1) * size], NT)
                for leaf in (pair, pair + pairs)
            ]
            stacks.append(jnp.concatenate(both, axis=0).astype(jnp.bfloat16))
        for pair, stacked in enumerate(stacks, first):
            product = dot(stacked, stacked, NT)
            value = jnp.where(lane < rank, product[:rank], product[rank:]) * scale
            gram[pl.ds(pair, rank, stride=pairs), :] = value
    for relative in range(parts):
        first = jnp.bitwise_xor(place_ref[0], relative) * rows
        target = send_ref if relative % 2 else keep_ref
        for row in range(rows):
            at = pl.multiple_of((first + row) * pairs, pairs)
            target[relative // 2, row] = gram[pl.ds(at, pairs), :]


def finish_kernel(keep_ref, got_ref, received_ref, last_ref, out_ref):
    _, rows, pairs, width = keep_ref.shape
    half = width // 2
    lane = lax.broadcasted_iota(jnp.int32, (pairs, width), 1)
    for row in range(0, rows, 2):
        even, odd = (
            keep_ref[0, at]
            + got_ref[0, at]
            + received_ref[0, at].astype(jnp.float32)
            + last_ref[at]
            for at in (row, row + 1)
        )
        at = slice(row * half, (row + 2) * half)
        out_ref[:pairs, at] = jnp.where(lane < half, even, pltpu.roll(odd, half, 1))
        out_ref[pairs:, at] = jnp.where(lane < half, pltpu.roll(even, half, 1), odd)


def turn_kernel(*refs):
    levels, out_ref = refs[:-1], refs[-1]
    for height, level in enumerate(levels):
        turned = level[...].T
        half = turned.shape[0] // 2
        out_ref[height] = jnp.concatenate([turned[:half], turned[half:]], axis=1)


def params(mib):
    return pltpu.CompilerParams(vmem_limit_bytes=mib * 2**20)


def own_pass(index, number, upper, mats, own, samples, blocks, basis):
    slots, count = index.shape
    size = blocks.shape[1]
    columns = own.shape[0]
    heights, rank, _ = upper.shape
    tasks = pltpu.SMEM((TASK_ROWS, LANES), jnp.int32)
    far = lambda value: pltpu.with_memory_space_constraint(value, pltpu.HBM)
    return pl.pallas_call(
        own_kernel,
        in_specs=[ANY, ANY, VMEM, VMEM, ANY, ANY, ANY, ANY],
        out_specs=(VMEM, VMEM, VMEM, VMEM, VMEM, SMEM, SMEM),
        out_shape=(
            pltpu.VMEM((count, columns, size), jnp.float32),
            pltpu.VMEM(blocks.shape, blocks.dtype),
            pltpu.VMEM(basis.shape, basis.dtype),
            pltpu.VMEM((2 * rank, count * size), jnp.bfloat16),
            pltpu.VMEM((heights - 1, 2 * rank, 2 * rank), jnp.float32),
            tasks,
            tasks,
        ),
        scratch_shapes=[
            tasks,
            pltpu.VMEM((3, TASK_ROWS, LANES), jnp.int32),
            pltpu.VMEM((slots, count), jnp.int32),
            pltpu.VMEM((1, count), jnp.int32),
            pltpu.VMEM(own.shape, own.dtype),
            pltpu.VMEM(samples.shape, samples.dtype),
            pltpu.VMEM((count + 1, columns, size), jnp.bfloat16),
            pltpu.SemaphoreType.DMA((9,)),
        ],
        compiler_params=params(8),
        name="own_pass",
    )(
        far(index),
        far(number),
        resident(upper),
        resident(mats),
        far(own),
        far(samples),
        far(blocks),
        far(basis),
    )


def side_pass(tasks, side, near, blocks):
    count, columns, size = near.shape
    slots = blocks.shape[0] // count

    def kernel(task_ref, side_ref, near_ref, blocks_ref, acc, source):
        side_kernel(task_ref, side_ref, near_ref, blocks_ref, slots, acc, source)

    return pl.pallas_call(
        kernel,
        in_specs=[SMEM] + [VMEM] * 3,
        out_specs=VMEM,
        out_shape=pltpu.VMEM((count, columns, size), jnp.float32),
        input_output_aliases={2: 0},
        scratch_shapes=[pltpu.VMEM((count + 1, columns, size), jnp.bfloat16)],
        compiler_params=params(8),
        name="side_pass",
    )(tasks, resident(side), near, blocks)


def far_pass(tasks, side, near, blocks, weight):
    count, columns, size = near.shape
    rank = weight.shape[0] // 2
    return pl.pallas_call(
        far_kernel,
        in_specs=[SMEM] + [VMEM] * 4,
        out_specs=(VMEM, VMEM, VMEM),
        out_shape=(
            pltpu.VMEM((columns, count * size), jnp.bfloat16),
            pltpu.VMEM((columns // 2, 2 * rank), jnp.float32),
            pltpu.VMEM((count, columns, size), jnp.float32),
        ),
        input_output_aliases={2: 2},
        scratch_shapes=[pltpu.VMEM((count + 1, columns, size), jnp.bfloat16)],
        compiler_params=params(8),
        name="far_pass",
    )(tasks, resident(side), near, blocks, weight)


def coeff_pass(far, basis):
    count, rank, _ = basis.shape
    columns = far.shape[0]
    return pl.pallas_call(
        coeff_kernel,
        in_specs=[VMEM, VMEM],
        out_specs=ANY,
        out_shape=pltpu.HBM((count, rank, columns), jnp.float32),
        scratch_shapes=[
            pltpu.VMEM((count, rank, columns), jnp.float32),
            pltpu.SemaphoreType.DMA((count // PER_STEP,)),
        ],
        compiler_params=params(8),
        name="coeff_pass",
    )(far, basis)


def gram_pass(place, far, basis, parts):
    count, rank, _ = basis.shape
    columns = far.shape[0]
    pairs = count // 2
    shape = (parts // 2, rank // parts, pairs, 2 * rank)
    return pl.pallas_call(
        functools.partial(gram_kernel, 1.0 / (columns * parts)),
        in_specs=[SMEM, VMEM, VMEM],
        out_specs=(VMEM, VMEM),
        out_shape=(pltpu.VMEM(shape, jnp.float32), pltpu.VMEM(shape, jnp.float32)),
        scratch_shapes=[pltpu.VMEM((rank * pairs, 2 * rank), jnp.float32)],
        compiler_params=params(8),
        name="gram_pass",
    )(place, far, basis)


def exchange(value, axis, flip):
    return lax.ppermute(value, axis, [(i, i ^ flip) for i in range(lax.axis_size(axis))])


def swap(value, axis, first):
    pairs = [(i, i + 1) for i in range(first, lax.axis_size(axis) - 1, 2)]
    return lax.ppermute(value, axis, pairs + [(j, i) for i, j in pairs])


def shards(
    samples, omega, leaf_basis, near_blocks, near_index, near_count, inner_transfer, upper_transfer
):
    count = near_count.shape[0]
    slots = near_index.shape[1]
    rank = leaf_basis.shape[1]
    size = leaf_basis.shape[2]
    groups = lax.axis_size("leaf")
    parts = lax.axis_size("samp")
    device = lax.axis_index("leaf")
    place = lax.axis_index("samp").astype(jnp.int32)

    own = omega.T
    first = swap(own, "leaf", 1)
    second = swap(own, "leaf", 0)

    heights = groups.bit_length() - 1
    rows = []
    offset, width = 0, groups
    for height in range(heights):
        rows.append(
            lax.dynamic_slice_in_dim(
                upper_transfer, offset + jnp.right_shift(device, height), 1, axis=0
            )
        )
        offset, width = offset + width, width // 2
    upper = jnp.concatenate(rows, axis=0).reshape(heights, rank, rank)

    blocks = near_blocks.reshape(count * slots, size, size)
    near, blocks, basis, weight, twice, crossing_tasks, tasks = own_pass(
        near_index.T,
        near_count.reshape(1, count),
        upper,
        inner_transfer.reshape(-1, rank),
        own,
        samples.T,
        blocks,
        leaf_basis,
    )
    near = side_pass(tasks, second, near, blocks)
    far, part, _ = far_pass(crossing_tasks, first, near, blocks, weight)

    flips = (1, 3, 4, 8, 24)
    levels = []
    accum = part
    for height in range(heights):
        if height:
            accum = jnp.dot(accum, twice[height - 1], precision=lax.Precision.HIGHEST)
        if height == heights - 1:
            accum, far = lax.optimization_barrier((accum, far))
            coeffs = coeff_pass(far, basis)
        other = exchange(accum, "leaf", flips[height])
        if height == 0:
            keep, send = gram_pass(place.reshape(1), far, basis, parts)
            got = exchange(send, "samp", 1)
        elif height == 2:
            leaving = (keep[1:3] + got[1:3]).astype(jnp.bfloat16)
            other, _ = lax.optimization_barrier((other, leaving))
            received = exchange(leaving, "samp", 2)
        elif height == 3:
            leaving = keep[3] + got[3] + received[1].astype(jnp.float32)
            other, _ = lax.optimization_barrier((other, leaving))
            last = exchange(leaving, "samp", 6)
        elif height == 4:
            leaf_gram = pl.pallas_call(
                finish_kernel,
                in_specs=[VMEM] * 4,
                out_specs=VMEM,
                out_shape=jax.ShapeDtypeStruct((count, rank * rank // parts), jnp.float32),
                compiler_params=params(8),
                name="finish",
            )(keep, *map(resident, [got, received, last]))
            other, _ = lax.optimization_barrier((other, leaf_gram))
        accum = accum + other
        levels.append(accum)
    ancestors = pl.pallas_call(
        turn_kernel,
        in_specs=[VMEM] * heights,
        out_specs=VMEM,
        out_shape=jax.ShapeDtypeStruct((heights, rank, 2 * part.shape[0]), jnp.float32),
        compiler_params=params(8),
        name="turn",
    )(*map(resident, levels))
    return coeffs, leaf_gram, ancestors[None]


def solution(mesh):
    return jax.shard_map(
        shards,
        mesh=mesh,
        in_specs=(
            P("leaf", "samp"),
            P("leaf", "samp"),
            P("leaf", None, None),
            P("leaf", None, None, None),
            P("leaf", None),
            P("leaf"),
            P("leaf", None),
            P(),
        ),
        out_specs=(P("leaf", None, "samp"), P("leaf", "samp"), P("leaf", None, None, "samp")),
        check_vma=False,
    )
```

```python
import functools

import jax
import jax.numpy as jnp
from jax import lax
from jax.experimental import pallas as pl
from jax.experimental.pallas import tpu as pltpu
from jax.sharding import PartitionSpec as P

NT = (((1,), (1,)), ((), ()))
NN = (((1,), (0,)), ((), ()))
PER_STEP = 8
PER_TASKS = 2 * PER_STEP
LANES = 128
TASK_ROWS = 8
LIST_ROWS = 3
VMEM = pl.BlockSpec(memory_space=pltpu.VMEM)
SMEM = pl.BlockSpec(memory_space=pltpu.SMEM)
ANY = pl.BlockSpec(memory_space=pl.ANY)


def dot(a, b, dims):
    return lax.dot_general(a, b, dims, preferred_element_type=jnp.float32)


def split(value):
    high = value.astype(jnp.bfloat16)
    return high, (value - high.astype(jnp.float32)).astype(jnp.bfloat16)


def resident(value):
    return pltpu.with_memory_space_constraint(value, pltpu.VMEM)


def spread(source, first, ref, size):
    for leaf in range(ref.shape[1] // size):
        source[first + leaf] = ref[:, leaf * size : (leaf + 1) * size]


def subtract_near(count, task_ref, source, blocks_ref, acc_ref, slots):
    shift = count.bit_length()
    low = (1 << shift) - 1
    per_row = LANES // PER_TASKS

    def body(step, carry):
        done = []
        row = lax.div(step, per_row)
        at = lax.rem(step, per_row) * PER_TASKS
        for task in range(PER_STEP):
            one = task_ref[row, at + 2 * task]
            two = task_ref[row, at + 2 * task + 1]
            left, right = jnp.right_shift(one, shift), jnp.right_shift(two, shift)
            fetched = jnp.concatenate(
                [source[jnp.bitwise_and(one, low)], source[jnp.bitwise_and(two, low)]], axis=1
            )
            matrix = jnp.concatenate([blocks_ref[left], blocks_ref[right]], axis=1)
            done.append((lax.div(left, slots), dot(fetched, matrix, NT)))
        for leaf, near in done:
            acc_ref[leaf] = acc_ref[leaf] - near
        return carry

    lax.fori_loop(0, task_ref[LIST_ROWS - 1, LANES - 1], body, 0)


def list_tasks(index, number, device, lists_ref):
    slots, count = index.shape
    shift = count.bit_length()
    slot = lax.broadcasted_iota(jnp.int32, (slots, count), 0)
    leaf = lax.broadcasted_iota(jnp.int32, (slots, count), 1)
    at = index - (device * count - count)
    alive = slot < number
    before, after = at < count, at >= 2 * count
    even = jnp.broadcast_to(jnp.bitwise_and(device, 1), at.shape) == 0
    side = jnp.where(before == even, 1, 2)
    kind = jnp.where(jnp.logical_or(before, after), side, 0)
    code = jnp.left_shift(leaf * slots + slot, shift) + jnp.bitwise_and(at, count - 1)
    blank = count
    earlier_slot = (
        lax.broadcasted_iota(jnp.int32, (slots, slots), 1)
        < lax.broadcasted_iota(jnp.int32, (slots, slots), 0)
    ).astype(jnp.bfloat16)
    earlier_leaf = (
        lax.broadcasted_iota(jnp.int32, (count, count), 0)
        < lax.broadcasted_iota(jnp.int32, (count, count), 1)
    ).astype(jnp.bfloat16)
    place = jnp.full((slots, count), -1, jnp.int32)
    steps = []
    for which in range(3):
        chosen = jnp.logical_and(alive, kind == which)
        mark = jnp.where(chosen, 1.0, 0.0)
        rank = dot(earlier_slot, mark.astype(jnp.bfloat16), NN)
        number_here = jnp.sum(mark, axis=0, keepdims=True).astype(jnp.int32)
        padded = (number_here + jnp.bitwise_and(number_here, 1)).astype(jnp.float32)
        base = dot(jnp.broadcast_to(padded, (slots, count)).astype(jnp.bfloat16), earlier_leaf, NN)
        here = (base + rank).astype(jnp.int32) + which * LIST_ROWS * LANES
        place = jnp.where(chosen, here, place)
        total = jnp.sum(padded, axis=1, keepdims=True).astype(jnp.int32)
        steps.append(jnp.right_shift(total + PER_TASKS - 1, PER_TASKS.bit_length() - 1))
    place, value = place.T, code.T - blank
    lane = lax.broadcasted_iota(jnp.int32, (count, LANES), 1)
    for which in range(3):
        for row in range(LIST_ROWS):
            target = lane + (which * LIST_ROWS + row) * LANES
            total = jnp.zeros((count, LANES), jnp.int32)
            for k in range(slots):
                total += jnp.where(place[:, k : k + 1] == target, value[:, k : k + 1], 0)
            line = jnp.sum(total, axis=0, keepdims=True) + blank
            if row == LIST_ROWS - 1:
                line = jnp.where(lane[:1] == LANES - 1, steps[which], line)
            lists_ref[which, row : row + 1] = line


def path_products(upper_ref, mats_ref, basis_ref, weight_ref):
    count, rank, size = basis_ref.shape
    nodes = [split(upper_ref[0].astype(jnp.float32).T)]
    blank = jnp.zeros((rank, size), basis_ref.dtype)
    width = 2
    offset = 2 * count - 2
    while width <= count:
        offset = offset - width
        later = []
        for parent, (high, low) in enumerate(nodes):
            first = (offset + 2 * parent) * rank
            pair = mats_ref[first : first + 2 * rank, :]
            product = dot(high, pair, NT) + dot(low, pair, NT)
            pair_high, pair_low = split(product)
            if width == count:
                bases = jnp.concatenate(
                    [
                        jnp.concatenate([basis_ref[2 * parent], blank], axis=1),
                        jnp.concatenate([blank, basis_ref[2 * parent + 1]], axis=1),
                    ],
                    axis=0,
                )
                weight = split(dot(pair_high, bases, NN) + dot(pair_low, bases, NN))
                at = slice(2 * parent * size, 2 * (parent + 1) * size)
                weight_ref[:rank, at], weight_ref[rank:, at] = weight
            else:
                later.append((pair_high[:, :rank], pair_low[:, :rank]))
                later.append((pair_high[:, rank:], pair_low[:, rank:]))
        nodes = later
        width = 2 * width


def own_kernel(
    index_any,
    number_any,
    upper_ref,
    mats_ref,
    own_any,
    samples_any,
    blocks_any,
    basis_any,
    acc_ref,
    blocks_ref,
    basis_ref,
    weight_ref,
    twice_ref,
    first_task_ref,
    second_task_ref,
    own_task,
    lists,
    index_ref,
    number_ref,
    own_ref,
    samples_ref,
    source,
    sems,
):
    pairs = (
        (index_any, index_ref),
        (number_any, number_ref),
        (basis_any, basis_ref),
        (own_any, own_ref),
        (samples_any, samples_ref),
        (blocks_any, blocks_ref),
        (lists.at[0], own_task),
        (lists.at[1], first_task_ref),
        (lists.at[2], second_task_ref),
    )
    copies = [
        pltpu.make_async_copy(origin, target, sems.at[place])
        for place, (origin, target) in enumerate(pairs)
    ]
    for copy in copies[:6]:
        copy.start()
    slots, count = index_ref.shape
    size = blocks_ref.shape[1]
    rank = upper_ref.shape[1]
    copies[0].wait()
    copies[1].wait()
    list_tasks(index_ref[...], number_ref[...], lax.axis_index("leaf"), lists)
    for copy in copies[6:]:
        copy.start()
    copies[2].wait()
    path_products(upper_ref, mats_ref, basis_ref, weight_ref)
    for height in range(1, upper_ref.shape[0]):
        matrix = upper_ref[height].astype(jnp.float32)
        blank = jnp.zeros_like(matrix)
        twice_ref[height - 1, :rank] = jnp.concatenate([matrix, blank], axis=1)
        twice_ref[height - 1, rank:] = jnp.concatenate([blank, matrix], axis=1)
    copies[3].wait()
    spread(source, 0, own_ref, size)
    source[count] = jnp.zeros_like(source[count])
    copies[4].wait()
    for leaf in range(count):
        acc_ref[leaf] = samples_ref[:, leaf * size : (leaf + 1) * size].astype(jnp.float32)
    for copy in copies[5:]:
        copy.wait()
    subtract_near(count, own_task, source, blocks_ref, acc_ref, slots)


def side_kernel(task_ref, side_ref, near_ref, blocks_ref, slots, acc, source):
    del near_ref
    count, _, size = acc.shape
    spread(source, 0, side_ref, size)
    source[count] = jnp.zeros_like(source[count])
    subtract_near(count, task_ref, source, blocks_ref, acc, slots)


def far_kernel(
    task_ref, side_ref, near_ref, blocks_ref, weight_ref, far_ref, part_ref, acc, source
):
    count, _, size = acc.shape
    slots = blocks_ref.shape[0] // count
    side_kernel(task_ref, side_ref, near_ref, blocks_ref, slots, acc, source)
    for leaf in range(count):
        far_ref[:, leaf * size : (leaf + 1) * size] = acc[leaf].astype(jnp.bfloat16)
    product = dot(weight_ref[...], far_ref[...], NT)
    rank = product.shape[0] // 2
    turned = (product[:rank] + product[rank:]).T
    half = turned.shape[0] // 2
    part_ref[...] = jnp.concatenate([turned[:half], turned[half:]], axis=1)


def coeff_kernel(far_ref, basis_ref, coeff_any, coeff_ref, sems):
    count, _, size = basis_ref.shape
    copies = []
    for first in range(0, count, PER_STEP):
        for leaf in range(first, first + PER_STEP):
            far = far_ref[:, leaf * size : (leaf + 1) * size]
            coeff_ref[leaf] = dot(basis_ref[leaf], far, NT)
        these = pl.ds(first, PER_STEP)
        copies.append(
            pltpu.make_async_copy(coeff_ref.at[these], coeff_any.at[these], sems.at[len(copies)])
        )
        copies[-1].start()
    for copy in copies:
        copy.wait()


def gram_kernel(scale, place_ref, far_ref, basis_ref, keep_ref, send_ref, gram):
    parts, rows, pairs, width = keep_ref.shape
    parts = 2 * parts
    rank = width // 2
    size = basis_ref.shape[2]
    lane = lax.broadcasted_iota(jnp.int32, (rank, width), 1)
    for first in range(0, pairs, PER_STEP):
        stacks = []
        for pair in range(first, first + PER_STEP):
            both = [
                dot(basis_ref[leaf], far_ref[:, leaf * size : (leaf + 1) * size], NT)
                for leaf in (pair, pair + pairs)
            ]
            stacks.append(jnp.concatenate(both, axis=0).astype(jnp.bfloat16))
        for pair, stacked in enumerate(stacks, first):
            product = dot(stacked, stacked, NT)
            value = jnp.where(lane < rank, product[:rank], product[rank:]) * scale
            gram[pl.ds(pair, rank, stride=pairs), :] = value
    for relative in range(parts):
        first = jnp.bitwise_xor(place_ref[0], relative) * rows
        target = send_ref if relative % 2 else keep_ref
        for row in range(rows):
            at = pl.multiple_of((first + row) * pairs, pairs)
            target[relative // 2, row] = gram[pl.ds(at, pairs), :]


def finish_kernel(keep_ref, got_ref, received_ref, last_ref, out_ref):
    _, rows, pairs, width = keep_ref.shape
    half = width // 2
    lane = lax.broadcasted_iota(jnp.int32, (pairs, width), 1)
    for row in range(0, rows, 2):
        even, odd = (
            keep_ref[0, at]
            + got_ref[0, at]
            + received_ref[0, at].astype(jnp.float32)
            + last_ref[at]
            for at in (row, row + 1)
        )
        at = slice(row * half, (row + 2) * half)
        out_ref[:pairs, at] = jnp.where(lane < half, even, pltpu.roll(odd, half, 1))
        out_ref[pairs:, at] = jnp.where(lane < half, pltpu.roll(even, half, 1), odd)


def turn_kernel(*refs):
    levels, out_ref = refs[:-1], refs[-1]
    for height, level in enumerate(levels):
        turned = level[...].T
        half = turned.shape[0] // 2
        out_ref[height] = jnp.concatenate([turned[:half], turned[half:]], axis=1)


def params(mib):
    return pltpu.CompilerParams(vmem_limit_bytes=mib * 2**20)


def own_pass(index, number, upper, mats, own, samples, blocks, basis):
    slots, count = index.shape
    size = blocks.shape[1]
    columns = own.shape[0]
    heights, rank, _ = upper.shape
    tasks = pltpu.SMEM((TASK_ROWS, LANES), jnp.int32)
    far = lambda value: pltpu.with_memory_space_constraint(value, pltpu.HBM)
    return pl.pallas_call(
        own_kernel,
        in_specs=[ANY, ANY, VMEM, VMEM, ANY, ANY, ANY, ANY],
        out_specs=(VMEM, VMEM, VMEM, VMEM, VMEM, SMEM, SMEM),
        out_shape=(
            pltpu.VMEM((count, columns, size), jnp.float32),
            pltpu.VMEM(blocks.shape, blocks.dtype),
            pltpu.VMEM(basis.shape, basis.dtype),
            pltpu.VMEM((2 * rank, count * size), jnp.bfloat16),
            pltpu.VMEM((heights - 1, 2 * rank, 2 * rank), jnp.float32),
            tasks,
            tasks,
        ),
        scratch_shapes=[
            tasks,
            pltpu.VMEM((3, TASK_ROWS, LANES), jnp.int32),
            pltpu.VMEM((slots, count), jnp.int32),
            pltpu.VMEM((1, count), jnp.int32),
            pltpu.VMEM(own.shape, own.dtype),
            pltpu.VMEM(samples.shape, samples.dtype),
            pltpu.VMEM((count + 1, columns, size), jnp.bfloat16),
            pltpu.SemaphoreType.DMA((9,)),
        ],
        compiler_params=params(8),
        name="own_pass",
    )(
        far(index),
        far(number),
        resident(upper),
        resident(mats),
        far(own),
        far(samples),
        far(blocks),
        far(basis),
    )


def side_pass(tasks, side, near, blocks):
    count, columns, size = near.shape
    slots = blocks.shape[0] // count

    def kernel(task_ref, side_ref, near_ref, blocks_ref, acc, source):
        side_kernel(task_ref, side_ref, near_ref, blocks_ref, slots, acc, source)

    return pl.pallas_call(
        kernel,
        in_specs=[SMEM] + [VMEM] * 3,
        out_specs=VMEM,
        out_shape=pltpu.VMEM((count, columns, size), jnp.float32),
        input_output_aliases={2: 0},
        scratch_shapes=[pltpu.VMEM((count + 1, columns, size), jnp.bfloat16)],
        compiler_params=params(8),
        name="side_pass",
    )(tasks, resident(side), near, blocks)


def far_pass(tasks, side, near, blocks, weight):
    count, columns, size = near.shape
    rank = weight.shape[0] // 2
    return pl.pallas_call(
        far_kernel,
        in_specs=[SMEM] + [VMEM] * 4,
        out_specs=(VMEM, VMEM, VMEM),
        out_shape=(
            pltpu.VMEM((columns, count * size), jnp.bfloat16),
            pltpu.VMEM((columns // 2, 2 * rank), jnp.float32),
            pltpu.VMEM((count, columns, size), jnp.float32),
        ),
        input_output_aliases={2: 2},
        scratch_shapes=[pltpu.VMEM((count + 1, columns, size), jnp.bfloat16)],
        compiler_params=params(8),
        name="far_pass",
    )(tasks, resident(side), near, blocks, weight)


def coeff_pass(far, basis):
    count, rank, _ = basis.shape
    columns = far.shape[0]
    return pl.pallas_call(
        coeff_kernel,
        in_specs=[VMEM, VMEM],
        out_specs=ANY,
        out_shape=pltpu.HBM((count, rank, columns), jnp.float32),
        scratch_shapes=[
            pltpu.VMEM((count, rank, columns), jnp.float32),
            pltpu.SemaphoreType.DMA((count // PER_STEP,)),
        ],
        compiler_params=params(8),
        name="coeff_pass",
    )(far, basis)


def gram_pass(place, far, basis, parts):
    count, rank, _ = basis.shape
    columns = far.shape[0]
    pairs = count // 2
    shape = (parts // 2, rank // parts, pairs, 2 * rank)
    return pl.pallas_call(
        functools.partial(gram_kernel, 1.0 / (columns * parts)),
        in_specs=[SMEM, VMEM, VMEM],
        out_specs=(VMEM, VMEM),
        out_shape=(pltpu.VMEM(shape, jnp.float32), pltpu.VMEM(shape, jnp.float32)),
        scratch_shapes=[pltpu.VMEM((rank * pairs, 2 * rank), jnp.float32)],
        compiler_params=params(8),
        name="gram_pass",
    )(place, far, basis)


def exchange(value, axis, flip):
    return lax.ppermute(value, axis, [(i, i ^ flip) for i in range(lax.axis_size(axis))])


def swap(value, axis, first):
    pairs = [(i, i + 1) for i in range(first, lax.axis_size(axis) - 1, 2)]
    return lax.ppermute(value, axis, pairs + [(j, i) for i, j in pairs])


def shards(
    samples, omega, leaf_basis, near_blocks, near_index, near_count, inner_transfer, upper_transfer
):
    count = near_count.shape[0]
    slots = near_index.shape[1]
    rank = leaf_basis.shape[1]
    size = leaf_basis.shape[2]
    groups = lax.axis_size("leaf")
    parts = lax.axis_size("samp")
    device = lax.axis_index("leaf")
    place = lax.axis_index("samp").astype(jnp.int32)

    own = omega.T
    first = swap(own, "leaf", 1)
    second = swap(own, "leaf", 0)

    heights = groups.bit_length() - 1
    rows = []
    offset, width = 0, groups
    for height in range(heights):
        rows.append(
            lax.dynamic_slice_in_dim(
                upper_transfer, offset + jnp.right_shift(device, height), 1, axis=0
            )
        )
        offset, width = offset + width, width // 2
    upper = jnp.concatenate(rows, axis=0).reshape(heights, rank, rank)

    blocks = near_blocks.reshape(count * slots, size, size)
    near, blocks, basis, weight, twice, crossing_tasks, tasks = own_pass(
        near_index.T,
        near_count.reshape(1, count),
        upper,
        inner_transfer.reshape(-1, rank),
        own,
        samples.T,
        blocks,
        leaf_basis,
    )
    near = side_pass(tasks, second, near, blocks)
    far, part, _ = far_pass(crossing_tasks, first, near, blocks, weight)

    flips = (1, 3, 4, 8, 24)
    levels = []
    accum = part
    for height in range(heights):
        if height:
            accum = jnp.dot(accum, twice[height - 1], precision=lax.Precision.HIGHEST)
        if height == 1:
            accum, far = lax.optimization_barrier((accum, far))
            coeffs = coeff_pass(far, basis)
        other = exchange(accum, "leaf", flips[height])
        if height == 1:
            other, coeffs = lax.optimization_barrier((other, coeffs))
        if height == 0:
            keep, send = gram_pass(place.reshape(1), far, basis, parts)
            got = exchange(send, "samp", 1)
        elif height == 2:
            leaving = (keep[1:3] + got[1:3]).astype(jnp.bfloat16)
            other, _ = lax.optimization_barrier((other, leaving))
            received = exchange(leaving, "samp", 2)
        elif height == 3:
            leaving = keep[3] + got[3] + received[1].astype(jnp.float32)
            other, _ = lax.optimization_barrier((other, leaving))
            last = exchange(leaving, "samp", 6)
        elif height == 4:
            leaf_gram = pl.pallas_call(
                finish_kernel,
                in_specs=[VMEM] * 4,
                out_specs=VMEM,
                out_shape=jax.ShapeDtypeStruct((count, rank * rank // parts), jnp.float32),
                compiler_params=params(8),
                name="finish",
            )(keep, *map(resident, [got, received, last]))
            other, _ = lax.optimization_barrier((other, leaf_gram))
        accum = accum + other
        levels.append(accum)
    ancestors = pl.pallas_call(
        turn_kernel,
        in_specs=[VMEM] * heights,
        out_specs=VMEM,
        out_shape=jax.ShapeDtypeStruct((heights, rank, 2 * part.shape[0]), jnp.float32),
        compiler_params=params(8),
        name="turn",
    )(*map(resident, levels))
    return coeffs, leaf_gram, ancestors[None]


def solution(mesh):
    return jax.shard_map(
        shards,
        mesh=mesh,
        in_specs=(
            P("leaf", "samp"),
            P("leaf", "samp"),
            P("leaf", None, None),
            P("leaf", None, None, None),
            P("leaf", None),
            P("leaf"),
            P("leaf", None),
            P(),
        ),
        out_specs=(P("leaf", None, "samp"), P("leaf", "samp"), P("leaf", None, None, "samp")),
        check_vma=False,
    )
```
